128 devices in a mesh: ctx: 16 (over z_hi, x, core), hx: 8 (over y, z_lo).
Axes of the slice: x: 4, y: 4, z: 4 (z_hi: 2, z_lo: 2; z = z_hi * 2 + z_lo), core: 2. Of those that a mesh axis runs over, the one named last changes fastest.
Arguments:
- tokens: bfloat16 [8192, 5120], P('ctx'), may hold values from -6 to 6
- attn_gain: bfloat16 [5120], replicated, may hold values from 0.5 to 1.5
- ffn_gain: bfloat16 [5120], replicated, may hold values from 0.5 to 1.5
- w_query: bfloat16 [5120, 3072], P('ctx', 'hx'), may hold values from -3 to 3
- w_key: bfloat16 [5120, 1024], P('ctx', 'hx'), may hold values from -1 to 1
- w_value: bfloat16 [5120, 1024], P('ctx', 'hx'), may hold values from -0.078125 to 0.078125
- w_out: bfloat16 [3072, 5120], P('hx'), may hold values from -0.109375 to 0.109375
- w_router: bfloat16 [5120, 16], replicated, may hold values from -0.078125 to 0.078125
- routes: int32 [8192, 1], P('ctx'), may hold values from 0 to 15; in each aligned block of 512 rows (0 to 511, 512 to 1023, ...) at most 64 rows name the same one
- w_gate: bfloat16 [16, 5120, 4096], P('ctx', None, 'hx'), may hold values from -0.078125 to 0.078125
- w_up: bfloat16 [16, 5120, 4096], P('ctx', None, 'hx'), may hold values from -0.078125 to 0.078125
- w_down: bfloat16 [16, 4096, 5120], P('ctx', 'hx'), may hold values from -0.09375 to 0.09375
Outputs:
- layer_out: bfloat16 [8192, 5120], P('ctx', 'hx')
The draws below stay inside these ranges and needn't reach their ends.
Inputs may be any that keep to these rules, and one draw needn't show every extreme that they name: `routes`: within the 512 rows of one device, no expert is named by more than 64 rows, a bound that some block reaches.
All inputs are finite; a program needn't handle non-finite values.
Results may differ from the reference program's by a relative error of at most 0.0095.
Values may be sent and summed in bfloat16 or wider, within the bound.
A program may use at most 128 MiB of HBM per device.

```python
import math
import jax
import jax.numpy as jnp
import numpy as np
from jax import lax

D = 5120
HEADS = 24
KV_HEADS = 8
HD = 128
FF = 4096
TOK_DEV = 512
TOKENS = 8192
EXPERTS = 16
CAP = 64
N_CTX = 16
N_HX = 8


def draw_tokens(key, part):
    normal_values = jax.random.normal(jax.random.fold_in(key, 21), (TOKENS, D), jnp.float32)
    return jnp.clip(normal_values, -6.0, 6.0).astype(jnp.bfloat16)


def attention_weights(key):
    key_mat = jax.random.normal(jax.random.fold_in(key, 11), (D, KV_HEADS, HD), jnp.float32) * D ** (-0.5)
    loose = jax.random.normal(jax.random.fold_in(key, 12), (D, HEADS, HD), jnp.float32) * D ** (-0.5)
    return (key_mat.reshape(D, KV_HEADS * HD), loose.reshape(D, HEADS * HD))


def draw_w_query(key, part):
    key_mat, loose = attention_weights(key)
    return jnp.clip(loose, -3.0, 3.0).astype(jnp.bfloat16)


def draw_w_key(key, part):
    key_mat, loose = attention_weights(key)
    return jnp.clip(key_mat, -1.0, 1.0).astype(jnp.bfloat16)


def steps_of(stream_key, dims, pieces, smallest, top_value):
    def one(dim, shards_of):
        steps = jax.random.uniform(jax.random.fold_in(jax.random.fold_in(stream_key, 6), dim), (shards_of,), jnp.float32, smallest / len(pieces), top_value / len(pieces))
        return jnp.repeat(jnp.exp(steps), dims[dim] // shards_of).reshape((-1,) + (1,) * (len(dims) - dim - 1))

    factor_of = one(*pieces[0])
    for cut in pieces[1:]:
        factor_of = factor_of * one(*cut)
    return factor_of


def shared_out(key, own, number, rows, amount, top, reach, lean):
    order = jax.random.permutation(key, amount)
    heavy_load, ordinary = portions_of(amount, rows * top, reach, lean, True), portions_of(amount, rows * top, reach, lean, False)
    places = jnp.arange(amount)

    def named(tallies, turn):
        used = int((tallies > 0).sum())
        fixed = max(1, used // 4)
        moved = fixed + (places - fixed + turn * (used - fixed)) % max(1, amount - fixed)
        return jnp.zeros((amount,), jnp.int32).at[order[jnp.where(places < fixed, places, moved)]].set(jnp.asarray(tallies, jnp.int32))

    tallies = jnp.where(number % 4 == 0, named(heavy_load, number // 4), named(ordinary, number - number // 4 - 1))
    mixed = jax.random.permutation(jax.random.fold_in(own, 3), amount)
    giver, taker = mixed[0:amount // 2 * 2:2], mixed[1:amount // 2 * 2:2]
    margin = jnp.minimum(tallies[giver] - 1, reach - tallies[taker]) // 2
    margin = jnp.where((giver == order[0]) | (taker == order[0]) | (tallies[taker] == 0), 0, jnp.maximum(margin, 0))
    moved = jax.random.randint(jax.random.fold_in(own, 4), (amount // 2,), 0, 1 << 20) % (margin + 1)
    tallies = tallies.at[giver].add(-moved).at[taker].add(moved)
    labels = jnp.searchsorted(jnp.cumsum(tallies), jnp.arange(rows * top), side="right").astype(jnp.int32)
    listing = labels.reshape(top, rows).T
    listing = listing[jax.random.permutation(jax.random.fold_in(own, 1), rows)]
    turn = jax.random.randint(jax.random.fold_in(own, 2), (rows, 1), 0, top)
    return jnp.take_along_axis(listing, (jnp.arange(top)[None, :] + turn) % top, axis=1)


def portions_of(amount, total, bound, skew, full):
    loads = [(1 << 20) // math.isqrt(rank ** skew) + 1 for rank in range(1, amount + 1)]
    largest = bound if full else min(bound, max(-(-total // amount), total * loads[0] // sum(loads)))
    least = 1 if total - largest >= amount - 1 else 0
    given, rest = [largest] + [least] * (amount - 1), total - largest - least * (amount - 1)
    while rest > 0:
        movable = [i for i in range(1, amount) if given[i] < largest] or [i for i in range(1, amount) if given[i] < bound]
        whole, remaining = sum([loads[i] for i in movable]), rest
        for i in movable:
            addition = min(bound - given[i], max(1, remaining * loads[i] // whole), rest)
            given[i] = given[i] + addition
            rest = rest - addition
    return np.array(given)


def bell_draw(key, extent, scale, bound, cuts=(), held_as=jnp.bfloat16):
    values = jax.random.normal(key, extent, jnp.float32) * scale
    if len(cuts) > 0:
        values = steps_of(key, extent, cuts, -0.22, 0.18) * values
    return jnp.clip(values, min=-bound, max=bound).astype(held_as)


def setup_inputs(seed: int = 0) -> dict:
    streams_of = jax.random.split(jax.random.key(seed), 13)
    tokens = draw_tokens(jax.random.fold_in(streams_of[12], 71), 0)
    attn_gain = jnp.clip(1.0 + 0.1 * jax.random.normal(streams_of[1], (D,), jnp.float32), 0.5, 1.5).astype(jnp.bfloat16)
    ffn_gain = jnp.clip(1.0 + 0.1 * jax.random.normal(streams_of[2], (D,), jnp.float32), 0.5, 1.5).astype(jnp.bfloat16)
    w_query = draw_w_query(jax.random.fold_in(streams_of[12], 71), 0)
    w_key = draw_w_key(jax.random.fold_in(streams_of[12], 71), 0)
    w_value = bell_draw(streams_of[5], (D, KV_HEADS * HD), D ** -0.5, 0.078125, ((0, 16), (1, 8)))
    w_out = bell_draw(streams_of[6], (HEADS * HD, D), (HEADS * HD) ** -0.5, 0.109375, ((0, 8),))
    w_router = bell_draw(streams_of[7], (D, EXPERTS), D ** -0.5, 0.078125)
    routes_keys = jax.random.split(jax.random.fold_in(streams_of[8], 1), TOKENS // TOK_DEV)
    routes_turns = jax.random.permutation(jax.random.fold_in(streams_of[8], 3), TOKENS // TOK_DEV)
    routes = jax.vmap(lambda own, number: shared_out(jax.random.fold_in(streams_of[8], 2), own, number, TOK_DEV, EXPERTS, 1, CAP, 2))(routes_keys, routes_turns).reshape((TOKENS, 1))
    w_gate = bell_draw(streams_of[9], (EXPERTS, D, FF), D ** -0.5, 0.078125, ((0, 16), (2, 8)))
    w_up = bell_draw(streams_of[10], (EXPERTS, D, FF), D ** -0.5, 0.078125, ((0, 16), (2, 8)))
    w_down = bell_draw(streams_of[11], (EXPERTS, FF, D), FF ** -0.5, 0.09375, ((0, 16), (1, 8)))
    return dict(tokens=tokens, attn_gain=attn_gain, ffn_gain=ffn_gain, w_query=w_query, w_key=w_key, w_value=w_value, w_out=w_out, w_router=w_router, routes=routes, w_gate=w_gate, w_up=w_up, w_down=w_down)


epsilon = 1e-05

def root_norm(values, gains):
    floats = values.astype(jnp.float32)
    inverse = lax.rsqrt(lax.optimization_barrier(jnp.mean(floats * floats, axis=-1, keepdims=True)) + epsilon)
    return (floats * inverse * gains.astype(jnp.float32)).astype(jnp.bfloat16)

def reference(tokens, attn_gain, ffn_gain, w_query, w_key, w_value, w_out, w_router, routes, w_gate, w_up, w_down):
    normed = root_norm(tokens, attn_gain)
    queries = jnp.dot(normed, w_query, preferred_element_type=jnp.float32).astype(jnp.bfloat16)
    key_proj = jnp.dot(normed, w_key, preferred_element_type=jnp.float32).astype(jnp.bfloat16)
    value_proj = jnp.dot(normed, w_value, preferred_element_type=jnp.float32).astype(jnp.bfloat16)
    group_size = HEADS // KV_HEADS
    head_share = HEADS * HD // N_HX
    queries_all = queries.reshape(TOKENS, KV_HEADS, group_size, HD)
    key_heads = key_proj.reshape(TOKENS, KV_HEADS, HD).astype(jnp.float32)
    value_heads = value_proj.reshape(TOKENS, KV_HEADS, HD).astype(jnp.float32)
    key_pos = jnp.arange(TOKENS, dtype=jnp.int32)
    out_groups = w_out.reshape(N_HX, head_share, D).astype(jnp.float32)

    def attend(block_index):
        begin = block_index * TOK_DEV
        queries_block = lax.dynamic_slice_in_dim(queries_all, begin, TOK_DEV, 0).astype(jnp.float32)
        scores = jnp.einsum('tkgd,skd->tkgs', queries_block, key_heads) * HD ** (-0.5)
        query_pos = begin + jnp.arange(TOK_DEV, dtype=jnp.int32)
        visible = (key_pos[None, :] <= query_pos[:, None])[:, None, None, :]
        masked = jnp.where(visible, scores, -jnp.inf)
        row_max = lax.optimization_barrier(jnp.max(masked, axis=-1, keepdims=True))
        weights = jnp.where(visible, jnp.exp(scores - row_max), 0.0)
        weight_sum = lax.optimization_barrier(jnp.sum(weights, axis=-1))
        rounded = lax.optimization_barrier(weights.astype(jnp.bfloat16))
        mixed = jnp.einsum('tkgs,skd->tkgd', rounded.astype(jnp.float32), value_heads)
        attended = (mixed / weight_sum[..., None]).astype(jnp.bfloat16).reshape(TOK_DEV, N_HX, head_share)
        partial_out = jnp.einsum('tgh,ghd->tgd', attended.astype(jnp.float32), out_groups)
        rounded_out = lax.optimization_barrier(partial_out.astype(jnp.bfloat16))
        return lax.optimization_barrier(jnp.sum(rounded_out.astype(jnp.float32), axis=1))
    attn_sum = lax.map(attend, jnp.arange(N_CTX, dtype=jnp.int32)).reshape(TOKENS, D)
    stream = (tokens.astype(jnp.float32) + attn_sum).astype(jnp.bfloat16)
    normed2 = root_norm(stream, ffn_gain)
    logits = jnp.dot(normed2, w_router, preferred_element_type=jnp.float32)
    chosen = routes[:, 0].astype(jnp.int32)
    onehot = chosen[:, None] == jnp.arange(EXPERTS, dtype=jnp.int32)[None, :]
    router_score = jax.nn.sigmoid(lax.optimization_barrier(jnp.sum(jnp.where(onehot, logits, 0.0), axis=-1)))
    routed = (normed2.astype(jnp.float32) * router_score[:, None]).astype(jnp.bfloat16)
    counts = jnp.cumsum(onehot.astype(jnp.int32).reshape(N_CTX, TOK_DEV, EXPERTS), axis=1).reshape(TOKENS, EXPERTS)
    position = lax.optimization_barrier(jnp.sum(jnp.where(onehot, counts, 0), axis=-1)).astype(jnp.int32) - 1
    block_of = jnp.arange(TOKENS, dtype=jnp.int32) // TOK_DEV
    slot_index = (chosen * (N_CTX * CAP) + block_of * CAP + position).astype(jnp.int32)
    buffer = jnp.zeros((EXPERTS * N_CTX * CAP, D), jnp.bfloat16).at[slot_index].set(routed)
    buffer = buffer.reshape(EXPERTS, N_CTX * CAP, D)
    hidden_share = FF // N_HX

    def expert(operands):
        expert_rows, gate_mat, up_mat, down_mat = operands
        gate_out = jnp.dot(expert_rows, gate_mat, preferred_element_type=jnp.float32)
        up_out = jnp.dot(expert_rows, up_mat, preferred_element_type=jnp.float32)
        hidden = (jax.nn.silu(gate_out) * up_out).astype(jnp.bfloat16)
        parts = jnp.einsum('rgf,gfd->rgd', hidden.reshape(N_CTX * CAP, N_HX, hidden_share).astype(jnp.float32), down_mat.reshape(N_HX, hidden_share, D).astype(jnp.float32))
        rounded_parts = lax.optimization_barrier(parts.astype(jnp.bfloat16))
        return lax.optimization_barrier(jnp.sum(rounded_parts.astype(jnp.float32), axis=1)).astype(jnp.bfloat16)
    expert_all = lax.map(expert, (buffer, w_gate, w_up, w_down)).reshape(EXPERTS * N_CTX * CAP, D)
    expert_out = expert_all[slot_index]
    return (stream.astype(jnp.float32) + expert_out.astype(jnp.float32)).astype(jnp.bfloat16)
```

```python
import functools
import math
import jax
import jax.numpy as jnp
from jax import lax
from jax.experimental import pallas as pl
from jax.experimental.pallas import tpu as pltpu
from jax.sharding import PartitionSpec as P

HD = 128
epsilon = 1e-05
MESH = pl.DeviceIdType.MESH


def place():
    ctx, hx = lax.axis_index("ctx"), lax.axis_index("hx")
    z_hi, x, core = ctx // 8, (ctx // 2) % 4, ctx % 2
    y, z_lo = hx // 2, hx % 2
    return z_hi, x, core, y, z_lo


def ctx_of(z_hi, x, core):
    return z_hi * 8 + x * 2 + core


def greet(devices):
    barrier = pltpu.get_barrier_semaphore()
    for device in devices:
        pl.semaphore_signal(barrier, inc=1, device_id=device, device_id_type=MESH)
    pl.semaphore_wait(barrier, len(devices))


class Sends:
    def __init__(self, send_sem, recv_sem):
        self.send_sem, self.recv_sem, self.started = send_sem, recv_sem, []

    def start(self, k, src, dst, device):
        copy = pltpu.make_async_remote_copy(
            src_ref=src,
            dst_ref=dst,
            send_sem=self.send_sem.at[k],
            recv_sem=self.recv_sem.at[k],
            device_id=device,
            device_id_type=MESH,
        )
        copy.start()
        self.started.append(copy)

    def arrived(self, k, dst):
        pltpu.make_async_copy(dst, dst, self.recv_sem.at[k]).wait()

    def drain(self):
        for copy in self.started:
            copy.wait_send()


def hx_gather_kernel(rows, cols, split, a, out, held, local_sem, send_sem, recv_sem):
    z_hi, x, core, y, z_lo = place()
    ctx = ctx_of(z_hi, x, core)
    right, left, far = (y + 1) % 4, (y + 3) % 4, (y + 2) % 4
    other = 1 - z_lo
    to_right, to_left, to_z = (ctx, right * 2 + z_lo), (ctx, left * 2 + z_lo), (ctx, y * 2 + other)
    load = pltpu.make_async_copy(a, held, local_sem.at[0])
    load.start()
    greet((to_right, to_left, to_z))

    first = (0, split)
    first_0, first_1 = (0, split // 2), (split // 2, split // 2)
    rest = (split, rows - split)
    half = (rows - split) // 2
    rest_0, rest_1 = (split, half), (split + half, half)

    def at(y_of, z_of, part):
        return out.at[pl.ds(part[0], part[1]), pl.ds((y_of * 2 + z_of) * cols, cols)]

    def own(part):
        return a.at[pl.ds(part[0], part[1]), :]

    sends = Sends(send_sem, recv_sem)

    def forward(k, y_of, z_of, part, device):
        sends.start(k, at(y_of, z_of, part), at(y_of, z_of, part), device)

    sends.start(0, own(first), at(y, z_lo, first), to_z)
    sends.start(1, own(first), at(y, z_lo, first), to_right)
    sends.start(2, own(first), at(y, z_lo, first), to_left)
    sends.start(3, own(rest), at(y, z_lo, rest), to_right)
    sends.start(4, own(rest), at(y, z_lo, rest), to_left)
    sends.start(5, own(rest), at(y, z_lo, rest), to_z)
    load.wait()
    keep = pltpu.make_async_copy(held, out.at[:, pl.ds((y * 2 + z_lo) * cols, cols)], local_sem.at[1])
    keep.start()
    sends.arrived(0, at(y, other, first))
    forward(6, y, other, first, to_right)
    forward(7, y, other, first, to_left)
    sends.arrived(3, at(left, z_lo, rest))
    forward(10, left, z_lo, rest_0, to_right)
    forward(11, left, z_lo, rest, to_z)
    sends.arrived(4, at(right, z_lo, rest))
    forward(12, right, z_lo, rest_1, to_left)
    forward(13, right, z_lo, rest, to_z)
    sends.arrived(1, at(left, z_lo, first))
    forward(8, left, z_lo, first_0, to_right)
    sends.arrived(2, at(right, z_lo, first))
    forward(9, right, z_lo, first_1, to_left)
    sends.arrived(6, at(left, other, first))
    forward(14, left, other, first_0, to_right)
    sends.arrived(7, at(right, other, first))
    forward(15, right, other, first_1, to_left)
    sends.arrived(10, at(far, z_lo, rest_0))
    forward(16, far, z_lo, rest_0, to_z)
    sends.arrived(12, at(far, z_lo, rest_1))
    forward(17, far, z_lo, rest_1, to_z)
    sends.arrived(5, at(y, other, rest))
    sends.arrived(8, at(far, z_lo, first_0))
    sends.arrived(9, at(far, z_lo, first_1))
    sends.arrived(11, at(left, other, rest))
    sends.arrived(13, at(right, other, rest))
    sends.arrived(14, at(far, other, first_0))
    sends.arrived(15, at(far, other, first_1))
    sends.arrived(16, at(far, other, rest_0))
    sends.arrived(17, at(far, other, rest_1))
    sends.drain()
    keep.wait()


def hx_gather(a, call_id, name):
    rows, cols = a.shape
    split = rows * 5 // 9 // 32 * 32
    sent = rows * cols * 2 * 7
    return pl.pallas_call(
        functools.partial(hx_gather_kernel, rows, cols, split),
        out_shape=jax.ShapeDtypeStruct((rows, cols * 8), a.dtype),
        in_specs=[pl.BlockSpec(memory_space=pl.ANY)],
        out_specs=pl.BlockSpec(memory_space=pl.ANY),
        scratch_shapes=[
            pltpu.VMEM((rows, cols), a.dtype),
            pltpu.SemaphoreType.DMA((2,)),
            pltpu.SemaphoreType.DMA((18,)),
            pltpu.SemaphoreType.DMA((18,)),
        ],
        compiler_params=pltpu.CompilerParams(collective_id=call_id, has_side_effects=True),
        name=name,
    )(a)


def ctx_gather_kernel(rows, a, out, transit, held, local_sem, send_sem, recv_sem):
    z_hi, x, core, y, z_lo = place()
    hx = y * 2 + z_lo
    z = z_hi * 2 + z_lo
    up, down = (z + 1) % 4, (z + 3) % 4
    right, left, far = (x + 1) % 4, (x + 3) % 4, (x + 2) % 4
    other = 1 - z_hi
    to_right, to_left = (ctx_of(z_hi, right, core), hx), (ctx_of(z_hi, left, core), hx)
    to_up = (ctx_of(up // 2, x, core), y * 2 + up % 2)
    to_down = (ctx_of(down // 2, x, core), y * 2 + down % 2)
    to_core = (ctx_of(z_hi, x, 1 - core), hx)
    load = pltpu.make_async_copy(a, held, local_sem.at[0])
    load.start()
    greet((to_right, to_left, to_up, to_down, to_core))
    whole, half_0, half_1 = (0, rows), (0, rows // 2), (rows // 2, rows // 2)

    def at(z_of, x_of, core_of, part):
        return out.at[pl.ds(ctx_of(z_of, x_of, core_of) * rows + part[0], part[1]), :]

    def own(part):
        return a.at[pl.ds(part[0], part[1]), :]

    sends = Sends(send_sem, recv_sem)

    def forward(k, z_of, x_of, part, device):
        sends.start(k, at(z_of, x_of, core, part), at(z_of, x_of, core, part), device)

    def arrived(k, z_of, x_of, part):
        sends.arrived(k, at(z_of, x_of, core, part))

    sends.start(0, own(half_0), transit.at[0], to_up)
    sends.start(1, own(half_1), transit.at[1], to_down)
    sends.start(2, own(whole), at(z_hi, x, core, whole), to_right)
    sends.start(3, own(whole), at(z_hi, x, core, whole), to_left)
    sends.start(4, own(whole), at(z_hi, x, core, whole), to_core)
    load.wait()
    keep = pltpu.make_async_copy(held, at(z_hi, x, core, whole), local_sem.at[1])
    keep.start()
    sends.arrived(0, transit.at[0])
    sends.start(5, transit.at[0], at(down // 2, x, core, half_0), to_up)
    sends.arrived(1, transit.at[1])
    sends.start(6, transit.at[1], at(up // 2, x, core, half_1), to_down)
    arrived(2, z_hi, left, whole)
    forward(10, z_hi, left, half_0, to_right)
    forward(11, z_hi, left, whole, to_core)
    arrived(3, z_hi, right, whole)
    forward(12, z_hi, right, half_1, to_left)
    forward(13, z_hi, right, whole, to_core)
    arrived(5, other, x, half_0)
    arrived(6, other, x, half_1)
    forward(7, other, x, whole, to_right)
    forward(8, other, x, whole, to_left)
    forward(9, other, x, whole, to_core)
    arrived(10, z_hi, far, half_0)
    arrived(12, z_hi, far, half_1)
    forward(18, z_hi, far, whole, to_core)
    arrived(7, other, left, whole)
    forward(14, other, left, half_0, to_right)
    forward(15, other, left, whole, to_core)
    arrived(8, other, right, whole)
    forward(16, other, right, half_1, to_left)
    forward(17, other, right, whole, to_core)
    arrived(14, other, far, half_0)
    arrived(16, other, far, half_1)
    forward(19, other, far, whole, to_core)

    def from_core(k, z_of, x_of):
        sends.arrived(k, at(z_of, x_of, 1 - core, whole))

    from_core(4, z_hi, x)
    from_core(11, z_hi, left)
    from_core(13, z_hi, right)
    from_core(9, other, x)
    from_core(18, z_hi, far)
    from_core(15, other, left)
    from_core(17, other, right)
    from_core(19, other, far)
    sends.drain()
    keep.wait()


def ctx_gather(a, call_id, name):
    rows, cols = a.shape
    return pl.pallas_call(
        functools.partial(ctx_gather_kernel, rows),
        out_shape=(
            jax.ShapeDtypeStruct((rows * 16, cols), a.dtype),
            jax.ShapeDtypeStruct((2, rows // 2, cols), a.dtype),
        ),
        in_specs=[pl.BlockSpec(memory_space=pl.ANY)],
        out_specs=(pl.BlockSpec(memory_space=pl.ANY), pl.BlockSpec(memory_space=pl.ANY)),
        scratch_shapes=[
            pltpu.VMEM((rows, cols), a.dtype),
            pltpu.SemaphoreType.DMA((2,)),
            pltpu.SemaphoreType.DMA((20,)),
            pltpu.SemaphoreType.DMA((20,)),
        ],
        compiler_params=pltpu.CompilerParams(collective_id=call_id, has_side_effects=True),
        name=name,
    )(a)[0]


def hx_spread_kernel(rows, cols, pick, a, out, held, local_sem, send_sem, recv_sem):
    ctx, me = lax.axis_index("ctx"), lax.axis_index("hx")

    def block(p):
        return a.at[:, pl.ds(p * cols, cols)] if pick else a

    load = pltpu.make_async_copy(block(me), held, local_sem.at[0])
    load.start()
    greet([(ctx, (me + k) % 8) for k in range(1, 8)])
    sends = Sends(send_sem, recv_sem)
    for k in range(1, 8):
        peer = (me + k) % 8
        sends.start(k, block(peer), out.at[pl.ds(me * rows, rows), :], (ctx, peer))
    load.wait()
    keep = pltpu.make_async_copy(held, out.at[pl.ds(me * rows, rows), :], local_sem.at[1])
    keep.start()
    for k in range(1, 8):
        sends.arrived(k, out.at[pl.ds((me + 8 - k) % 8 * rows, rows), :])
    sends.drain()
    keep.wait()


def hx_spread(a, cols, pick, call_id, name):
    rows = a.shape[0]
    return pl.pallas_call(
        functools.partial(hx_spread_kernel, rows, cols, pick),
        out_shape=jax.ShapeDtypeStruct((rows * 8, cols), a.dtype),
        in_specs=[pl.BlockSpec(memory_space=pl.ANY)],
        out_specs=pl.BlockSpec(memory_space=pl.ANY),
        scratch_shapes=[
            pltpu.VMEM((rows, cols), a.dtype),
            pltpu.SemaphoreType.DMA((2,)),
            pltpu.SemaphoreType.DMA((8,)),
            pltpu.SemaphoreType.DMA((8,)),
        ],
        compiler_params=pltpu.CompilerParams(collective_id=call_id, has_side_effects=True),
        name=name,
    )(a)


def ctx_exchange_kernel(rows, a, out, held, local_sem, send_sem, recv_sem):
    me, hx = lax.axis_index("ctx"), lax.axis_index("hx")

    def block(ref, p):
        return ref.at[pl.ds(p * rows, rows), :]

    load = pltpu.make_async_copy(block(a, me), held, local_sem.at[0])
    load.start()
    greet([((me + k) % 16, hx) for k in range(1, 16)])
    sends = Sends(send_sem, recv_sem)
    for k in range(1, 16):
        peer = (me + k) % 16
        sends.start(k, block(a, peer), block(out, me), (peer, hx))
    load.wait()
    keep = pltpu.make_async_copy(held, block(out, me), local_sem.at[1])
    keep.start()
    for k in range(1, 16):
        sends.arrived(k, block(out, (me + 16 - k) % 16))
    sends.drain()
    keep.wait()


def ctx_exchange(a, call_id, name):
    rows, cols = a.shape[0] // 16, a.shape[1]
    return pl.pallas_call(
        functools.partial(ctx_exchange_kernel, rows),
        out_shape=jax.ShapeDtypeStruct(a.shape, a.dtype),
        in_specs=[pl.BlockSpec(memory_space=pl.ANY)],
        out_specs=pl.BlockSpec(memory_space=pl.ANY),
        scratch_shapes=[
            pltpu.VMEM((rows, cols), a.dtype),
            pltpu.SemaphoreType.DMA((2,)),
            pltpu.SemaphoreType.DMA((16,)),
            pltpu.SemaphoreType.DMA((16,)),
        ],
        compiler_params=pltpu.CompilerParams(collective_id=call_id, has_side_effects=True),
        name=name,
    )(a)


def attend_kernel(q_t, kv, out):
    me = lax.axis_index("ctx")
    tok = q_t.shape[1]
    heads = q_t.shape[0] // HD
    scale = HD ** (-0.5) * math.log2(math.e)

    def visit(block, held, diagonal):
        at = pl.multiple_of(block * tok, tok)
        keys = kv[pl.ds(at, tok), :HD]
        values = kv[pl.ds(at, tok), HD:]
        new = []
        for h in range(heads):
            top, total, acc = held[h]
            scores = jnp.dot(keys, q_t[h * HD : (h + 1) * HD, :], preferred_element_type=jnp.float32) * scale
            if diagonal:
                key_pos = lax.broadcasted_iota(jnp.int32, scores.shape, 0)
                query_pos = lax.broadcasted_iota(jnp.int32, scores.shape, 1)
                scores = jnp.where(key_pos <= query_pos, scores, -1e30)
            new_top = jnp.maximum(top, jnp.max(scores, axis=0, keepdims=True))
            weights = jnp.exp2(scores - new_top)
            factor = jnp.exp2(top - new_top)
            total = total * factor + jnp.sum(weights, axis=0, keepdims=True)
            mixed = lax.dot_general(
                values,
                weights.astype(jnp.bfloat16),
                (((0,), (0,)), ((), ())),
                preferred_element_type=jnp.float32,
            )
            new.append((new_top, total, acc * factor + mixed))
        return tuple(new)

    start = tuple(
        (
            jnp.full((1, tok), -1e30, jnp.float32),
            jnp.zeros((1, tok), jnp.float32),
            jnp.zeros((HD, tok), jnp.float32),
        )
        for _ in range(heads)
    )
    held = visit(me, start, True)
    held = lax.fori_loop(0, me, lambda b, held: visit(b, held, False), held)
    for h in range(heads):
        top, total, acc = held[h]
        out[:, h * HD : (h + 1) * HD] = (acc / total).T.astype(out.dtype)


def attend(q_t, kv):
    cols, tok = q_t.shape
    return pl.pallas_call(
        attend_kernel,
        out_shape=jax.ShapeDtypeStruct((tok, cols), jnp.bfloat16),
        in_specs=[pl.BlockSpec(memory_space=pltpu.VMEM)] * 2,
        out_specs=pl.BlockSpec(memory_space=pltpu.VMEM),
        compiler_params=pltpu.CompilerParams(vmem_limit_bytes=48 << 20),
        cost_estimate=pl.CostEstimate(
            flops=cols * kv.shape[0] * tok * 4,
            bytes_accessed=kv.size * 2,
            transcendentals=cols // HD * tok * kv.shape[0],
        ),
        name="attend",
    )(q_t, kv)


def body(tokens, attn_gain, ffn_gain, w_query, w_key, w_value, w_out, w_router, routes, w_gate, w_up, w_down):
    f32, bf16 = jnp.float32, jnp.bfloat16
    hx = lax.axis_index("hx")
    tok_rows, full_width = tokens.shape
    width = full_width // 8
    q_cols = w_query.shape[1]

    out_cols = lax.all_to_all(w_out, "hx", split_axis=1, concat_axis=0, tiled=True)
    down_cols = lax.all_to_all(w_down[0], "hx", split_axis=1, concat_axis=0, tiled=True)

    weights = ctx_gather(jnp.concatenate((w_query, w_key, w_value), axis=1), 2, "gather_weights")
    floats = tokens.astype(f32)
    inverse = lax.rsqrt(jnp.mean(floats * floats, axis=-1, keepdims=True) + epsilon)
    normed = (floats * inverse * attn_gain.astype(f32)).astype(bf16)
    q_t = jnp.einsum("td,dc->ct", normed, weights[:, :q_cols], preferred_element_type=f32).astype(bf16)
    kv_own = jnp.dot(normed, weights[:, q_cols:], preferred_element_type=f32).astype(bf16)
    kv = ctx_gather(kv_own, 3, "gather_kv")
    attended = hx_gather(attend(q_t, kv), 4, "gather_attended")

    share = jnp.dot(attended, out_cols, preferred_element_type=f32)
    own_tokens = lax.dynamic_slice_in_dim(tokens, hx * width, width, 1)
    own_gain = lax.dynamic_slice_in_dim(ffn_gain, hx * width, width, 0).astype(f32)
    own_router = lax.dynamic_slice_in_dim(w_router, hx * width, width, 0)
    stream = (own_tokens.astype(f32) + share).astype(bf16)
    stream_f = stream.astype(f32)

    experts = w_router.shape[1]
    chosen = routes[:, 0]
    onehot = chosen[:, None] == jnp.arange(experts, dtype=jnp.int32)[None, :]
    capacity = tok_rows // 8
    counts = jnp.cumsum(onehot.astype(jnp.int32), axis=0)
    position = jnp.sum(jnp.where(onehot, counts, 0), axis=-1) - 1
    slot = chosen * capacity + position
    picks = (slot[None, :] == jnp.arange(experts * capacity, dtype=jnp.int32)[:, None]).astype(bf16)

    gained = stream_f * own_gain
    part_logits = jnp.dot(gained.astype(bf16), own_router, preferred_element_type=f32)
    part_logit = jnp.sum(jnp.where(onehot, part_logits, 0.0), axis=-1)
    part_square = jnp.sum(stream_f * stream_f, axis=-1)
    parts = jnp.concatenate(
        (part_square[None, :], part_logit[None, :], jnp.zeros((6, tok_rows), f32)), axis=0
    )
    sums = jnp.sum(hx_spread(parts, tok_rows, False, 7, "gather_sums").reshape(8, 8, tok_rows), axis=0)
    inverse2 = lax.rsqrt(sums[0] / full_width + epsilon)[:, None]
    score = jax.nn.sigmoid(sums[1][:, None] * inverse2)
    normed2 = (stream_f * inverse2 * own_gain).astype(bf16)
    routed = (normed2.astype(f32) * score).astype(bf16)
    buffer = jnp.dot(picks, routed, preferred_element_type=f32).astype(bf16)
    arrived = ctx_exchange(buffer, 6, "dispatch")
    rows = hx_gather(arrived, 1, "gather_rows")
    gate = jnp.dot(rows, w_gate[0], preferred_element_type=f32)
    up = jnp.dot(rows, w_up[0], preferred_element_type=f32)
    hidden = (jax.nn.silu(gate) * up).astype(bf16)
    hidden_all = hx_gather(hidden, 8, "gather_hidden")
    expert_rows = jnp.dot(hidden_all, down_cols, preferred_element_type=f32).astype(bf16)
    returned = ctx_exchange(expert_rows, 9, "give_back")
    expert_out = lax.dot_general(picks, returned, (((0,), (0,)), ((), ())), preferred_element_type=f32)
    return (stream_f + expert_out.astype(bf16).astype(f32)).astype(bf16)


def solution(mesh):
    in_specs = (
        P("ctx", None),
        P(),
        P(),
        P("ctx", "hx"),
        P("ctx", "hx"),
        P("ctx", "hx"),
        P("hx", None),
        P(),
        P("ctx", None),
        P("ctx", None, "hx"),
        P("ctx", None, "hx"),
        P("ctx", "hx", None),
    )
    return jax.shard_map(body, mesh=mesh, in_specs=in_specs, out_specs=P("ctx", "hx"), check_vma=False)
```

```python
import functools
import math
import jax
import jax.numpy as jnp
from jax import lax
from jax.experimental import pallas as pl
from jax.experimental.pallas import tpu as pltpu
from jax.sharding import PartitionSpec as P

HD = 128
epsilon = 1e-05
MESH = pl.DeviceIdType.MESH


def place():
    ctx, hx = lax.axis_index("ctx"), lax.axis_index("hx")
    z_hi, x, core = ctx // 8, (ctx // 2) % 4, ctx % 2
    y, z_lo = hx // 2, hx % 2
    return z_hi, x, core, y, z_lo


def ctx_of(z_hi, x, core):
    return z_hi * 8 + x * 2 + core


def greet(devices):
    barrier = pltpu.get_barrier_semaphore()
    for device in devices:
        pl.semaphore_signal(barrier, inc=1, device_id=device, device_id_type=MESH)
    pl.semaphore_wait(barrier, len(devices))


class Sends:
    def __init__(self, send_sem, recv_sem):
        self.send_sem, self.recv_sem, self.started = send_sem, recv_sem, []

    def start(self, k, src, dst, device):
        copy = pltpu.make_async_remote_copy(
            src_ref=src,
            dst_ref=dst,
            send_sem=self.send_sem.at[k],
            recv_sem=self.recv_sem.at[k],
            device_id=device,
            device_id_type=MESH,
        )
        copy.start()
        self.started.append(copy)

    def arrived(self, k, dst):
        pltpu.make_async_copy(dst, dst, self.recv_sem.at[k]).wait()

    def drain(self):
        for copy in self.started:
            copy.wait_send()


def hx_gather_kernel(rows, cols, split, a, out, held, local_sem, send_sem, recv_sem):
    z_hi, x, core, y, z_lo = place()
    ctx = ctx_of(z_hi, x, core)
    right, left, far = (y + 1) % 4, (y + 3) % 4, (y + 2) % 4
    other = 1 - z_lo
    to_right, to_left, to_z = (ctx, right * 2 + z_lo), (ctx, left * 2 + z_lo), (ctx, y * 2 + other)
    load = pltpu.make_async_copy(a, held, local_sem.at[0])
    load.start()
    greet((to_right, to_left, to_z))

    first = (0, split)
    first_0, first_1 = (0, split // 2), (split // 2, split // 2)
    rest = (split, rows - split)
    half = (rows - split) // 2
    rest_0, rest_1 = (split, half), (split + half, half)

    def at(y_of, z_of, part):
        return out.at[pl.ds(part[0], part[1]), pl.ds((y_of * 2 + z_of) * cols, cols)]

    def own(part):
        return a.at[pl.ds(part[0], part[1]), :]

    sends = Sends(send_sem, recv_sem)

    def forward(k, y_of, z_of, part, device):
        sends.start(k, at(y_of, z_of, part), at(y_of, z_of, part), device)

    sends.start(0, own(first), at(y, z_lo, first), to_z)
    sends.start(1, own(first), at(y, z_lo, first), to_right)
    sends.start(2, own(first), at(y, z_lo, first), to_left)
    sends.start(3, own(rest), at(y, z_lo, rest), to_right)
    sends.start(4, own(rest), at(y, z_lo, rest), to_left)
    sends.start(5, own(rest), at(y, z_lo, rest), to_z)
    load.wait()
    keep = pltpu.make_async_copy(held, out.at[:, pl.ds((y * 2 + z_lo) * cols, cols)], local_sem.at[1])
    keep.start()
    sends.arrived(0, at(y, other, first))
    forward(6, y, other, first, to_right)
    forward(7, y, other, first, to_left)
    sends.arrived(3, at(left, z_lo, rest))
    forward(10, left, z_lo, rest_0, to_right)
    forward(11, left, z_lo, rest, to_z)
    sends.arrived(4, at(right, z_lo, rest))
    forward(12, right, z_lo, rest_1, to_left)
    forward(13, right, z_lo, rest, to_z)
    sends.arrived(1, at(left, z_lo, first))
    forward(8, left, z_lo, first_0, to_right)
    sends.arrived(2, at(right, z_lo, first))
    forward(9, right, z_lo, first_1, to_left)
    sends.arrived(6, at(left, other, first))
    forward(14, left, other, first_0, to_right)
    sends.arrived(7, at(right, other, first))
    forward(15, right, other, first_1, to_left)
    sends.arrived(10, at(far, z_lo, rest_0))
    forward(16, far, z_lo, rest_0, to_z)
    sends.arrived(12, at(far, z_lo, rest_1))
    forward(17, far, z_lo, rest_1, to_z)
    sends.arrived(5, at(y, other, rest))
    sends.arrived(8, at(far, z_lo, first_0))
    sends.arrived(9, at(far, z_lo, first_1))
    sends.arrived(11, at(left, other, rest))
    sends.arrived(13, at(right, other, rest))
    sends.arrived(14, at(far, other, first_0))
    sends.arrived(15, at(far, other, first_1))
    sends.arrived(16, at(far, other, rest_0))
    sends.arrived(17, at(far, other, rest_1))
    sends.drain()
    keep.wait()


def hx_gather(a, call_id, name):
    rows, cols = a.shape
    split = rows * 5 // 9 // 32 * 32
    sent = rows * cols * 2 * 7
    return pl.pallas_call(
        functools.partial(hx_gather_kernel, rows, cols, split),
        out_shape=jax.ShapeDtypeStruct((rows, cols * 8), a.dtype),
        in_specs=[pl.BlockSpec(memory_space=pl.ANY)],
        out_specs=pl.BlockSpec(memory_space=pl.ANY),
        scratch_shapes=[
            pltpu.VMEM((rows, cols), a.dtype),
            pltpu.SemaphoreType.DMA((2,)),
            pltpu.SemaphoreType.DMA((18,)),
            pltpu.SemaphoreType.DMA((18,)),
        ],
        compiler_params=pltpu.CompilerParams(collective_id=call_id, has_side_effects=True),
        name=name,
    )(a)


def ctx_gather_steps(rows, a, out, transit, sends, keep_own, hooks):
    z_hi, x, core, y, z_lo = place()
    hx = y * 2 + z_lo
    z = z_hi * 2 + z_lo
    up, down = (z + 1) % 4, (z + 3) % 4
    right, left, far = (x + 1) % 4, (x + 3) % 4, (x + 2) % 4
    other = 1 - z_hi
    to_right, to_left = (ctx_of(z_hi, right, core), hx), (ctx_of(z_hi, left, core), hx)
    to_up = (ctx_of(up // 2, x, core), y * 2 + up % 2)
    to_down = (ctx_of(down // 2, x, core), y * 2 + down % 2)
    to_core = (ctx_of(z_hi, x, 1 - core), hx)
    whole, half_0, half_1 = (0, rows), (0, rows // 2), (rows // 2, rows // 2)

    def at(z_of, x_of, core_of, part):
        return out.at[pl.ds(ctx_of(z_of, x_of, core_of) * rows + part[0], part[1]), :]

    def own(part):
        return a.at[pl.ds(part[0], part[1]), :]

    def forward(k, z_of, x_of, part, device):
        sends.start(k, at(z_of, x_of, core, part), at(z_of, x_of, core, part), device)

    def arrived(k, z_of, x_of, part):
        sends.arrived(k, at(z_of, x_of, core, part))

    sends.start(0, own(half_0), transit.at[0], to_up)
    sends.start(1, own(half_1), transit.at[1], to_down)
    sends.start(2, own(whole), at(z_hi, x, core, whole), to_right)
    sends.start(3, own(whole), at(z_hi, x, core, whole), to_left)
    sends.start(4, own(whole), at(z_hi, x, core, whole), to_core)
    keep_own(at(z_hi, x, core, whole))
    sends.arrived(0, transit.at[0])
    sends.start(5, transit.at[0], at(down // 2, x, core, half_0), to_up)
    sends.arrived(1, transit.at[1])
    sends.start(6, transit.at[1], at(up // 2, x, core, half_1), to_down)
    hooks[0]()
    arrived(2, z_hi, left, whole)
    forward(10, z_hi, left, half_0, to_right)
    forward(11, z_hi, left, whole, to_core)
    arrived(3, z_hi, right, whole)
    forward(12, z_hi, right, half_1, to_left)
    forward(13, z_hi, right, whole, to_core)
    arrived(5, other, x, half_0)
    arrived(6, other, x, half_1)
    forward(7, other, x, whole, to_right)
    forward(8, other, x, whole, to_left)
    forward(9, other, x, whole, to_core)
    hooks[1]()
    arrived(10, z_hi, far, half_0)
    arrived(12, z_hi, far, half_1)
    forward(18, z_hi, far, whole, to_core)
    hooks[2]()
    arrived(7, other, left, whole)
    forward(14, other, left, half_0, to_right)
    forward(15, other, left, whole, to_core)
    arrived(8, other, right, whole)
    forward(16, other, right, half_1, to_left)
    forward(17, other, right, whole, to_core)
    arrived(14, other, far, half_0)
    arrived(16, other, far, half_1)
    forward(19, other, far, whole, to_core)

    def from_core(k, z_of, x_of):
        sends.arrived(k, at(z_of, x_of, 1 - core, whole))

    from_core(4, z_hi, x)
    from_core(11, z_hi, left)
    from_core(13, z_hi, right)
    from_core(9, other, x)
    from_core(18, z_hi, far)
    from_core(15, other, left)
    from_core(17, other, right)
    from_core(19, other, far)


def ctx_neighbours():
    z_hi, x, core, y, z_lo = place()
    hx = y * 2 + z_lo
    z = z_hi * 2 + z_lo
    up, down = (z + 1) % 4, (z + 3) % 4
    return (
        (ctx_of(z_hi, (x + 1) % 4, core), hx),
        (ctx_of(z_hi, (x + 3) % 4, core), hx),
        (ctx_of(up // 2, x, core), y * 2 + up % 2),
        (ctx_of(down // 2, x, core), y * 2 + down % 2),
        (ctx_of(z_hi, x, 1 - core), hx),
    )


def gather_weights_kernel(
    rows, a, w_out, w_down, out, transit, out_cols, down_cols, held, held_out, held_down, local_sem, send_sem, recv_sem
):
    z_hi, x, core, y, z_lo = place()
    ctx, me = ctx_of(z_hi, x, core), y * 2 + z_lo
    depth, width = w_out.shape[0], out_cols.shape[1]
    deep = w_down.shape[0]
    part = depth // 2
    mine = pl.ds(me * width, width)
    loads = (
        pltpu.make_async_copy(a, held, local_sem.at[0]),
        pltpu.make_async_copy(w_out.at[:, mine], held_out, local_sem.at[1]),
        pltpu.make_async_copy(w_down.at[:, mine], held_down, local_sem.at[2]),
    )
    for load in loads:
        load.start()
    greet(ctx_neighbours() + tuple((ctx, (me + k) % 8) for k in range(1, 8)))
    sends = Sends(send_sem, recv_sem)
    keeps = []

    def cut(y_step, flip):
        return (y + y_step) % 4 * 2 + (1 - z_lo if flip else z_lo)

    order = ((1, 0), (3, 0), (2, 0), (0, 1), (1, 1), (3, 1), (2, 1))

    def share(i):
        peer = cut(*order[i])
        src = w_out.at[pl.ds(core * part, part), pl.ds(peer * width, width)]
        sends.start(20 + i, src, out_cols.at[pl.ds(me * depth + core * part, part), :], (ctx, peer))

    def keep_own(place_own):
        for load in loads:
            load.wait()
        for held_ref, dst in (
            (held, place_own),
            (held_out, out_cols.at[pl.ds(me * depth, depth), :]),
            (held_down, down_cols.at[pl.ds(me * deep, deep), :]),
        ):
            keep = pltpu.make_async_copy(held_ref, dst, local_sem.at[3 + len(keeps)])
            keep.start()
            keeps.append(keep)
        for i in range(3):
            share(i)

    def cross():
        for i in range(3, 7):
            share(i)
        peer = cut(0, 1)
        src = w_down.at[pl.ds(0, deep // 2), pl.ds(peer * width, width)]
        sends.start(34, src, down_cols.at[pl.ds(me * deep, deep // 2), :], (ctx, peer))

    def hand_on(first, last):
        for i in range(first, last):
            y_step, flip = order[i]
            source = cut((4 - y_step) % 4, flip)
            block = out_cols.at[pl.ds(source * depth + core * part, part), :]
            sends.arrived(20 + i, block)
            sends.start(27 + i, block, block, (ctx_of(z_hi, x, 1 - core), me))

    ctx_gather_steps(
        rows, a, out, transit, sends, keep_own, (cross, lambda: hand_on(0, 2), lambda: hand_on(2, 3))
    )
    hand_on(3, 7)
    for i in range(7):
        y_step, flip = order[i]
        source = cut((4 - y_step) % 4, flip)
        sends.arrived(27 + i, out_cols.at[pl.ds(source * depth + (1 - core) * part, part), :])
    sends.arrived(34, down_cols.at[pl.ds(cut(0, 1) * deep, deep // 2), :])
    sends.drain()
    for keep in keeps:
        keep.wait()


ANY = pl.BlockSpec(memory_space=pl.ANY)


def gather_weights(a, w_out, w_down, call_id):
    rows, cols = a.shape
    depth, deep, width = w_out.shape[0], w_down.shape[0], w_out.shape[1] // 8
    weights, _, out_cols, down_cols = pl.pallas_call(
        functools.partial(gather_weights_kernel, rows),
        out_shape=(
            jax.ShapeDtypeStruct((rows * 16, cols), a.dtype),
            jax.ShapeDtypeStruct((2, rows // 2, cols), a.dtype),
            jax.ShapeDtypeStruct((depth * 8, width), a.dtype),
            jax.ShapeDtypeStruct((deep * 8, width), a.dtype),
        ),
        in_specs=[ANY] * 3,
        out_specs=(ANY,) * 4,
        scratch_shapes=[
            pltpu.VMEM((rows, cols), a.dtype),
            pltpu.VMEM((depth, width), a.dtype),
            pltpu.VMEM((deep, width), a.dtype),
            pltpu.SemaphoreType.DMA((6,)),
            pltpu.SemaphoreType.DMA((35,)),
            pltpu.SemaphoreType.DMA((35,)),
        ],
        compiler_params=pltpu.CompilerParams(collective_id=call_id, has_side_effects=True),
        name="gather_weights",
    )(a, w_out, w_down)
    return weights, out_cols, down_cols


def gather_kv_kernel(rows, a, w_down, _, out, transit, passing, down_cols, held, local_sem, send_sem, recv_sem):
    z_hi, x, core, y, z_lo = place()
    ctx, me = ctx_of(z_hi, x, core), y * 2 + z_lo
    deep, width = w_down.shape[0], down_cols.shape[1]
    half = deep // 2
    right, left, far, other = (y + 1) % 4, (y + 3) % 4, (y + 2) % 4, 1 - z_lo
    to_right, to_left = (ctx, right * 2 + z_lo), (ctx, left * 2 + z_lo)
    across_right, across_left = (ctx, right * 2 + other), (ctx, left * 2 + other)
    load = pltpu.make_async_copy(a, held, local_sem.at[0])
    load.start()
    greet(ctx_neighbours() + (to_right, to_left, across_right, across_left, (ctx, y * 2 + other)))
    sends = Sends(send_sem, recv_sem)
    keeps = []

    def cut(h, target):
        return w_down.at[pl.ds(h * half, half), pl.ds(target * width, width)]

    def rows_of(source, h):
        return down_cols.at[pl.ds(source * deep + h * half, half), :]

    def keep_own(place_own):
        load.wait()
        keep = pltpu.make_async_copy(held, place_own, local_sem.at[1])
        keep.start()
        keeps.append(keep)
        sends.start(20, cut(0, far * 2 + z_lo), passing.at[0], to_right)
        sends.start(21, cut(0, far * 2 + other), passing.at[1], to_right)
        sends.start(22, cut(1, far * 2 + z_lo), passing.at[2], to_left)
        sends.start(23, cut(1, far * 2 + other), passing.at[3], to_left)

    def cross():
        sends.start(28, cut(1, y * 2 + other), rows_of(me, 1), (ctx, y * 2 + other))

    def near():
        sends.arrived(20, passing.at[0])
        sends.start(24, passing.at[0], rows_of(left * 2 + z_lo, 0), to_right)
        sends.arrived(22, passing.at[2])
        sends.start(26, passing.at[2], rows_of(right * 2 + z_lo, 1), to_left)

    def across():
        sends.arrived(21, passing.at[1])
        sends.start(25, passing.at[1], rows_of(left * 2 + z_lo, 0), across_right)
        sends.arrived(23, passing.at[3])
        sends.start(27, passing.at[3], rows_of(right * 2 + z_lo, 1), across_left)

    ctx_gather_steps(rows, a, out, transit, sends, keep_own, (cross, near, across))
    sends.arrived(28, rows_of(y * 2 + other, 1))
    sends.arrived(24, rows_of(far * 2 + z_lo, 0))
    sends.arrived(26, rows_of(far * 2 + z_lo, 1))
    sends.arrived(25, rows_of(far * 2 + other, 0))
    sends.arrived(27, rows_of(far * 2 + other, 1))
    sends.drain()
    for keep in keeps:
        keep.wait()


def gather_kv(a, w_down, down_cols, call_id):
    rows, cols = a.shape
    deep, width = w_down.shape[0], w_down.shape[1] // 8
    kv, _, _, down_cols = pl.pallas_call(
        functools.partial(gather_kv_kernel, rows),
        out_shape=(
            jax.ShapeDtypeStruct((rows * 16, cols), a.dtype),
            jax.ShapeDtypeStruct((2, rows // 2, cols), a.dtype),
            jax.ShapeDtypeStruct((4, deep // 2, width), a.dtype),
            jax.ShapeDtypeStruct((deep * 8, width), a.dtype),
        ),
        in_specs=[ANY] * 3,
        out_specs=(ANY,) * 4,
        input_output_aliases={2: 3},
        scratch_shapes=[
            pltpu.VMEM((rows, cols), a.dtype),
            pltpu.SemaphoreType.DMA((2,)),
            pltpu.SemaphoreType.DMA((29,)),
            pltpu.SemaphoreType.DMA((29,)),
        ],
        compiler_params=pltpu.CompilerParams(collective_id=call_id, has_side_effects=True),
        name="gather_kv",
    )(a, w_down, down_cols)
    return kv, down_cols


def hx_spread_kernel(rows, cols, pick, a, out, held, local_sem, send_sem, recv_sem):
    ctx, me = lax.axis_index("ctx"), lax.axis_index("hx")

    def block(p):
        return a.at[:, pl.ds(p * cols, cols)] if pick else a

    load = pltpu.make_async_copy(block(me), held, local_sem.at[0])
    load.start()
    greet([(ctx, (me + k) % 8) for k in range(1, 8)])
    sends = Sends(send_sem, recv_sem)
    for k in range(1, 8):
        peer = (me + k) % 8
        sends.start(k, block(peer), out.at[pl.ds(me * rows, rows), :], (ctx, peer))
    load.wait()
    keep = pltpu.make_async_copy(held, out.at[pl.ds(me * rows, rows), :], local_sem.at[1])
    keep.start()
    for k in range(1, 8):
        sends.arrived(k, out.at[pl.ds((me + 8 - k) % 8 * rows, rows), :])
    sends.drain()
    keep.wait()


def hx_spread(a, cols, pick, call_id, name):
    rows = a.shape[0]
    return pl.pallas_call(
        functools.partial(hx_spread_kernel, rows, cols, pick),
        out_shape=jax.ShapeDtypeStruct((rows * 8, cols), a.dtype),
        in_specs=[pl.BlockSpec(memory_space=pl.ANY)],
        out_specs=pl.BlockSpec(memory_space=pl.ANY),
        scratch_shapes=[
            pltpu.VMEM((rows, cols), a.dtype),
            pltpu.SemaphoreType.DMA((2,)),
            pltpu.SemaphoreType.DMA((8,)),
            pltpu.SemaphoreType.DMA((8,)),
        ],
        compiler_params=pltpu.CompilerParams(collective_id=call_id, has_side_effects=True),
        name=name,
    )(a)


def ctx_exchange_kernel(rows, a, out, held, local_sem, send_sem, recv_sem):
    me, hx = lax.axis_index("ctx"), lax.axis_index("hx")

    def block(ref, p):
        return ref.at[pl.ds(p * rows, rows), :]

    load = pltpu.make_async_copy(block(a, me), held, local_sem.at[0])
    load.start()
    greet([((me + k) % 16, hx) for k in range(1, 16)])
    sends = Sends(send_sem, recv_sem)
    for k in range(1, 16):
        peer = (me + k) % 16
        sends.start(k, block(a, peer), block(out, me), (peer, hx))
    load.wait()
    keep = pltpu.make_async_copy(held, block(out, me), local_sem.at[1])
    keep.start()
    for k in range(1, 16):
        sends.arrived(k, block(out, (me + 16 - k) % 16))
    sends.drain()
    keep.wait()


def ctx_exchange(a, call_id, name):
    rows, cols = a.shape[0] // 16, a.shape[1]
    return pl.pallas_call(
        functools.partial(ctx_exchange_kernel, rows),
        out_shape=jax.ShapeDtypeStruct(a.shape, a.dtype),
        in_specs=[pl.BlockSpec(memory_space=pl.ANY)],
        out_specs=pl.BlockSpec(memory_space=pl.ANY),
        scratch_shapes=[
            pltpu.VMEM((rows, cols), a.dtype),
            pltpu.SemaphoreType.DMA((2,)),
            pltpu.SemaphoreType.DMA((16,)),
            pltpu.SemaphoreType.DMA((16,)),
        ],
        compiler_params=pltpu.CompilerParams(collective_id=call_id, has_side_effects=True),
        name=name,
    )(a)


def attend_kernel(q_t, kv, w_down, _, out, down_cols, send_sem, recv_sem):
    me, hx = lax.axis_index("ctx"), lax.axis_index("hx")
    y, z_lo = hx // 2, hx % 2
    deep, width = w_down.shape[0], down_cols.shape[1]
    order = ((1, 0), (3, 1), (1, 1), (3, 0))

    def peer_of(y_step, flip):
        return (y + y_step) % 4 * 2 + (1 - z_lo if flip else z_lo)

    greet([(me, peer_of(*step)) for step in order])
    sends = Sends(send_sem, recv_sem)
    for i, step in enumerate(order):
        peer = peer_of(*step)
        src = w_down.at[:, pl.ds(peer * width, width)]
        sends.start(i, src, down_cols.at[pl.ds(hx * deep, deep), :], (me, peer))
    tok = q_t.shape[1]
    heads = q_t.shape[0] // HD
    scale = HD ** (-0.5) * math.log2(math.e)

    def visit(block, held, diagonal):
        at = pl.multiple_of(block * tok, tok)
        keys = kv[pl.ds(at, tok), :HD]
        values = kv[pl.ds(at, tok), HD:]
        new = []
        for h in range(heads):
            top, total, acc = held[h]
            scores = jnp.dot(keys, q_t[h * HD : (h + 1) * HD, :], preferred_element_type=jnp.float32) * scale
            if diagonal:
                key_pos = lax.broadcasted_iota(jnp.int32, scores.shape, 0)
                query_pos = lax.broadcasted_iota(jnp.int32, scores.shape, 1)
                scores = jnp.where(key_pos <= query_pos, scores, -1e30)
            new_top = jnp.maximum(top, jnp.max(scores, axis=0, keepdims=True))
            weights = jnp.exp2(scores - new_top)
            factor = jnp.exp2(top - new_top)
            total = total * factor + jnp.sum(weights, axis=0, keepdims=True)
            mixed = lax.dot_general(
                values,
                weights.astype(jnp.bfloat16),
                (((0,), (0,)), ((), ())),
                preferred_element_type=jnp.float32,
            )
            new.append((new_top, total, acc * factor + mixed))
        return tuple(new)

    start = tuple(
        (
            jnp.full((1, tok), -1e30, jnp.float32),
            jnp.zeros((1, tok), jnp.float32),
            jnp.zeros((HD, tok), jnp.float32),
        )
        for _ in range(heads)
    )
    held = visit(me, start, True)
    held = lax.fori_loop(0, me, lambda b, held: visit(b, held, False), held)
    for h in range(heads):
        top, total, acc = held[h]
        out[:, h * HD : (h + 1) * HD] = (acc / total).T.astype(out.dtype)
    for i, (y_step, flip) in enumerate(order):
        source = peer_of(4 - y_step, flip)
        sends.arrived(i, down_cols.at[pl.ds(source * deep, deep), :])
    sends.drain()


def attend(q_t, kv, w_down, down_cols, call_id):
    cols, tok = q_t.shape
    return pl.pallas_call(
        attend_kernel,
        out_shape=(
            jax.ShapeDtypeStruct((tok, cols), jnp.bfloat16),
            jax.ShapeDtypeStruct(down_cols.shape, jnp.bfloat16),
        ),
        in_specs=[pl.BlockSpec(memory_space=pltpu.VMEM)] * 2 + [ANY] * 2,
        out_specs=(pl.BlockSpec(memory_space=pltpu.VMEM), ANY),
        input_output_aliases={3: 1},
        scratch_shapes=[pltpu.SemaphoreType.DMA((4,)), pltpu.SemaphoreType.DMA((4,))],
        compiler_params=pltpu.CompilerParams(
            vmem_limit_bytes=48 << 20, collective_id=call_id, has_side_effects=True
        ),
        cost_estimate=pl.CostEstimate(
            flops=cols * kv.shape[0] * tok * 4,
            bytes_accessed=kv.size * 2,
            transcendentals=cols // HD * tok * kv.shape[0],
        ),
        name="attend",
    )(q_t, kv, w_down, down_cols)


def body(tokens, attn_gain, ffn_gain, w_query, w_key, w_value, w_out, w_router, routes, w_gate, w_up, w_down):
    f32, bf16 = jnp.float32, jnp.bfloat16
    hx = lax.axis_index("hx")
    tok_rows, full_width = tokens.shape
    width = full_width // 8
    q_cols = w_query.shape[1]

    w_down = w_down[0]

    weights, out_cols, down_cols = gather_weights(
        jnp.concatenate((w_query, w_key, w_value), axis=1), w_out, w_down, 2
    )
    floats = tokens.astype(f32)
    inverse = lax.rsqrt(jnp.mean(floats * floats, axis=-1, keepdims=True) + epsilon)
    normed = (floats * inverse * attn_gain.astype(f32)).astype(bf16)
    q_t = jnp.einsum("td,dc->ct", normed, weights[:, :q_cols], preferred_element_type=f32).astype(bf16)
    kv_own = jnp.dot(normed, weights[:, q_cols:], preferred_element_type=f32).astype(bf16)
    kv, down_cols = gather_kv(kv_own, w_down, down_cols, 3)
    attended, down_cols = attend(q_t, kv, w_down, down_cols, 5)
    attended = hx_gather(attended, 4, "gather_attended")

    share = jnp.dot(attended, out_cols, preferred_element_type=f32)
    own_tokens = lax.dynamic_slice_in_dim(tokens, hx * width, width, 1)
    own_gain = lax.dynamic_slice_in_dim(ffn_gain, hx * width, width, 0).astype(f32)
    own_router = lax.dynamic_slice_in_dim(w_router, hx * width, width, 0)
    stream = (own_tokens.astype(f32) + share).astype(bf16)
    stream_f = stream.astype(f32)

    experts = w_router.shape[1]
    chosen = routes[:, 0]
    onehot = chosen[:, None] == jnp.arange(experts, dtype=jnp.int32)[None, :]
    capacity = tok_rows // 8
    counts = jnp.cumsum(onehot.astype(jnp.int32), axis=0)
    position = jnp.sum(jnp.where(onehot, counts, 0), axis=-1) - 1
    slot = chosen * capacity + position
    picks = (slot[None, :] == jnp.arange(experts * capacity, dtype=jnp.int32)[:, None]).astype(bf16)

    gained = stream_f * own_gain
    part_logits = jnp.dot(gained.astype(bf16), own_router, preferred_element_type=f32)
    part_logit = jnp.sum(jnp.where(onehot, part_logits, 0.0), axis=-1)
    part_square = jnp.sum(stream_f * stream_f, axis=-1)
    parts = jnp.concatenate(
        (part_square[None, :], part_logit[None, :], jnp.zeros((6, tok_rows), f32)), axis=0
    )
    sums = jnp.sum(hx_spread(parts, tok_rows, False, 7, "gather_sums").reshape(8, 8, tok_rows), axis=0)
    inverse2 = lax.rsqrt(sums[0] / full_width + epsilon)[:, None]
    score = jax.nn.sigmoid(sums[1][:, None] * inverse2)
    normed2 = (stream_f * inverse2 * own_gain).astype(bf16)
    routed = (normed2.astype(f32) * score).astype(bf16)
    buffer = jnp.dot(picks, routed, preferred_element_type=f32).astype(bf16)
    arrived = ctx_exchange(buffer, 6, "dispatch")
    rows = hx_gather(arrived, 1, "gather_rows")
    gate = jnp.dot(rows, w_gate[0], preferred_element_type=f32)
    up = jnp.dot(rows, w_up[0], preferred_element_type=f32)
    hidden = (jax.nn.silu(gate) * up).astype(bf16)
    hidden_all = hx_gather(hidden, 8, "gather_hidden")
    expert_rows = jnp.dot(hidden_all, down_cols, preferred_element_type=f32).astype(bf16)
    returned = ctx_exchange(expert_rows, 9, "give_back")
    expert_out = lax.dot_general(picks, returned, (((0,), (0,)), ((), ())), preferred_element_type=f32)
    return (stream_f + expert_out.astype(bf16).astype(f32)).astype(bf16)


def solution(mesh):
    in_specs = (
        P("ctx", None),
        P(),
        P(),
        P("ctx", "hx"),
        P("ctx", "hx"),
        P("ctx", "hx"),
        P("hx", None),
        P(),
        P("ctx", None),
        P("ctx", None, "hx"),
        P("ctx", None, "hx"),
        P("ctx", "hx", None),
    )
    return jax.shard_map(body, mesh=mesh, in_specs=in_specs, out_specs=P("ctx", "hx"), check_vma=False)
```

```python
import functools
import math
import jax
import jax.numpy as jnp
from jax import lax
from jax.experimental import pallas as pl
from jax.experimental.pallas import tpu as pltpu
from jax.sharding import PartitionSpec as P

HD = 128
epsilon = 1e-05
MESH = pl.DeviceIdType.MESH


def place():
    ctx, hx = lax.axis_index("ctx"), lax.axis_index("hx")
    z_hi, x, core = ctx // 8, (ctx // 2) % 4, ctx % 2
    y, z_lo = hx // 2, hx % 2
    return z_hi, x, core, y, z_lo


def ctx_of(z_hi, x, core):
    return z_hi * 8 + x * 2 + core


def greet(devices):
    barrier = pltpu.get_barrier_semaphore()
    for device in devices:
        pl.semaphore_signal(barrier, inc=1, device_id=device, device_id_type=MESH)
    pl.semaphore_wait(barrier, len(devices))


class Sends:
    def __init__(self, send_sem, recv_sem):
        self.send_sem, self.recv_sem, self.started = send_sem, recv_sem, []

    def start(self, k, src, dst, device):
        copy = pltpu.make_async_remote_copy(
            src_ref=src,
            dst_ref=dst,
            send_sem=self.send_sem.at[k],
            recv_sem=self.recv_sem.at[k],
            device_id=device,
            device_id_type=MESH,
        )
        copy.start()
        self.started.append(copy)

    def arrived(self, k, dst):
        pltpu.make_async_copy(dst, dst, self.recv_sem.at[k]).wait()

    def drain(self):
        for copy in self.started:
            copy.wait_send()


def hx_gather_kernel(rows, cols, split, a, out, held, local_sem, send_sem, recv_sem):
    z_hi, x, core, y, z_lo = place()
    ctx = ctx_of(z_hi, x, core)
    right, left, far = (y + 1) % 4, (y + 3) % 4, (y + 2) % 4
    other = 1 - z_lo
    to_right, to_left, to_z = (ctx, right * 2 + z_lo), (ctx, left * 2 + z_lo), (ctx, y * 2 + other)
    load = pltpu.make_async_copy(a, held, local_sem.at[0])
    load.start()
    greet((to_right, to_left, to_z))

    first = (0, split)
    first_0, first_1 = (0, split // 2), (split // 2, split // 2)
    rest = (split, rows - split)
    half = (rows - split) // 2
    rest_0, rest_1 = (split, half), (split + half, half)

    def at(y_of, z_of, part):
        return out.at[pl.ds(part[0], part[1]), pl.ds((y_of * 2 + z_of) * cols, cols)]

    def own(part):
        return a.at[pl.ds(part[0], part[1]), :]

    sends = Sends(send_sem, recv_sem)

    def forward(k, y_of, z_of, part, device):
        sends.start(k, at(y_of, z_of, part), at(y_of, z_of, part), device)

    sends.start(0, own(first), at(y, z_lo, first), to_z)
    sends.start(1, own(first), at(y, z_lo, first), to_right)
    sends.start(2, own(first), at(y, z_lo, first), to_left)
    sends.start(3, own(rest), at(y, z_lo, rest), to_right)
    sends.start(4, own(rest), at(y, z_lo, rest), to_left)
    sends.start(5, own(rest), at(y, z_lo, rest), to_z)
    load.wait()
    keep = pltpu.make_async_copy(held, out.at[:, pl.ds((y * 2 + z_lo) * cols, cols)], local_sem.at[1])
    keep.start()
    sends.arrived(0, at(y, other, first))
    forward(6, y, other, first, to_right)
    forward(7, y, other, first, to_left)
    sends.arrived(3, at(left, z_lo, rest))
    forward(10, left, z_lo, rest_0, to_right)
    forward(11, left, z_lo, rest, to_z)
    sends.arrived(4, at(right, z_lo, rest))
    forward(12, right, z_lo, rest_1, to_left)
    forward(13, right, z_lo, rest, to_z)
    sends.arrived(1, at(left, z_lo, first))
    forward(8, left, z_lo, first_0, to_right)
    sends.arrived(2, at(right, z_lo, first))
    forward(9, right, z_lo, first_1, to_left)
    sends.arrived(6, at(left, other, first))
    forward(14, left, other, first_0, to_right)
    sends.arrived(7, at(right, other, first))
    forward(15, right, other, first_1, to_left)
    sends.arrived(10, at(far, z_lo, rest_0))
    forward(16, far, z_lo, rest_0, to_z)
    sends.arrived(12, at(far, z_lo, rest_1))
    forward(17, far, z_lo, rest_1, to_z)
    sends.arrived(5, at(y, other, rest))
    sends.arrived(8, at(far, z_lo, first_0))
    sends.arrived(9, at(far, z_lo, first_1))
    sends.arrived(11, at(left, other, rest))
    sends.arrived(13, at(right, other, rest))
    sends.arrived(14, at(far, other, first_0))
    sends.arrived(15, at(far, other, first_1))
    sends.arrived(16, at(far, other, rest_0))
    sends.arrived(17, at(far, other, rest_1))
    sends.drain()
    keep.wait()


def hx_gather(a, call_id, name):
    rows, cols = a.shape
    split = rows * 5 // 9 // 32 * 32
    sent = rows * cols * 2 * 7
    return pl.pallas_call(
        functools.partial(hx_gather_kernel, rows, cols, split),
        out_shape=jax.ShapeDtypeStruct((rows, cols * 8), a.dtype),
        in_specs=[pl.BlockSpec(memory_space=pl.ANY)],
        out_specs=pl.BlockSpec(memory_space=pl.ANY),
        scratch_shapes=[
            pltpu.VMEM((rows, cols), a.dtype),
            pltpu.SemaphoreType.DMA((2,)),
            pltpu.SemaphoreType.DMA((18,)),
            pltpu.SemaphoreType.DMA((18,)),
        ],
        compiler_params=pltpu.CompilerParams(collective_id=call_id, has_side_effects=True),
        name=name,
    )(a)


def ctx_gather_steps(rows, a, out, transit, sends, keep_own, hooks):
    z_hi, x, core, y, z_lo = place()
    hx = y * 2 + z_lo
    z = z_hi * 2 + z_lo
    up, down = (z + 1) % 4, (z + 3) % 4
    right, left, far = (x + 1) % 4, (x + 3) % 4, (x + 2) % 4
    other = 1 - z_hi
    to_right, to_left = (ctx_of(z_hi, right, core), hx), (ctx_of(z_hi, left, core), hx)
    to_up = (ctx_of(up // 2, x, core), y * 2 + up % 2)
    to_down = (ctx_of(down // 2, x, core), y * 2 + down % 2)
    to_core = (ctx_of(z_hi, x, 1 - core), hx)
    whole, half_0, half_1 = (0, rows), (0, rows // 2), (rows // 2, rows // 2)

    def at(z_of, x_of, core_of, part):
        return out.at[pl.ds(ctx_of(z_of, x_of, core_of) * rows + part[0], part[1]), :]

    def own(part):
        return a.at[pl.ds(part[0], part[1]), :]

    def forward(k, z_of, x_of, part, device):
        sends.start(k, at(z_of, x_of, core, part), at(z_of, x_of, core, part), device)

    def arrived(k, z_of, x_of, part):
        sends.arrived(k, at(z_of, x_of, core, part))

    sends.start(0, own(half_0), transit.at[0], to_up)
    sends.start(1, own(half_1), transit.at[1], to_down)
    sends.start(2, own(whole), at(z_hi, x, core, whole), to_right)
    sends.start(3, own(whole), at(z_hi, x, core, whole), to_left)
    sends.start(4, own(whole), at(z_hi, x, core, whole), to_core)
    keep_own(at(z_hi, x, core, whole))
    sends.arrived(0, transit.at[0])
    sends.start(5, transit.at[0], at(down // 2, x, core, half_0), to_up)
    sends.arrived(1, transit.at[1])
    sends.start(6, transit.at[1], at(up // 2, x, core, half_1), to_down)
    hooks[0]()
    arrived(2, z_hi, left, whole)
    forward(10, z_hi, left, half_0, to_right)
    forward(11, z_hi, left, whole, to_core)
    arrived(3, z_hi, right, whole)
    forward(12, z_hi, right, half_1, to_left)
    forward(13, z_hi, right, whole, to_core)
    arrived(5, other, x, half_0)
    arrived(6, other, x, half_1)
    forward(7, other, x, whole, to_right)
    forward(8, other, x, whole, to_left)
    forward(9, other, x, whole, to_core)
    hooks[1]()
    arrived(10, z_hi, far, half_0)
    arrived(12, z_hi, far, half_1)
    forward(18, z_hi, far, whole, to_core)
    hooks[2]()
    arrived(7, other, left, whole)
    forward(14, other, left, half_0, to_right)
    forward(15, other, left, whole, to_core)
    arrived(8, other, right, whole)
    forward(16, other, right, half_1, to_left)
    forward(17, other, right, whole, to_core)
    arrived(14, other, far, half_0)
    arrived(16, other, far, half_1)
    forward(19, other, far, whole, to_core)

    def from_core(k, z_of, x_of):
        sends.arrived(k, at(z_of, x_of, 1 - core, whole))

    from_core(4, z_hi, x)
    from_core(11, z_hi, left)
    from_core(13, z_hi, right)
    from_core(9, other, x)
    from_core(18, z_hi, far)
    from_core(15, other, left)
    from_core(17, other, right)
    from_core(19, other, far)


def ctx_neighbours():
    z_hi, x, core, y, z_lo = place()
    hx = y * 2 + z_lo
    z = z_hi * 2 + z_lo
    up, down = (z + 1) % 4, (z + 3) % 4
    return (
        (ctx_of(z_hi, (x + 1) % 4, core), hx),
        (ctx_of(z_hi, (x + 3) % 4, core), hx),
        (ctx_of(up // 2, x, core), y * 2 + up % 2),
        (ctx_of(down // 2, x, core), y * 2 + down % 2),
        (ctx_of(z_hi, x, 1 - core), hx),
    )


def gather_weights_kernel(
    rows, a, w_out, w_down, out, transit, out_cols, down_cols, held, held_out, held_down, local_sem, send_sem, recv_sem
):
    z_hi, x, core, y, z_lo = place()
    ctx, me = ctx_of(z_hi, x, core), y * 2 + z_lo
    depth, width = w_out.shape[0], out_cols.shape[1]
    deep = w_down.shape[0]
    part = depth // 2
    mine = pl.ds(me * width, width)
    loads = (
        pltpu.make_async_copy(a, held, local_sem.at[0]),
        pltpu.make_async_copy(w_out.at[:, mine], held_out, local_sem.at[1]),
        pltpu.make_async_copy(w_down.at[:, mine], held_down, local_sem.at[2]),
    )
    for load in loads:
        load.start()
    greet(ctx_neighbours() + tuple((ctx, (me + k) % 8) for k in range(1, 8)))
    sends = Sends(send_sem, recv_sem)
    keeps = []

    def cut(y_step, flip):
        return (y + y_step) % 4 * 2 + (1 - z_lo if flip else z_lo)

    order = ((1, 0), (3, 0), (2, 0), (0, 1), (1, 1), (3, 1), (2, 1))

    def share(i):
        peer = cut(*order[i])
        src = w_out.at[pl.ds(core * part, part), pl.ds(peer * width, width)]
        sends.start(20 + i, src, out_cols.at[pl.ds(me * depth + core * part, part), :], (ctx, peer))

    def keep_own(place_own):
        for load in loads:
            load.wait()
        for held_ref, dst in (
            (held, place_own),
            (held_out, out_cols.at[pl.ds(me * depth, depth), :]),
            (held_down, down_cols.at[pl.ds(me * deep, deep), :]),
        ):
            keep = pltpu.make_async_copy(held_ref, dst, local_sem.at[3 + len(keeps)])
            keep.start()
            keeps.append(keep)
        for i in range(3):
            share(i)

    def cross():
        for i in range(3, 7):
            share(i)
        peer = cut(0, 1)
        src = w_down.at[pl.ds(0, deep // 2), pl.ds(peer * width, width)]
        sends.start(34, src, down_cols.at[pl.ds(me * deep, deep // 2), :], (ctx, peer))

    def hand_on(first, last):
        for i in range(first, last):
            y_step, flip = order[i]
            source = cut((4 - y_step) % 4, flip)
            block = out_cols.at[pl.ds(source * depth + core * part, part), :]
            sends.arrived(20 + i, block)
            sends.start(27 + i, block, block, (ctx_of(z_hi, x, 1 - core), me))

    ctx_gather_steps(
        rows, a, out, transit, sends, keep_own, (cross, lambda: hand_on(0, 2), lambda: hand_on(2, 3))
    )
    hand_on(3, 7)
    for i in range(7):
        y_step, flip = order[i]
        source = cut((4 - y_step) % 4, flip)
        sends.arrived(27 + i, out_cols.at[pl.ds(source * depth + (1 - core) * part, part), :])
    sends.arrived(34, down_cols.at[pl.ds(cut(0, 1) * deep, deep // 2), :])
    sends.drain()
    for keep in keeps:
        keep.wait()


ANY = pl.BlockSpec(memory_space=pl.ANY)


def gather_weights(a, w_out, w_down, call_id):
    rows, cols = a.shape
    depth, deep, width = w_out.shape[0], w_down.shape[0], w_out.shape[1] // 8
    weights, _, out_cols, down_cols = pl.pallas_call(
        functools.partial(gather_weights_kernel, rows),
        out_shape=(
            jax.ShapeDtypeStruct((rows * 16, cols), a.dtype),
            jax.ShapeDtypeStruct((2, rows // 2, cols), a.dtype),
            jax.ShapeDtypeStruct((depth * 8, width), a.dtype),
            jax.ShapeDtypeStruct((deep * 8, width), a.dtype),
        ),
        in_specs=[ANY] * 3,
        out_specs=(ANY,) * 4,
        scratch_shapes=[
            pltpu.VMEM((rows, cols), a.dtype),
            pltpu.VMEM((depth, width), a.dtype),
            pltpu.VMEM((deep, width), a.dtype),
            pltpu.SemaphoreType.DMA((6,)),
            pltpu.SemaphoreType.DMA((35,)),
            pltpu.SemaphoreType.DMA((35,)),
        ],
        compiler_params=pltpu.CompilerParams(collective_id=call_id, has_side_effects=True),
        name="gather_weights",
    )(a, w_out, w_down)
    return weights, out_cols, down_cols


def gather_kv_kernel(rows, a, w_down, _, out, transit, passing, down_cols, held, local_sem, send_sem, recv_sem):
    z_hi, x, core, y, z_lo = place()
    ctx, me = ctx_of(z_hi, x, core), y * 2 + z_lo
    deep, width = w_down.shape[0], down_cols.shape[1]
    half = deep // 2
    right, left, far, other = (y + 1) % 4, (y + 3) % 4, (y + 2) % 4, 1 - z_lo
    to_right, to_left = (ctx, right * 2 + z_lo), (ctx, left * 2 + z_lo)
    across_right, across_left = (ctx, right * 2 + other), (ctx, left * 2 + other)
    load = pltpu.make_async_copy(a, held, local_sem.at[0])
    load.start()
    greet(ctx_neighbours() + (to_right, to_left, across_right, across_left, (ctx, y * 2 + other)))
    sends = Sends(send_sem, recv_sem)
    keeps = []

    def cut(h, target):
        return w_down.at[pl.ds(h * half, half), pl.ds(target * width, width)]

    def rows_of(source, h):
        return down_cols.at[pl.ds(source * deep + h * half, half), :]

    def keep_own(place_own):
        load.wait()
        keep = pltpu.make_async_copy(held, place_own, local_sem.at[1])
        keep.start()
        keeps.append(keep)
        sends.start(20, cut(0, far * 2 + z_lo), passing.at[0], to_right)
        sends.start(21, cut(0, far * 2 + other), passing.at[1], to_right)
        sends.start(22, cut(1, far * 2 + z_lo), passing.at[2], to_left)
        sends.start(23, cut(1, far * 2 + other), passing.at[3], to_left)

    def cross():
        sends.start(28, cut(1, y * 2 + other), rows_of(me, 1), (ctx, y * 2 + other))

    def near():
        sends.arrived(20, passing.at[0])
        sends.start(24, passing.at[0], rows_of(left * 2 + z_lo, 0), to_right)
        sends.arrived(22, passing.at[2])
        sends.start(26, passing.at[2], rows_of(right * 2 + z_lo, 1), to_left)

    def across():
        sends.arrived(21, passing.at[1])
        sends.start(25, passing.at[1], rows_of(left * 2 + z_lo, 0), across_right)
        sends.arrived(23, passing.at[3])
        sends.start(27, passing.at[3], rows_of(right * 2 + z_lo, 1), across_left)

    ctx_gather_steps(rows, a, out, transit, sends, keep_own, (cross, near, across))
    sends.arrived(28, rows_of(y * 2 + other, 1))
    sends.arrived(24, rows_of(far * 2 + z_lo, 0))
    sends.arrived(26, rows_of(far * 2 + z_lo, 1))
    sends.arrived(25, rows_of(far * 2 + other, 0))
    sends.arrived(27, rows_of(far * 2 + other, 1))
    sends.drain()
    for keep in keeps:
        keep.wait()


def gather_kv(a, w_down, down_cols, call_id):
    rows, cols = a.shape
    deep, width = w_down.shape[0], w_down.shape[1] // 8
    kv, _, _, down_cols = pl.pallas_call(
        functools.partial(gather_kv_kernel, rows),
        out_shape=(
            jax.ShapeDtypeStruct((rows * 16, cols), a.dtype),
            jax.ShapeDtypeStruct((2, rows // 2, cols), a.dtype),
            jax.ShapeDtypeStruct((4, deep // 2, width), a.dtype),
            jax.ShapeDtypeStruct((deep * 8, width), a.dtype),
        ),
        in_specs=[ANY] * 3,
        out_specs=(ANY,) * 4,
        input_output_aliases={2: 3},
        scratch_shapes=[
            pltpu.VMEM((rows, cols), a.dtype),
            pltpu.SemaphoreType.DMA((2,)),
            pltpu.SemaphoreType.DMA((29,)),
            pltpu.SemaphoreType.DMA((29,)),
        ],
        compiler_params=pltpu.CompilerParams(collective_id=call_id, has_side_effects=True),
        name="gather_kv",
    )(a, w_down, down_cols)
    return kv, down_cols


def hx_spread_kernel(rows, cols, pick, a, out, held, local_sem, send_sem, recv_sem):
    ctx, me = lax.axis_index("ctx"), lax.axis_index("hx")

    def block(p):
        return a.at[:, pl.ds(p * cols, cols)] if pick else a

    load = pltpu.make_async_copy(block(me), held, local_sem.at[0])
    load.start()
    greet([(ctx, (me + k) % 8) for k in range(1, 8)])
    sends = Sends(send_sem, recv_sem)
    for k in range(1, 8):
        peer = (me + k) % 8
        sends.start(k, block(peer), out.at[pl.ds(me * rows, rows), :], (ctx, peer))
    load.wait()
    keep = pltpu.make_async_copy(held, out.at[pl.ds(me * rows, rows), :], local_sem.at[1])
    keep.start()
    for k in range(1, 8):
        sends.arrived(k, out.at[pl.ds((me + 8 - k) % 8 * rows, rows), :])
    sends.drain()
    keep.wait()


def hx_spread(a, cols, pick, call_id, name):
    rows = a.shape[0]
    return pl.pallas_call(
        functools.partial(hx_spread_kernel, rows, cols, pick),
        out_shape=jax.ShapeDtypeStruct((rows * 8, cols), a.dtype),
        in_specs=[pl.BlockSpec(memory_space=pl.ANY)],
        out_specs=pl.BlockSpec(memory_space=pl.ANY),
        scratch_shapes=[
            pltpu.VMEM((rows, cols), a.dtype),
            pltpu.SemaphoreType.DMA((2,)),
            pltpu.SemaphoreType.DMA((8,)),
            pltpu.SemaphoreType.DMA((8,)),
        ],
        compiler_params=pltpu.CompilerParams(collective_id=call_id, has_side_effects=True),
        name=name,
    )(a)


def ctx_exchange_kernel(rows, a, out, held, local_sem, send_sem, recv_sem):
    me, hx = lax.axis_index("ctx"), lax.axis_index("hx")

    def block(ref, p):
        return ref.at[pl.ds(p * rows, rows), :]

    load = pltpu.make_async_copy(block(a, me), held, local_sem.at[0])
    load.start()
    greet([((me + k) % 16, hx) for k in range(1, 16)])
    sends = Sends(send_sem, recv_sem)
    for k in range(1, 16):
        peer = (me + k) % 16
        sends.start(k, block(a, peer), block(out, me), (peer, hx))
    load.wait()
    keep = pltpu.make_async_copy(held, block(out, me), local_sem.at[1])
    keep.start()
    for k in range(1, 16):
        sends.arrived(k, block(out, (me + 16 - k) % 16))
    sends.drain()
    keep.wait()


def ctx_exchange(a, call_id, name):
    rows, cols = a.shape[0] // 16, a.shape[1]
    return pl.pallas_call(
        functools.partial(ctx_exchange_kernel, rows),
        out_shape=jax.ShapeDtypeStruct(a.shape, a.dtype),
        in_specs=[pl.BlockSpec(memory_space=pl.ANY)],
        out_specs=pl.BlockSpec(memory_space=pl.ANY),
        scratch_shapes=[
            pltpu.VMEM((rows, cols), a.dtype),
            pltpu.SemaphoreType.DMA((2,)),
            pltpu.SemaphoreType.DMA((16,)),
            pltpu.SemaphoreType.DMA((16,)),
        ],
        compiler_params=pltpu.CompilerParams(collective_id=call_id, has_side_effects=True),
        name=name,
    )(a)


class Gather:
    def __init__(self, buf, row, rows, split, cols, sends, base):
        z_hi, x, core, y, z_lo = place()
        ctx = ctx_of(z_hi, x, core)
        self.buf, self.cols, self.sends, self.base = buf, cols, sends, base
        self.y, self.z, self.other = y, z_lo, 1 - z_lo
        self.right, self.left, self.far = (y + 1) % 4, (y + 3) % 4, (y + 2) % 4
        self.to_right, self.to_left = (ctx, self.right * 2 + z_lo), (ctx, self.left * 2 + z_lo)
        self.to_z = (ctx, y * 2 + self.other)
        half, rest = split // 2, rows - split
        self.first, self.first_0, self.first_1 = (row, split), (row, half), (row + half, half)
        self.rest, self.rest_0 = (row + split, rest), (row + split, rest // 2)
        self.rest_1 = (row + split + rest // 2, rest // 2)

    def at(self, y_of, z_of, part):
        return self.buf.at[pl.ds(part[0], part[1]), pl.ds((y_of * 2 + z_of) * self.cols, self.cols)]

    def go(self, k, y_of, z_of, part, device):
        ref = self.at(y_of, z_of, part)
        self.sends.start(self.base + k, ref, ref, device)

    def got(self, k, y_of, z_of, part):
        self.sends.arrived(self.base + k, self.at(y_of, z_of, part))

    def own(self):
        y, z = self.y, self.z
        self.go(0, y, z, self.first, self.to_z)
        self.go(1, y, z, self.first, self.to_right)
        self.go(2, y, z, self.first, self.to_left)
        self.go(3, y, z, self.rest, self.to_right)
        self.go(4, y, z, self.rest, self.to_left)
        self.go(5, y, z, self.rest, self.to_z)

    def step_a(self):
        self.got(0, self.y, self.other, self.first)
        self.go(6, self.y, self.other, self.first, self.to_right)
        self.go(7, self.y, self.other, self.first, self.to_left)

    def step_b(self):
        self.got(3, self.left, self.z, self.rest)
        self.go(10, self.left, self.z, self.rest_0, self.to_right)
        self.go(11, self.left, self.z, self.rest, self.to_z)
        self.got(4, self.right, self.z, self.rest)
        self.go(12, self.right, self.z, self.rest_1, self.to_left)
        self.go(13, self.right, self.z, self.rest, self.to_z)

    def step_c(self):
        self.got(1, self.left, self.z, self.first)
        self.go(8, self.left, self.z, self.first_0, self.to_right)
        self.got(2, self.right, self.z, self.first)
        self.go(9, self.right, self.z, self.first_1, self.to_left)

    def step_d(self):
        self.got(10, self.far, self.z, self.rest_0)
        self.go(16, self.far, self.z, self.rest_0, self.to_z)
        self.got(12, self.far, self.z, self.rest_1)
        self.go(17, self.far, self.z, self.rest_1, self.to_z)

    def step_e(self):
        self.got(6, self.left, self.other, self.first)
        self.go(14, self.left, self.other, self.first_0, self.to_right)
        self.got(7, self.right, self.other, self.first)
        self.go(15, self.right, self.other, self.first_1, self.to_left)

    def finish(self):
        self.got(5, self.y, self.other, self.rest)
        self.got(8, self.far, self.z, self.first_0)
        self.got(9, self.far, self.z, self.first_1)
        self.got(11, self.left, self.other, self.rest)
        self.got(13, self.right, self.other, self.rest)
        self.got(14, self.far, self.other, self.first_0)
        self.got(15, self.far, self.other, self.first_1)
        self.got(16, self.far, self.other, self.rest_0)
        self.got(17, self.far, self.other, self.rest_1)


PARTS = 2


def experts_kernel(
    buffer, w_gate, w_up, down_cols, out, rows, hidden, done, gate_v, up_v, down_v, local_sem, send_sem, recv_sem
):
    z_hi, x, core, y, z_lo = place()
    me, hx = ctx_of(z_hi, x, core), y * 2 + z_lo
    width, deep = buffer.shape[1], w_gate.shape[1]
    total = buffer.shape[0]
    chunk = total // PARTS
    slot = chunk // 16
    loads = (
        pltpu.make_async_copy(w_gate, gate_v, local_sem.at[0]),
        pltpu.make_async_copy(w_up, up_v, local_sem.at[1]),
        pltpu.make_async_copy(down_cols, down_v, local_sem.at[2]),
    )
    mine = pl.ds(hx * width, width)
    keeps = [
        pltpu.make_async_copy(
            buffer.at[pl.ds(c * chunk + me * slot, slot), :],
            rows.at[pl.ds(c * chunk + me * slot, slot), mine],
            local_sem.at[3 + c],
        )
        for c in range(PARTS)
    ]
    for copy in keeps:
        copy.start()
    near = ((y + 1) % 4 * 2 + z_lo, (y + 3) % 4 * 2 + z_lo, y * 2 + 1 - z_lo)
    greet([((me + k) % 16, hx) for k in range(1, 16)] + [(me, p) for p in near])
    sends = Sends(send_sem, recv_sem)

    def spot(c, p):
        return pl.ds(c * chunk + p * slot, slot)

    def dispatch(c):
        for k in range(1, 16):
            peer = (me + k) % 16
            sends.start(c * 15 + k - 1, buffer.at[spot(c, peer), :], rows.at[spot(c, me), mine], (peer, hx))

    def dispatched(c):
        keeps[c].wait()
        for k in range(1, 16):
            sends.arrived(c * 15 + k - 1, rows.at[spot(c, (me + 16 - k) % 16), mine])

    def give(c):
        base = PARTS * 15
        for k in range(1, 16):
            peer = (me + k) % 16
            sends.start(base + c * 15 + k - 1, done.at[spot(c, peer), :], out.at[spot(c, me), :], (peer, hx))
        keep = pltpu.make_async_copy(done.at[spot(c, me), :], out.at[spot(c, me), :], local_sem.at[3 + PARTS + c])
        keep.start()
        keeps.append(keep)

    def given(c):
        base = PARTS * 15
        for k in range(1, 16):
            sends.arrived(base + c * 15 + k - 1, out.at[spot(c, (me + 16 - k) % 16), :])

    def hide(c, n):
        step = 256
        r, f = pl.ds(c * chunk, chunk), pl.ds(n * step, step)
        gate = jnp.dot(rows[r, :], gate_v[:, f], preferred_element_type=jnp.float32)
        up = jnp.dot(rows[r, :], up_v[:, f], preferred_element_type=jnp.float32)
        spread = pl.ds(pl.multiple_of(hx * deep + n * step, step), step)
        hidden[r, spread] = (gate * jax.nn.sigmoid(gate) * up).astype(hidden.dtype)

    def lower(c):
        r = pl.ds(c * chunk, chunk)
        for at, step in ((0, 256), (256, 256), (512, 128)):
            f = pl.ds(at, step)
            done[r, f] = jnp.dot(hidden[r, :], down_v[:, f], preferred_element_type=jnp.float32).astype(done.dtype)

    base = PARTS * 30
    split = chunk * 9 // 16 // 32 * 32
    row_gathers = [Gather(rows, c * chunk, chunk, split, width, sends, base + 18 * c) for c in range(PARTS)]
    base += 18 * PARTS
    hid_gathers = [Gather(hidden, c * chunk, chunk, split, deep, sends, base + 18 * c) for c in range(PARTS)]
    r0, r1 = row_gathers
    h0, h1 = hid_gathers

    for c in range(PARTS):
        dispatch(c)
    for load in loads:
        load.start()
    dispatched(0)
    r0.own()
    r0.step_a()
    r0.step_b()
    dispatched(1)
    r1.own()
    r0.step_c()
    r0.step_d()
    r0.step_e()
    r1.step_a()
    r1.step_b()
    r0.finish()
    for load in loads:
        load.wait()
    hide(0, 0)
    r1.step_c()
    r1.step_d()
    hide(0, 1)
    r1.step_e()
    h0.own()
    r1.finish()
    hide(1, 0)
    h0.step_a()
    h0.step_b()
    hide(1, 1)
    h0.step_c()
    h1.own()
    h0.step_d()
    h0.step_e()
    h1.step_a()
    h1.step_b()
    h0.finish()
    lower(0)
    h1.step_c()
    h1.step_d()
    give(0)
    h1.step_e()
    h1.finish()
    lower(1)
    given(0)
    give(1)
    given(1)
    sends.drain()
    for keep in keeps[PARTS:]:
        keep.wait()


def run_experts(buffer, w_gate, w_up, down_cols, call_id):
    total, width = buffer.shape
    full, deep = w_gate.shape
    copies = PARTS * 66
    return pl.pallas_call(
        experts_kernel,
        out_shape=jax.ShapeDtypeStruct((total, width), buffer.dtype),
        in_specs=[ANY] * 4,
        out_specs=ANY,
        scratch_shapes=[
            pltpu.VMEM((total, full), buffer.dtype),
            pltpu.VMEM((total, deep * 8), buffer.dtype),
            pltpu.VMEM((total, width), buffer.dtype),
            pltpu.VMEM((full, deep), buffer.dtype),
            pltpu.VMEM((full, deep), buffer.dtype),
            pltpu.VMEM((deep * 8, width), buffer.dtype),
            pltpu.SemaphoreType.DMA((3 + 2 * PARTS,)),
            pltpu.SemaphoreType.DMA((copies,)),
            pltpu.SemaphoreType.DMA((copies,)),
        ],
        compiler_params=pltpu.CompilerParams(
            collective_id=call_id, has_side_effects=True, vmem_limit_bytes=60 << 20
        ),
        name="experts",
    )(buffer, w_gate, w_up, down_cols)


def attend_kernel(q_t, kv, w_down, _, out, down_cols, send_sem, recv_sem):
    me, hx = lax.axis_index("ctx"), lax.axis_index("hx")
    y, z_lo = hx // 2, hx % 2
    deep, width = w_down.shape[0], down_cols.shape[1]
    order = ((1, 0), (3, 1), (1, 1), (3, 0))

    def peer_of(y_step, flip):
        return (y + y_step) % 4 * 2 + (1 - z_lo if flip else z_lo)

    greet([(me, peer_of(*step)) for step in order])
    sends = Sends(send_sem, recv_sem)
    for i, step in enumerate(order):
        peer = peer_of(*step)
        src = w_down.at[:, pl.ds(peer * width, width)]
        sends.start(i, src, down_cols.at[pl.ds(hx * deep, deep), :], (me, peer))
    tok = q_t.shape[1]
    heads = q_t.shape[0] // HD
    scale = HD ** (-0.5) * math.log2(math.e)

    def visit(block, held, diagonal):
        at = pl.multiple_of(block * tok, tok)
        keys = kv[pl.ds(at, tok), :HD]
        values = kv[pl.ds(at, tok), HD:]
        new = []
        for h in range(heads):
            top, total, acc = held[h]
            scores = jnp.dot(keys, q_t[h * HD : (h + 1) * HD, :], preferred_element_type=jnp.float32) * scale
            if diagonal:
                key_pos = lax.broadcasted_iota(jnp.int32, scores.shape, 0)
                query_pos = lax.broadcasted_iota(jnp.int32, scores.shape, 1)
                scores = jnp.where(key_pos <= query_pos, scores, -1e30)
            new_top = jnp.maximum(top, jnp.max(scores, axis=0, keepdims=True))
            weights = jnp.exp2(scores - new_top)
            factor = jnp.exp2(top - new_top)
            total = total * factor + jnp.sum(weights, axis=0, keepdims=True)
            mixed = lax.dot_general(
                values,
                weights.astype(jnp.bfloat16),
                (((0,), (0,)), ((), ())),
                preferred_element_type=jnp.float32,
            )
            new.append((new_top, total, acc * factor + mixed))
        return tuple(new)

    start = tuple(
        (
            jnp.full((1, tok), -1e30, jnp.float32),
            jnp.zeros((1, tok), jnp.float32),
            jnp.zeros((HD, tok), jnp.float32),
        )
        for _ in range(heads)
    )
    held = visit(me, start, True)
    held = lax.fori_loop(0, me, lambda b, held: visit(b, held, False), held)
    for h in range(heads):
        top, total, acc = held[h]
        out[:, h * HD : (h + 1) * HD] = (acc / total).T.astype(out.dtype)
    for i, (y_step, flip) in enumerate(order):
        source = peer_of(4 - y_step, flip)
        sends.arrived(i, down_cols.at[pl.ds(source * deep, deep), :])
    sends.drain()


def attend(q_t, kv, w_down, down_cols, call_id):
    cols, tok = q_t.shape
    return pl.pallas_call(
        attend_kernel,
        out_shape=(
            jax.ShapeDtypeStruct((tok, cols), jnp.bfloat16),
            jax.ShapeDtypeStruct(down_cols.shape, jnp.bfloat16),
        ),
        in_specs=[pl.BlockSpec(memory_space=pltpu.VMEM)] * 2 + [ANY] * 2,
        out_specs=(pl.BlockSpec(memory_space=pltpu.VMEM), ANY),
        input_output_aliases={3: 1},
        scratch_shapes=[pltpu.SemaphoreType.DMA((4,)), pltpu.SemaphoreType.DMA((4,))],
        compiler_params=pltpu.CompilerParams(
            vmem_limit_bytes=48 << 20, collective_id=call_id, has_side_effects=True
        ),
        cost_estimate=pl.CostEstimate(
            flops=cols * kv.shape[0] * tok * 4,
            bytes_accessed=kv.size * 2,
            transcendentals=cols // HD * tok * kv.shape[0],
        ),
        name="attend",
    )(q_t, kv, w_down, down_cols)


def body(tokens, attn_gain, ffn_gain, w_query, w_key, w_value, w_out, w_router, routes, w_gate, w_up, w_down):
    f32, bf16 = jnp.float32, jnp.bfloat16
    hx = lax.axis_index("hx")
    tok_rows, full_width = tokens.shape
    width = full_width // 8
    q_cols = w_query.shape[1]

    w_down = w_down[0]

    weights, out_cols, down_cols = gather_weights(
        jnp.concatenate((w_query, w_key, w_value), axis=1), w_out, w_down, 2
    )
    floats = tokens.astype(f32)
    inverse = lax.rsqrt(jnp.mean(floats * floats, axis=-1, keepdims=True) + epsilon)
    normed = (floats * inverse * attn_gain.astype(f32)).astype(bf16)
    q_t = jnp.einsum("td,dc->ct", normed, weights[:, :q_cols], preferred_element_type=f32).astype(bf16)
    kv_own = jnp.dot(normed, weights[:, q_cols:], preferred_element_type=f32).astype(bf16)
    kv, down_cols = gather_kv(kv_own, w_down, down_cols, 3)
    attended, down_cols = attend(q_t, kv, w_down, down_cols, 5)
    attended = hx_gather(attended, 4, "gather_attended")

    share = jnp.dot(attended, out_cols, preferred_element_type=f32)
    own_tokens = lax.dynamic_slice_in_dim(tokens, hx * width, width, 1)
    own_gain = lax.dynamic_slice_in_dim(ffn_gain, hx * width, width, 0).astype(f32)
    own_router = lax.dynamic_slice_in_dim(w_router, hx * width, width, 0)
    stream = (own_tokens.astype(f32) + share).astype(bf16)
    stream_f = stream.astype(f32)

    experts = w_router.shape[1]
    chosen = routes[:, 0]
    onehot = chosen[:, None] == jnp.arange(experts, dtype=jnp.int32)[None, :]
    capacity = tok_rows // 8
    counts = jnp.cumsum(onehot.astype(jnp.int32), axis=0)
    position = jnp.sum(jnp.where(onehot, counts, 0), axis=-1) - 1
    slots = capacity // PARTS
    slot = position // slots * (experts * slots) + chosen * slots + position % slots
    picks = (slot[None, :] == jnp.arange(experts * capacity, dtype=jnp.int32)[:, None]).astype(bf16)

    gained = stream_f * own_gain
    part_logits = jnp.dot(gained.astype(bf16), own_router, preferred_element_type=f32)
    part_logit = jnp.sum(jnp.where(onehot, part_logits, 0.0), axis=-1)
    part_square = jnp.sum(stream_f * stream_f, axis=-1)
    parts = jnp.concatenate(
        (part_square[None, :], part_logit[None, :], jnp.zeros((6, tok_rows), f32)), axis=0
    )
    sums = jnp.sum(hx_spread(parts, tok_rows, False, 7, "gather_sums").reshape(8, 8, tok_rows), axis=0)
    inverse2 = lax.rsqrt(sums[0] / full_width + epsilon)[:, None]
    score = jax.nn.sigmoid(sums[1][:, None] * inverse2)
    normed2 = (stream_f * inverse2 * own_gain).astype(bf16)
    routed = (normed2.astype(f32) * score).astype(bf16)
    buffer = jnp.dot(picks, routed, preferred_element_type=f32).astype(bf16)
    returned = run_experts(buffer, w_gate[0], w_up[0], down_cols, 6)
    expert_out = lax.dot_general(picks, returned, (((0,), (0,)), ((), ())), preferred_element_type=f32)
    return (stream_f + expert_out.astype(bf16).astype(f32)).astype(bf16)


def solution(mesh):
    in_specs = (
        P("ctx", None),
        P(),
        P(),
        P("ctx", "hx"),
        P("ctx", "hx"),
        P("ctx", "hx"),
        P("hx", None),
        P(),
        P("ctx", None),
        P("ctx", None, "hx"),
        P("ctx", None, "hx"),
        P("ctx", "hx", None),
    )
    return jax.shard_map(body, mesh=mesh, in_specs=in_specs, out_specs=P("ctx", "hx"), check_vma=False)
```

```python
import functools
import math
import jax
import jax.numpy as jnp
from jax import lax
from jax.experimental import pallas as pl
from jax.experimental.pallas import tpu as pltpu
from jax.sharding import PartitionSpec as P

HD = 128
epsilon = 1e-05
MESH = pl.DeviceIdType.MESH


def place():
    ctx, hx = lax.axis_index("ctx"), lax.axis_index("hx")
    z_hi, x, core = ctx // 8, (ctx // 2) % 4, ctx % 2
    y, z_lo = hx // 2, hx % 2
    return z_hi, x, core, y, z_lo


def ctx_of(z_hi, x, core):
    return z_hi * 8 + x * 2 + core


def greet(devices):
    barrier = pltpu.get_barrier_semaphore()
    for device in devices:
        pl.semaphore_signal(barrier, inc=1, device_id=device, device_id_type=MESH)
    pl.semaphore_wait(barrier, len(devices))


class Sends:
    def __init__(self, send_sem, recv_sem):
        self.send_sem, self.recv_sem, self.started = send_sem, recv_sem, []

    def start(self, k, src, dst, device):
        copy = pltpu.make_async_remote_copy(
            src_ref=src,
            dst_ref=dst,
            send_sem=self.send_sem.at[k],
            recv_sem=self.recv_sem.at[k],
            device_id=device,
            device_id_type=MESH,
        )
        copy.start()
        self.started.append(copy)

    def arrived(self, k, dst):
        pltpu.make_async_copy(dst, dst, self.recv_sem.at[k]).wait()

    def drain(self):
        for copy in self.started:
            copy.wait_send()


def ctx_neighbours():
    z_hi, x, core, y, z_lo = place()
    hx = y * 2 + z_lo
    z = z_hi * 2 + z_lo
    up, down = (z + 1) % 4, (z + 3) % 4
    return (
        (ctx_of(z_hi, (x + 1) % 4, core), hx),
        (ctx_of(z_hi, (x + 3) % 4, core), hx),
        (ctx_of(up // 2, x, core), y * 2 + up % 2),
        (ctx_of(down // 2, x, core), y * 2 + down % 2),
        (ctx_of(z_hi, x, 1 - core), hx),
    )


class Spread:
    def __init__(self, own, out, transit, rows, sends, base):
        z_hi, x, core, y, z_lo = place()
        hx = y * 2 + z_lo
        z = z_hi * 2 + z_lo
        up, down = (z + 1) % 4, (z + 3) % 4
        self.own_ref, self.out, self.transit, self.rows, self.sends, self.base = own, out, transit, rows, sends, base
        self.z, self.x, self.core, self.other = z_hi, x, core, 1 - z_hi
        self.right, self.left, self.far = (x + 1) % 4, (x + 3) % 4, (x + 2) % 4
        self.z_up, self.z_down = up // 2, down // 2
        self.to_right, self.to_left = (ctx_of(z_hi, self.right, core), hx), (ctx_of(z_hi, self.left, core), hx)
        self.to_up = (ctx_of(up // 2, x, core), y * 2 + up % 2)
        self.to_down = (ctx_of(down // 2, x, core), y * 2 + down % 2)
        self.to_core = (ctx_of(z_hi, x, 1 - core), hx)
        self.whole, self.half_0, self.half_1 = (0, rows), (0, rows // 2), (rows // 2, rows // 2)

    def at(self, z_of, x_of, core_of, part):
        return self.out.at[pl.ds(ctx_of(z_of, x_of, core_of) * self.rows + part[0], part[1]), :]

    def go(self, k, z_of, x_of, part, device):
        ref = self.at(z_of, x_of, self.core, part)
        self.sends.start(self.base + k, ref, ref, device)

    def got(self, k, z_of, x_of, part):
        self.sends.arrived(self.base + k, self.at(z_of, x_of, self.core, part))

    def from_core(self, k, z_of, x_of):
        self.sends.arrived(self.base + k, self.at(z_of, x_of, 1 - self.core, self.whole))

    def start(self):
        def own(part):
            return self.own_ref.at[pl.ds(part[0], part[1]), :]

        here = self.at(self.z, self.x, self.core, self.whole)
        self.sends.start(self.base + 0, own(self.half_0), self.transit.at[0], self.to_up)
        self.sends.start(self.base + 1, own(self.half_1), self.transit.at[1], self.to_down)
        self.sends.start(self.base + 2, own(self.whole), here, self.to_right)
        self.sends.start(self.base + 3, own(self.whole), here, self.to_left)
        self.sends.start(self.base + 4, own(self.whole), here, self.to_core)

    def pass_z(self):
        self.sends.arrived(self.base + 0, self.transit.at[0])
        self.sends.start(
            self.base + 5, self.transit.at[0], self.at(self.z_down, self.x, self.core, self.half_0), self.to_up
        )
        self.sends.arrived(self.base + 1, self.transit.at[1])
        self.sends.start(
            self.base + 6, self.transit.at[1], self.at(self.z_up, self.x, self.core, self.half_1), self.to_down
        )

    def pass_near(self):
        self.got(2, self.z, self.left, self.whole)
        self.go(10, self.z, self.left, self.half_0, self.to_right)
        self.go(11, self.z, self.left, self.whole, self.to_core)
        self.got(3, self.z, self.right, self.whole)
        self.go(12, self.z, self.right, self.half_1, self.to_left)
        self.go(13, self.z, self.right, self.whole, self.to_core)

    def pass_other(self):
        self.got(5, self.other, self.x, self.half_0)
        self.got(6, self.other, self.x, self.half_1)
        self.go(7, self.other, self.x, self.whole, self.to_right)
        self.go(8, self.other, self.x, self.whole, self.to_left)
        self.go(9, self.other, self.x, self.whole, self.to_core)

    def pass_far(self):
        self.got(10, self.z, self.far, self.half_0)
        self.got(12, self.z, self.far, self.half_1)
        self.go(18, self.z, self.far, self.whole, self.to_core)

    def pass_other_near(self):
        self.got(7, self.other, self.left, self.whole)
        self.go(14, self.other, self.left, self.half_0, self.to_right)
        self.go(15, self.other, self.left, self.whole, self.to_core)
        self.got(8, self.other, self.right, self.whole)
        self.go(16, self.other, self.right, self.half_1, self.to_left)
        self.go(17, self.other, self.right, self.whole, self.to_core)

    def pass_other_far(self):
        self.got(14, self.other, self.far, self.half_0)
        self.got(16, self.other, self.far, self.half_1)
        self.go(19, self.other, self.far, self.whole, self.to_core)


def front_kernel(
    tokens, gain, a, w_out, w_down, attended, out_cols, down_cols,
    normed, weights, transit_w, kv, transit_kv, passing, held_out, held_down, sums, q_t, top_v, total_v, acc_v,
    local_sem, send_sem, recv_sem,
):
    z_hi, x, core, y, z_lo = place()
    ctx, me = ctx_of(z_hi, x, core), y * 2 + z_lo
    other = 1 - z_hi
    tok, full = tokens.shape
    rows = a.shape[0]
    q_cols = q_t.shape[0]
    heads = q_cols // HD
    width, deep = held_out.shape[1], w_down.shape[0]
    half = deep // 2
    sub, piece = x * 2 + core, out_cols.shape[2]
    mine = pl.ds(me * width, width)
    loads = (
        pltpu.make_async_copy(tokens, normed, local_sem.at[0]),
        pltpu.make_async_copy(a, weights.at[pl.ds(ctx * rows, rows), :], local_sem.at[1]),
        pltpu.make_async_copy(w_out.at[pl.ds(sub * piece, piece), mine], held_out, local_sem.at[2]),
        pltpu.make_async_copy(w_down.at[:, mine], held_down, local_sem.at[3]),
    )
    for load in loads:
        load.start()
    greet(ctx_neighbours() + tuple((ctx, (me + k) % 8) for k in range(1, 8)))
    sends = Sends(send_sem, recv_sem)

    def peer_of(y_step, flip):
        return (y + y_step) % 4 * 2 + (1 - z_lo if flip else z_lo)

    order = ((1, 0), (3, 0), (2, 0), (0, 1), (1, 1), (3, 1), (2, 1))

    def share(i):
        peer = peer_of(*order[i])
        src = w_out.at[pl.ds(sub * piece, piece), pl.ds(peer * width, width)]
        sends.start(40 + i, src, out_cols.at[me, sub], (ctx, peer))

    right, left, far = (x + 1) % 4, (x + 3) % 4, (x + 2) % 4
    to_right, to_left = (ctx_of(z_hi, right, core), me), (ctx_of(z_hi, left, core), me)
    to_core = (ctx_of(z_hi, x, 1 - core), me)
    whole, half_0, half_1 = (0, 8), (0, 4), (4, 4)

    def of_chip(x_of, core_of, part):
        return out_cols.at[pl.ds(part[0], part[1]), x_of * 2 + core_of]

    def pass_out(k, x_of, part, device):
        block = of_chip(x_of, core, part)
        sends.start(k, block, block, device)

    def ring_start():
        for i in range(7):
            y_step, flip = order[i]
            sends.arrived(40 + i, out_cols.at[peer_of(4 - y_step, flip), sub])
        keep_out.wait()
        pass_out(47, x, whole, to_right)
        pass_out(48, x, whole, to_left)
        pass_out(49, x, whole, to_core)

    def ring_near():
        sends.arrived(47, of_chip(left, core, whole))
        pass_out(50, left, half_0, to_right)
        pass_out(51, left, whole, to_core)
        sends.arrived(48, of_chip(right, core, whole))
        pass_out(52, right, half_1, to_left)
        pass_out(53, right, whole, to_core)

    def ring_far():
        sends.arrived(50, of_chip(far, core, half_0))
        sends.arrived(52, of_chip(far, core, half_1))
        pass_out(67, far, whole, to_core)
        for k, x_of in ((49, x), (51, left), (53, right), (67, far)):
            sends.arrived(k, of_chip(x_of, 1 - core, whole))

    def down_rows(source, h, count):
        return down_cols.at[pl.ds(source * deep + h * half, count), :]

    def down_block(k, peer):
        sends.start(k, w_down.at[:, pl.ds(peer * width, width)], down_rows(me, 0, deep), (ctx, peer))

    def first_hop():
        for k, h, flip, step in ((55, 0, 0, 1), (57, 1, 0, 3), (56, 0, 1, 1), (58, 1, 1, 3)):
            src = w_down.at[pl.ds(h * half, half), pl.ds(peer_of(2, flip) * width, width)]
            sends.start(k, src, passing.at[k - 55], (ctx, peer_of(step, 0)))

    def second_hop(flip):
        for k, h, step in ((55 + flip, 0, 1), (57 + flip, 1, 3)):
            sends.arrived(k, passing.at[k - 55])
            source = peer_of(4 - step, 0)
            sends.start(k + 4, passing.at[k - 55], down_rows(source, h, half), (ctx, peer_of(step, flip)))

    spread_w = Spread(a, weights, transit_w, rows, sends, 0)
    spread_w.start()
    for i in range(3):
        share(i)

    loads[0].wait()
    loads[2].wait()
    keep_out = pltpu.make_async_copy(held_out, out_cols.at[me, sub], local_sem.at[4])
    keep_out.start()

    def norm(i, carry):
        r = pl.ds(pl.multiple_of(i * 64, 64), 64)
        floats = normed[r, :].astype(jnp.float32)
        inverse = lax.rsqrt(jnp.mean(floats * floats, axis=-1, keepdims=True) + epsilon)
        normed[r, :] = (floats * inverse * gain[...]).astype(normed.dtype)
        return carry

    lax.fori_loop(0, tok // 64, norm, 0)
    sums[...] = jnp.zeros_like(sums)

    def project(z_of, x_of):
        at = pl.multiple_of(ctx_of(z_of, x_of, 0) * rows, 2 * rows)
        sums[...] += jnp.dot(
            normed[:, pl.ds(at, 2 * rows)], weights[pl.ds(at, 2 * rows), :], preferred_element_type=jnp.float32
        )

    def two(visit):
        return lambda j, carry: (visit(j), carry)[1]

    spread_w.pass_z()
    for i in range(3, 7):
        share(i)
    down_block(54, peer_of(0, 1))
    first_hop()
    down_block(63, peer_of(1, 0))
    down_block(64, peer_of(3, 0))
    spread_w.pass_near()
    loads[1].wait()
    spread_w.from_core(4, z_hi, x)
    project(z_hi, x)
    spread_w.pass_other()
    spread_w.from_core(11, z_hi, spread_w.left)
    spread_w.from_core(13, z_hi, spread_w.right)
    lax.fori_loop(0, 2, two(lambda j: project(z_hi, (x + 1 + 2 * j) % 4)), 0)
    spread_w.pass_far()
    spread_w.from_core(9, other, x)
    project(other, x)
    spread_w.pass_other_near()
    spread_w.from_core(18, z_hi, spread_w.far)
    project(z_hi, spread_w.far)
    spread_w.from_core(15, other, spread_w.left)
    spread_w.from_core(17, other, spread_w.right)
    lax.fori_loop(0, 2, two(lambda j: project(other, (x + 1 + 2 * j) % 4)), 0)
    spread_w.pass_other_far()
    spread_w.from_core(19, other, spread_w.far)
    project(other, spread_w.far)

    own_rows = pl.ds(ctx * tok, tok)
    kv[own_rows, :] = sums[:, q_cols:].astype(kv.dtype)
    for h in range(heads):
        q_t[h * HD : (h + 1) * HD, :] = sums[:, h * HD : (h + 1) * HD].T.astype(q_t.dtype)
    top_v[...] = jnp.full_like(top_v, -1e30)
    total_v[...] = jnp.zeros_like(total_v)
    acc_v[...] = jnp.zeros_like(acc_v)
    scale = HD ** (-0.5) * math.log2(math.e)

    def visit(block, diagonal):
        at = pl.multiple_of(block * tok, tok)
        keys = kv[pl.ds(at, tok), :HD]
        values = kv[pl.ds(at, tok), HD:]
        for h in range(heads):
            r = slice(h * HD, (h + 1) * HD)
            top, total = top_v[h : h + 1, :], total_v[h : h + 1, :]
            scores = jnp.dot(keys, q_t[r, :], preferred_element_type=jnp.float32) * scale
            if diagonal:
                key_pos = lax.broadcasted_iota(jnp.int32, scores.shape, 0)
                query_pos = lax.broadcasted_iota(jnp.int32, scores.shape, 1)
                scores = jnp.where(key_pos <= query_pos, scores, -1e30)
            new_top = jnp.maximum(top, jnp.max(scores, axis=0, keepdims=True))
            weight = jnp.exp2(scores - new_top)
            factor = jnp.exp2(top - new_top)
            top_v[h : h + 1, :] = new_top
            total_v[h : h + 1, :] = total * factor + jnp.sum(weight, axis=0, keepdims=True)
            mixed = lax.dot_general(
                values, weight.astype(jnp.bfloat16), (((0,), (0,)), ((), ())), preferred_element_type=jnp.float32
            )
            acc_v[r, :] = acc_v[r, :] * factor + mixed

    def seen(block):
        @pl.when(block < ctx)
        def _():
            visit(block, False)

    spread_kv = Spread(kv.at[own_rows, :], kv, transit_kv, tok, sends, 20)
    spread_kv.start()
    visit(ctx, True)
    spread_kv.pass_z()
    down_block(65, peer_of(1, 1))
    down_block(66, peer_of(3, 1))
    spread_kv.pass_near()
    second_hop(0)
    spread_kv.pass_other()
    spread_kv.from_core(4, z_hi, x)
    seen(ctx_of(z_hi, x, 1 - core))
    spread_kv.from_core(11, z_hi, spread_kv.left)
    spread_kv.from_core(13, z_hi, spread_kv.right)
    lax.fori_loop(0, 4, two(lambda j: seen(ctx_of(z_hi, (x + 1 + j // 2 * 2) % 4, j % 2))), 0)
    spread_kv.pass_far()
    spread_kv.pass_other_near()
    ring_start()
    second_hop(1)
    spread_kv.from_core(9, other, x)
    spread_kv.from_core(18, z_hi, spread_kv.far)
    lax.fori_loop(0, 4, two(lambda j: seen(ctx_of((z_hi + 1 - j // 2) % 2, (x + j // 2 * 2) % 4, j % 2))), 0)
    spread_kv.pass_other_far()
    ring_near()
    spread_kv.from_core(15, other, spread_kv.left)
    spread_kv.from_core(17, other, spread_kv.right)
    spread_kv.from_core(19, other, spread_kv.far)
    lax.fori_loop(0, 6, two(lambda j: seen(ctx_of(other, (x + 1 + j // 2) % 4, j % 2))), 0)
    for h in range(heads):
        r = slice(h * HD, (h + 1) * HD)
        attended[:, r] = (acc_v[r, :] / total_v[h : h + 1, :]).T.astype(attended.dtype)

    loads[3].wait()
    keep_down = pltpu.make_async_copy(held_down, down_rows(me, 0, deep), local_sem.at[5])
    keep_down.start()
    ring_far()
    sends.arrived(54, down_rows(peer_of(0, 1), 0, deep))
    for flip in (0, 1):
        sends.arrived(59 + flip, down_rows(peer_of(2, flip), 0, half))
        sends.arrived(61 + flip, down_rows(peer_of(2, flip), 1, half))
    for k, y_step, flip in ((63, 1, 0), (64, 3, 0), (65, 1, 1), (66, 3, 1)):
        sends.arrived(k, down_rows(peer_of(4 - y_step, flip), 0, deep))
    sends.drain()
    keep_down.wait()


ANY = pl.BlockSpec(memory_space=pl.ANY)
VMEM = pl.BlockSpec(memory_space=pltpu.VMEM)


def run_front(tokens, gain, a, w_out, w_down, q_cols, call_id):
    bf16, f32 = jnp.bfloat16, jnp.float32
    tok, full = tokens.shape
    rows, cols = a.shape
    depth, deep, width = w_out.shape[0], w_down.shape[0], full // 8
    return pl.pallas_call(
        front_kernel,
        out_shape=(
            jax.ShapeDtypeStruct((tok, q_cols), bf16),
            jax.ShapeDtypeStruct((8, 8, depth // 8, width), bf16),
            jax.ShapeDtypeStruct((deep * 8, width), bf16),
        ),
        in_specs=[ANY, VMEM, ANY, ANY, ANY],
        out_specs=(VMEM, ANY, ANY),
        scratch_shapes=[
            pltpu.VMEM((tok, full), bf16),
            pltpu.VMEM((full, cols), bf16),
            pltpu.VMEM((2, rows // 2, cols), bf16),
            pltpu.VMEM((tok * 16, cols - q_cols), bf16),
            pltpu.VMEM((2, tok // 2, cols - q_cols), bf16),
            pltpu.VMEM((4, deep // 2, width), bf16),
            pltpu.VMEM((depth // 8, width), bf16),
            pltpu.VMEM((deep, width), bf16),
            pltpu.VMEM((tok, cols), f32),
            pltpu.VMEM((q_cols, tok), bf16),
            pltpu.VMEM((8, tok), f32),
            pltpu.VMEM((8, tok), f32),
            pltpu.VMEM((q_cols, tok), f32),
            pltpu.SemaphoreType.DMA((6,)),
            pltpu.SemaphoreType.DMA((68,)),
            pltpu.SemaphoreType.DMA((68,)),
        ],
        compiler_params=pltpu.CompilerParams(
            collective_id=call_id, has_side_effects=True, vmem_limit_bytes=56 << 20
        ),
        name="front",
    )(tokens, gain, a, w_out, w_down)


class Gather:
    def __init__(self, buf, row, rows, split, cols, sends, base, source=None):
        z_hi, x, core, y, z_lo = place()
        ctx = ctx_of(z_hi, x, core)
        self.buf, self.cols, self.sends, self.base, self.source = buf, cols, sends, base, source
        self.y, self.z, self.other = y, z_lo, 1 - z_lo
        self.right, self.left, self.far = (y + 1) % 4, (y + 3) % 4, (y + 2) % 4
        self.to_right, self.to_left = (ctx, self.right * 2 + z_lo), (ctx, self.left * 2 + z_lo)
        self.to_z = (ctx, y * 2 + self.other)
        half, rest = split // 2, rows - split
        self.first, self.first_0, self.first_1 = (row, split), (row, half), (row + half, half)
        self.rest, self.rest_0 = (row + split, rest), (row + split, rest // 2)
        self.rest_1 = (row + split + rest // 2, rest // 2)

    def at(self, y_of, z_of, part):
        return self.buf.at[pl.ds(part[0], part[1]), pl.ds((y_of * 2 + z_of) * self.cols, self.cols)]

    def go(self, k, y_of, z_of, part, device):
        ref = self.at(y_of, z_of, part)
        self.sends.start(self.base + k, ref, ref, device)

    def got(self, k, y_of, z_of, part):
        self.sends.arrived(self.base + k, self.at(y_of, z_of, part))

    def own(self):
        for k, part, device in (
            (0, self.first, self.to_z),
            (1, self.first, self.to_right),
            (2, self.first, self.to_left),
            (3, self.rest, self.to_right),
            (4, self.rest, self.to_left),
            (5, self.rest, self.to_z),
        ):
            here = self.at(self.y, self.z, part)
            src = here if self.source is None else self.source.at[pl.ds(part[0], part[1]), :]
            self.sends.start(self.base + k, src, here, device)

    def step_a(self):
        self.got(0, self.y, self.other, self.first)
        self.go(6, self.y, self.other, self.first, self.to_right)
        self.go(7, self.y, self.other, self.first, self.to_left)

    def step_b(self):
        self.got(3, self.left, self.z, self.rest)
        self.go(10, self.left, self.z, self.rest_0, self.to_right)
        self.go(11, self.left, self.z, self.rest, self.to_z)
        self.got(4, self.right, self.z, self.rest)
        self.go(12, self.right, self.z, self.rest_1, self.to_left)
        self.go(13, self.right, self.z, self.rest, self.to_z)

    def step_c(self):
        self.got(1, self.left, self.z, self.first)
        self.go(8, self.left, self.z, self.first_0, self.to_right)
        self.got(2, self.right, self.z, self.first)
        self.go(9, self.right, self.z, self.first_1, self.to_left)

    def step_d(self):
        self.got(10, self.far, self.z, self.rest_0)
        self.go(16, self.far, self.z, self.rest_0, self.to_z)
        self.got(12, self.far, self.z, self.rest_1)
        self.go(17, self.far, self.z, self.rest_1, self.to_z)

    def step_e(self):
        self.got(6, self.left, self.other, self.first)
        self.go(14, self.left, self.other, self.first_0, self.to_right)
        self.got(7, self.right, self.other, self.first)
        self.go(15, self.right, self.other, self.first_1, self.to_left)

    def finish_near(self, use):
        self.got(5, self.y, self.other, self.rest)
        use(self.y)
        self.got(11, self.left, self.other, self.rest)
        use(self.left)
        self.got(13, self.right, self.other, self.rest)
        use(self.right)

    def finish_far(self):
        self.got(8, self.far, self.z, self.first_0)
        self.got(9, self.far, self.z, self.first_1)
        self.got(14, self.far, self.other, self.first_0)
        self.got(15, self.far, self.other, self.first_1)
        self.got(16, self.far, self.other, self.rest_0)
        self.got(17, self.far, self.other, self.rest_1)

    def finish(self):
        self.finish_near(lambda y_of: None)
        self.finish_far()


PARTS = 2


def experts_kernel(
    attended, out_cols, tokens, gain, router, chosen, slots, w_gate, w_up, down_cols,
    out, share, all_att, out_v, stream, picks, buffer, back, parts, rows, hidden, done, gate_v, up_v, down_v,
    local_sem, send_sem, recv_sem,
):
    f32, bf16 = jnp.float32, jnp.bfloat16
    z_hi, x, core, y, z_lo = place()
    me, hx = ctx_of(z_hi, x, core), y * 2 + z_lo
    tok = tokens.shape[0]
    head_cols = attended.shape[1]
    width, deep = tokens.shape[1], w_gate.shape[1]
    total = buffer.shape[0]
    chunk = total // PARTS
    slot = chunk // 16
    loads = [
        pltpu.make_async_copy(w_gate, gate_v, local_sem.at[0]),
        pltpu.make_async_copy(w_up, up_v, local_sem.at[1]),
    ]
    loads.append(pltpu.make_async_copy(down_cols, down_v, local_sem.at[2]))
    mine = pl.ds(hx * width, width)
    early = (
        pltpu.make_async_copy(attended, all_att.at[:, pl.ds(hx * head_cols, head_cols)], local_sem.at[3]),
        pltpu.make_async_copy(out_cols, out_v, local_sem.at[4]),
    )
    for copy in early:
        copy.start()
    keeps = []
    greet([((me + k) % 16, hx) for k in range(1, 16)] + [(me, (hx + k) % 8) for k in range(1, 8)])
    sends = Sends(send_sem, recv_sem)

    def spot(c, p):
        return pl.ds(c * chunk + p * slot, slot)

    def dispatch(c):
        keep = pltpu.make_async_copy(buffer.at[spot(c, me), :], rows.at[spot(c, me), mine], local_sem.at[5 + c])
        keep.start()
        keeps.append(keep)
        for k in range(1, 16):
            peer = (me + k) % 16
            sends.start(c * 15 + k - 1, buffer.at[spot(c, peer), :], rows.at[spot(c, me), mine], (peer, hx))

    def dispatched(c):
        keeps[c].wait()
        for k in range(1, 16):
            sends.arrived(c * 15 + k - 1, rows.at[spot(c, (me + 16 - k) % 16), mine])

    def give(c):
        base = PARTS * 15
        for k in range(1, 16):
            peer = (me + k) % 16
            sends.start(base + c * 15 + k - 1, done.at[spot(c, peer), :], back.at[spot(c, me), :], (peer, hx))
        keep = pltpu.make_async_copy(done.at[spot(c, me), :], back.at[spot(c, me), :], local_sem.at[5 + PARTS + c])
        keep.start()
        keeps.append(keep)

    def given(c):
        base = PARTS * 15
        keeps[PARTS + c].wait()
        for k in range(1, 16):
            sends.arrived(base + c * 15 + k - 1, back.at[spot(c, (me + 16 - k) % 16), :])

    def hide(c, n):
        step = 256
        r, f = pl.ds(c * chunk, chunk), pl.ds(n * step, step)
        gate = jnp.dot(rows[r, :], gate_v[:, f], preferred_element_type=jnp.float32)
        up = jnp.dot(rows[r, :], up_v[:, f], preferred_element_type=jnp.float32)
        spread = pl.ds(pl.multiple_of(hx * deep + n * step, step), step)
        hidden[r, spread] = (gate * jax.nn.sigmoid(gate) * up).astype(hidden.dtype)

    def lower(c):
        r = pl.ds(c * chunk, chunk)
        for at, step in ((0, 256), (256, 256), (512, 128)):
            f = pl.ds(at, step)
            done[r, f] = jnp.dot(hidden[r, :], down_v[:, f], preferred_element_type=jnp.float32).astype(done.dtype)

    base = PARTS * 30
    split = chunk * 9 // 16 // 32 * 32
    row_gathers = [Gather(rows, c * chunk, chunk, split, width, sends, base + 18 * c) for c in range(PARTS)]
    base += 18 * PARTS
    hid_gathers = [Gather(hidden, c * chunk, chunk, split, deep, sends, base + 18 * c) for c in range(PARTS)]
    r0, r1 = row_gathers
    h0, h1 = hid_gathers

    base += 18 * PARTS
    att = Gather(all_att, 0, tok, tok * 9 // 16 // 32 * 32, head_cols, sends, base, attended)
    base += 18
    att.own()
    for load in loads:
        load.start()
    row_slot = lax.broadcasted_iota(jnp.int32, (total, tok), 0)
    picks[...] = jnp.where(row_slot == slots[...], 1.0, 0.0).astype(bf16)
    att.step_a()
    att.step_b()
    att.step_c()
    att.step_d()
    att.step_e()
    for copy in early:
        copy.wait()
    share[...] = tokens[...].astype(f32)

    def project(y_of):
        at = pl.ds(pl.multiple_of(y_of * 2 * head_cols, 2 * head_cols), 2 * head_cols)
        share[...] += jnp.dot(all_att[:, at], out_v[at, :], preferred_element_type=f32)

    att.finish_near(project)
    att.finish_far()
    project(att.far)
    stream[...] = share[...].astype(bf16)
    floats = stream[...].astype(f32)
    logits = jnp.dot((floats * gain[...]).astype(bf16), router[...], preferred_element_type=f32)
    lane = lax.broadcasted_iota(jnp.int32, logits.shape, 1)
    logit = jnp.sum(jnp.where(lane == chosen[...], logits, 0.0), axis=1, keepdims=True)
    square = jnp.sum(floats * floats, axis=1, keepdims=True)
    parts[hx] = jnp.where(lane == 0, square, jnp.where(lane == 1, logit, 0.0)).T[:8, :]
    for k in range(1, 8):
        sends.start(base + k - 1, parts.at[hx], parts.at[hx], (me, (hx + k) % 8))
    for k in range(1, 8):
        sends.arrived(base + k - 1, parts.at[(hx + 8 - k) % 8])
    both = jnp.sum(parts[...], axis=0)
    inverse = lax.rsqrt(both[0:1, :] / rows.shape[1] + epsilon)
    score = jax.nn.sigmoid(both[1:2, :] * inverse)
    line = lax.broadcasted_iota(jnp.int32, (128, tok), 0)
    column = jnp.where(line == 0, inverse, jnp.where(line == 1, score, 0.0)).T
    normed = (stream[...].astype(f32) * column[:, 0:1] * gain[...]).astype(bf16)
    routed = (normed.astype(f32) * column[:, 1:2]).astype(bf16)
    for c in range(PARTS):
        r = pl.ds(c * chunk, chunk)
        buffer[r, :] = jnp.dot(picks[r, :], routed, preferred_element_type=f32).astype(bf16)
        dispatch(c)
    dispatched(0)
    r0.own()
    r0.step_a()
    r0.step_b()
    dispatched(1)
    r1.own()
    r0.step_c()
    r0.step_d()
    r0.step_e()
    r1.step_a()
    r1.step_b()
    r0.finish()
    for load in loads:
        load.wait()
    hide(0, 0)
    r1.step_c()
    r1.step_d()
    hide(0, 1)
    r1.step_e()
    h0.own()
    r1.finish()
    hide(1, 0)
    h0.step_a()
    h0.step_b()
    hide(1, 1)
    h0.step_c()
    h1.own()
    h0.step_d()
    h0.step_e()
    h1.step_a()
    h1.step_b()
    h0.finish()
    lower(0)
    h1.step_c()
    h1.step_d()
    give(0)
    h1.step_e()
    h1.finish()
    lower(1)

    def placed(c):
        r = pl.ds(c * chunk, chunk)
        return lax.dot_general(picks[r, :], back[r, :], (((0,), (0,)), ((), ())), preferred_element_type=f32)

    given(0)
    give(1)
    found = placed(0)
    given(1)
    found = (found + placed(1)).astype(bf16).astype(f32)
    out[...] = (stream[...].astype(f32) + found).astype(out.dtype)
    sends.drain()


def run_experts(attended, out_cols, tokens, gain, router, chosen, slots, total, w_gate, w_up, down_cols, call_id):
    tok, width = tokens.shape
    full, deep = w_gate.shape
    bf16 = jnp.bfloat16
    copies = PARTS * 66 + 25
    return pl.pallas_call(
        experts_kernel,
        out_shape=jax.ShapeDtypeStruct((tok, width), bf16),
        in_specs=[ANY, ANY, VMEM, VMEM, VMEM, VMEM, VMEM, ANY, ANY, ANY],
        out_specs=VMEM,
        scratch_shapes=[
            pltpu.VMEM((tok, width), jnp.float32),
            pltpu.VMEM((tok, attended.shape[1] * 8), bf16),
            pltpu.VMEM(out_cols.shape, bf16),
            pltpu.VMEM((tok, width), bf16),
            pltpu.VMEM((total, tok), bf16),
            pltpu.VMEM((total, width), bf16),
            pltpu.VMEM((total, width), bf16),
            pltpu.VMEM((8, 8, tok), jnp.float32),
            pltpu.VMEM((total, full), bf16),
            pltpu.VMEM((total, deep * 8), bf16),
            pltpu.VMEM((total, width), bf16),
            pltpu.VMEM((full, deep), bf16),
            pltpu.VMEM((full, deep), bf16),
            pltpu.VMEM((deep * 8, width), bf16),
            pltpu.SemaphoreType.DMA((5 + 2 * PARTS,)),
            pltpu.SemaphoreType.DMA((copies,)),
            pltpu.SemaphoreType.DMA((copies,)),
        ],
        compiler_params=pltpu.CompilerParams(
            collective_id=call_id, has_side_effects=True, vmem_limit_bytes=63 << 20
        ),
        name="experts",
    )(attended, out_cols, tokens, gain, router, chosen, slots, w_gate, w_up, down_cols)


def body(tokens, attn_gain, ffn_gain, w_query, w_key, w_value, w_out, w_router, routes, w_gate, w_up, w_down):
    f32, bf16 = jnp.float32, jnp.bfloat16
    hx = lax.axis_index("hx")
    tok_rows, full_width = tokens.shape
    width = full_width // 8

    w_down = w_down[0]

    qkv = jnp.concatenate((w_query, w_key, w_value), axis=1)
    attended, out_cols, down_cols = run_front(
        tokens, attn_gain.astype(f32)[None, :], qkv, w_out, w_down, w_query.shape[1], 2
    )
    own_tokens = lax.dynamic_slice_in_dim(tokens, hx * width, width, 1)
    own_gain = lax.dynamic_slice_in_dim(ffn_gain, hx * width, width, 0).astype(f32)[None, :]
    own_router = lax.dynamic_slice_in_dim(w_router, hx * width, width, 0)
    experts = w_router.shape[1]
    own_router = jnp.pad(own_router, ((0, 0), (0, 128 - experts)))
    capacity = tok_rows // 8
    chosen = routes[:, 0]
    onehot = chosen[:, None] == jnp.arange(experts, dtype=jnp.int32)[None, :]
    counts = jnp.cumsum(onehot.astype(jnp.int32), axis=0)
    position = jnp.sum(jnp.where(onehot, counts, 0), axis=-1) - 1
    slots = capacity // PARTS
    slot = position // slots * (experts * slots) + chosen * slots + position % slots
    return run_experts(
        attended, out_cols.reshape(-1, width), own_tokens, own_gain, own_router, routes, slot[None, :], experts * capacity,
        w_gate[0], w_up[0], down_cols, 6,
    )


def solution(mesh):
    in_specs = (
        P("ctx", None),
        P(),
        P(),
        P("ctx", "hx"),
        P("ctx", "hx"),
        P("ctx", "hx"),
        P("hx", None),
        P(),
        P("ctx", None),
        P("ctx", None, "hx"),
        P("ctx", None, "hx"),
        P("ctx", "hx", None),
    )
    return jax.shard_map(body, mesh=mesh, in_specs=in_specs, out_specs=P("ctx", "hx"), check_vma=False)
```

```python
import functools
import math
import jax
import jax.numpy as jnp
from jax import lax
from jax.experimental import pallas as pl
from jax.experimental.pallas import tpu as pltpu
from jax.sharding import PartitionSpec as P

HD = 128
epsilon = 1e-05
MESH = pl.DeviceIdType.MESH


def place():
    ctx, hx = lax.axis_index("ctx"), lax.axis_index("hx")
    z_hi, x, core = ctx // 8, (ctx // 2) % 4, ctx % 2
    y, z_lo = hx // 2, hx % 2
    return z_hi, x, core, y, z_lo


def ctx_of(z_hi, x, core):
    return z_hi * 8 + x * 2 + core


def greet(devices):
    barrier = pltpu.get_barrier_semaphore()
    for device in devices:
        pl.semaphore_signal(barrier, inc=1, device_id=device, device_id_type=MESH)
    pl.semaphore_wait(barrier, len(devices))


class Sends:
    def __init__(self, send_sem, recv_sem):
        self.send_sem, self.recv_sem, self.started = send_sem, recv_sem, []

    def start(self, k, src, dst, device):
        copy = pltpu.make_async_remote_copy(
            src_ref=src,
            dst_ref=dst,
            send_sem=self.send_sem.at[k],
            recv_sem=self.recv_sem.at[k],
            device_id=device,
            device_id_type=MESH,
        )
        copy.start()
        self.started.append(copy)

    def arrived(self, k, dst):
        pltpu.make_async_copy(dst, dst, self.recv_sem.at[k]).wait()

    def drain(self):
        for copy in self.started:
            copy.wait_send()


def ctx_neighbours():
    z_hi, x, core, y, z_lo = place()
    hx = y * 2 + z_lo
    z = z_hi * 2 + z_lo
    up, down = (z + 1) % 4, (z + 3) % 4
    return (
        (ctx_of(z_hi, (x + 1) % 4, core), hx),
        (ctx_of(z_hi, (x + 3) % 4, core), hx),
        (ctx_of(up // 2, x, core), y * 2 + up % 2),
        (ctx_of(down // 2, x, core), y * 2 + down % 2),
        (ctx_of(z_hi, x, 1 - core), hx),
    )


class Spread:
    def __init__(self, own, out, transit, rows, sends, base):
        z_hi, x, core, y, z_lo = place()
        hx = y * 2 + z_lo
        z = z_hi * 2 + z_lo
        up, down = (z + 1) % 4, (z + 3) % 4
        self.own_ref, self.out, self.transit, self.rows, self.sends, self.base = own, out, transit, rows, sends, base
        self.z, self.x, self.core, self.other = z_hi, x, core, 1 - z_hi
        self.right, self.left, self.far = (x + 1) % 4, (x + 3) % 4, (x + 2) % 4
        self.z_up, self.z_down = up // 2, down // 2
        self.to_right, self.to_left = (ctx_of(z_hi, self.right, core), hx), (ctx_of(z_hi, self.left, core), hx)
        self.to_up = (ctx_of(up // 2, x, core), y * 2 + up % 2)
        self.to_down = (ctx_of(down // 2, x, core), y * 2 + down % 2)
        self.to_core = (ctx_of(z_hi, x, 1 - core), hx)
        self.whole, self.half_0, self.half_1 = (0, rows), (0, rows // 2), (rows // 2, rows // 2)

    def at(self, z_of, x_of, core_of, part):
        return self.out.at[pl.ds(ctx_of(z_of, x_of, core_of) * self.rows + part[0], part[1]), :]

    def go(self, k, z_of, x_of, part, device):
        ref = self.at(z_of, x_of, self.core, part)
        self.sends.start(self.base + k, ref, ref, device)

    def got(self, k, z_of, x_of, part):
        self.sends.arrived(self.base + k, self.at(z_of, x_of, self.core, part))

    def from_core(self, k, z_of, x_of):
        self.sends.arrived(self.base + k, self.at(z_of, x_of, 1 - self.core, self.whole))

    def start(self):
        def own(part):
            return self.own_ref.at[pl.ds(part[0], part[1]), :]

        here = self.at(self.z, self.x, self.core, self.whole)
        self.sends.start(self.base + 0, own(self.half_0), self.transit.at[0], self.to_up)
        self.sends.start(self.base + 1, own(self.half_1), self.transit.at[1], self.to_down)
        self.sends.start(self.base + 2, own(self.whole), here, self.to_right)
        self.sends.start(self.base + 3, own(self.whole), here, self.to_left)
        self.sends.start(self.base + 4, own(self.whole), here, self.to_core)

    def pass_z(self):
        self.sends.arrived(self.base + 0, self.transit.at[0])
        self.sends.start(
            self.base + 5, self.transit.at[0], self.at(self.z_down, self.x, self.core, self.half_0), self.to_up
        )
        self.sends.arrived(self.base + 1, self.transit.at[1])
        self.sends.start(
            self.base + 6, self.transit.at[1], self.at(self.z_up, self.x, self.core, self.half_1), self.to_down
        )

    def pass_near(self):
        self.got(2, self.z, self.left, self.whole)
        self.go(10, self.z, self.left, self.half_0, self.to_right)
        self.go(11, self.z, self.left, self.whole, self.to_core)
        self.got(3, self.z, self.right, self.whole)
        self.go(12, self.z, self.right, self.half_1, self.to_left)
        self.go(13, self.z, self.right, self.whole, self.to_core)

    def pass_other(self):
        self.got(5, self.other, self.x, self.half_0)
        self.got(6, self.other, self.x, self.half_1)
        self.go(7, self.other, self.x, self.whole, self.to_right)
        self.go(8, self.other, self.x, self.whole, self.to_left)
        self.go(9, self.other, self.x, self.whole, self.to_core)

    def pass_far(self):
        self.got(10, self.z, self.far, self.half_0)
        self.got(12, self.z, self.far, self.half_1)
        self.go(18, self.z, self.far, self.whole, self.to_core)

    def pass_other_near(self):
        self.got(7, self.other, self.left, self.whole)
        self.go(14, self.other, self.left, self.half_0, self.to_right)
        self.go(15, self.other, self.left, self.whole, self.to_core)
        self.got(8, self.other, self.right, self.whole)
        self.go(16, self.other, self.right, self.half_1, self.to_left)
        self.go(17, self.other, self.right, self.whole, self.to_core)

    def pass_other_far(self):
        self.got(14, self.other, self.far, self.half_0)
        self.got(16, self.other, self.far, self.half_1)
        self.go(19, self.other, self.far, self.whole, self.to_core)


def front_kernel(
    tokens, gain, a, w_out, w_down, attended, out_cols, down_cols,
    normed, weights, transit_w, kv, transit_kv, passing, held_out, held_down, sums, q_t, top_v, total_v, acc_v,
    local_sem, send_sem, recv_sem,
):
    z_hi, x, core, y, z_lo = place()
    ctx, me = ctx_of(z_hi, x, core), y * 2 + z_lo
    other = 1 - z_hi
    tok, full = tokens.shape
    rows = a.shape[0]
    q_cols = q_t.shape[0]
    heads = q_cols // HD
    width, deep = held_out.shape[1], w_down.shape[0]
    half = deep // 2
    sub, piece = x * 2 + core, out_cols.shape[2]
    mine = pl.ds(me * width, width)
    loads = (
        pltpu.make_async_copy(tokens, normed, local_sem.at[0]),
        pltpu.make_async_copy(a, weights.at[pl.ds(ctx * rows, rows), :], local_sem.at[1]),
        pltpu.make_async_copy(w_out.at[pl.ds(sub * piece, piece), mine], held_out, local_sem.at[2]),
        pltpu.make_async_copy(w_down.at[:, mine], held_down, local_sem.at[3]),
    )
    for load in loads:
        load.start()
    greet(ctx_neighbours() + tuple((ctx, (me + k) % 8) for k in range(1, 8)))
    sends = Sends(send_sem, recv_sem)

    def peer_of(y_step, flip):
        return (y + y_step) % 4 * 2 + (1 - z_lo if flip else z_lo)

    order = ((1, 0), (3, 0), (2, 0), (0, 1), (1, 1), (3, 1), (2, 1))

    def share(i):
        peer = peer_of(*order[i])
        src = w_out.at[pl.ds(sub * piece, piece), pl.ds(peer * width, width)]
        sends.start(40 + i, src, out_cols.at[me, sub], (ctx, peer))

    right, left, far = (x + 1) % 4, (x + 3) % 4, (x + 2) % 4
    to_right, to_left = (ctx_of(z_hi, right, core), me), (ctx_of(z_hi, left, core), me)
    to_core = (ctx_of(z_hi, x, 1 - core), me)
    whole, half_0, half_1 = (0, 8), (0, 4), (4, 4)

    def of_chip(x_of, core_of, part):
        return out_cols.at[pl.ds(part[0], part[1]), x_of * 2 + core_of]

    def pass_out(k, x_of, part, device):
        block = of_chip(x_of, core, part)
        sends.start(k, block, block, device)

    def ring_start():
        for i in range(7):
            y_step, flip = order[i]
            sends.arrived(40 + i, out_cols.at[peer_of(4 - y_step, flip), sub])
        keep_out.wait()
        pass_out(47, x, whole, to_right)
        pass_out(48, x, whole, to_left)
        pass_out(49, x, whole, to_core)

    def ring_near():
        sends.arrived(47, of_chip(left, core, whole))
        pass_out(50, left, half_0, to_right)
        pass_out(51, left, whole, to_core)
        sends.arrived(48, of_chip(right, core, whole))
        pass_out(52, right, half_1, to_left)
        pass_out(53, right, whole, to_core)

    def ring_far():
        sends.arrived(50, of_chip(far, core, half_0))
        sends.arrived(52, of_chip(far, core, half_1))
        pass_out(67, far, whole, to_core)
        for k, x_of in ((49, x), (51, left), (53, right), (67, far)):
            sends.arrived(k, of_chip(x_of, 1 - core, whole))

    def down_rows(source, h, count):
        return down_cols.at[pl.ds(source * deep + h * half, count), :]

    def down_block(k, peer):
        sends.start(k, w_down.at[:, pl.ds(peer * width, width)], down_rows(me, 0, deep), (ctx, peer))

    def first_hop():
        for k, h, flip, step in ((55, 0, 0, 1), (57, 1, 0, 3), (56, 0, 1, 1), (58, 1, 1, 3)):
            src = w_down.at[pl.ds(h * half, half), pl.ds(peer_of(2, flip) * width, width)]
            sends.start(k, src, passing.at[k - 55], (ctx, peer_of(step, 0)))

    def second_hop(flip):
        for k, h, step in ((55 + flip, 0, 1), (57 + flip, 1, 3)):
            sends.arrived(k, passing.at[k - 55])
            source = peer_of(4 - step, 0)
            sends.start(k + 4, passing.at[k - 55], down_rows(source, h, half), (ctx, peer_of(step, flip)))

    spread_w = Spread(a, weights, transit_w, rows, sends, 0)
    spread_w.start()
    for i in range(3):
        share(i)

    loads[0].wait()
    loads[2].wait()
    keep_out = pltpu.make_async_copy(held_out, out_cols.at[me, sub], local_sem.at[4])
    keep_out.start()

    def norm(i, carry):
        r = pl.ds(pl.multiple_of(i * 64, 64), 64)
        floats = normed[r, :].astype(jnp.float32)
        inverse = lax.rsqrt(jnp.mean(floats * floats, axis=-1, keepdims=True) + epsilon)
        normed[r, :] = (floats * inverse * gain[...]).astype(normed.dtype)
        return carry

    lax.fori_loop(0, tok // 64, norm, 0)
    sums[...] = jnp.zeros_like(sums)

    def project(z_of, x_of):
        at = pl.multiple_of(ctx_of(z_of, x_of, 0) * rows, 2 * rows)
        sums[...] += jnp.dot(
            normed[:, pl.ds(at, 2 * rows)], weights[pl.ds(at, 2 * rows), :], preferred_element_type=jnp.float32
        )

    def two(visit):
        return lambda j, carry: (visit(j), carry)[1]

    spread_w.pass_z()
    for i in range(3, 7):
        share(i)
    down_block(54, peer_of(0, 1))
    first_hop()
    down_block(63, peer_of(1, 0))
    down_block(64, peer_of(3, 0))
    spread_w.pass_near()
    loads[1].wait()
    spread_w.from_core(4, z_hi, x)
    project(z_hi, x)
    spread_w.pass_other()
    spread_w.from_core(11, z_hi, spread_w.left)
    spread_w.from_core(13, z_hi, spread_w.right)
    lax.fori_loop(0, 2, two(lambda j: project(z_hi, (x + 1 + 2 * j) % 4)), 0)
    spread_w.pass_far()
    spread_w.from_core(9, other, x)
    project(other, x)
    spread_w.pass_other_near()
    spread_w.from_core(18, z_hi, spread_w.far)
    project(z_hi, spread_w.far)
    spread_w.from_core(15, other, spread_w.left)
    spread_w.from_core(17, other, spread_w.right)
    lax.fori_loop(0, 2, two(lambda j: project(other, (x + 1 + 2 * j) % 4)), 0)
    spread_w.pass_other_far()
    spread_w.from_core(19, other, spread_w.far)
    project(other, spread_w.far)

    own_rows = pl.ds(ctx * tok, tok)
    kv[own_rows, :] = sums[:, q_cols:].astype(kv.dtype)
    for h in range(heads):
        q_t[h * HD : (h + 1) * HD, :] = sums[:, h * HD : (h + 1) * HD].T.astype(q_t.dtype)
    top_v[...] = jnp.full_like(top_v, -1e30)
    total_v[...] = jnp.zeros_like(total_v)
    acc_v[...] = jnp.zeros_like(acc_v)
    scale = HD ** (-0.5) * math.log2(math.e)

    def visit(block, diagonal):
        at = pl.multiple_of(block * tok, tok)
        keys = kv[pl.ds(at, tok), :HD]
        values = kv[pl.ds(at, tok), HD:]
        for h in range(heads):
            r = slice(h * HD, (h + 1) * HD)
            top, total = top_v[h : h + 1, :], total_v[h : h + 1, :]
            scores = jnp.dot(keys, q_t[r, :], preferred_element_type=jnp.float32) * scale
            if diagonal:
                key_pos = lax.broadcasted_iota(jnp.int32, scores.shape, 0)
                query_pos = lax.broadcasted_iota(jnp.int32, scores.shape, 1)
                scores = jnp.where(key_pos <= query_pos, scores, -1e30)
            new_top = jnp.maximum(top, jnp.max(scores, axis=0, keepdims=True))
            weight = jnp.exp2(scores - new_top)
            factor = jnp.exp2(top - new_top)
            top_v[h : h + 1, :] = new_top
            total_v[h : h + 1, :] = total * factor + jnp.sum(weight, axis=0, keepdims=True)
            mixed = lax.dot_general(
                values, weight.astype(jnp.bfloat16), (((0,), (0,)), ((), ())), preferred_element_type=jnp.float32
            )
            acc_v[r, :] = acc_v[r, :] * factor + mixed

    def seen(block):
        @pl.when(block < ctx)
        def _():
            visit(block, False)

    spread_kv = Spread(kv.at[own_rows, :], kv, transit_kv, tok, sends, 20)
    spread_kv.start()
    visit(ctx, True)
    spread_kv.pass_z()
    down_block(65, peer_of(1, 1))
    down_block(66, peer_of(3, 1))
    spread_kv.pass_near()
    second_hop(0)
    spread_kv.pass_other()
    spread_kv.from_core(4, z_hi, x)
    seen(ctx_of(z_hi, x, 1 - core))
    spread_kv.from_core(11, z_hi, spread_kv.left)
    spread_kv.from_core(13, z_hi, spread_kv.right)
    lax.fori_loop(0, 4, two(lambda j: seen(ctx_of(z_hi, (x + 1 + j // 2 * 2) % 4, j % 2))), 0)
    spread_kv.pass_far()
    spread_kv.pass_other_near()
    ring_start()
    second_hop(1)
    spread_kv.from_core(9, other, x)
    spread_kv.from_core(18, z_hi, spread_kv.far)
    lax.fori_loop(0, 4, two(lambda j: seen(ctx_of((z_hi + 1 - j // 2) % 2, (x + j // 2 * 2) % 4, j % 2))), 0)
    spread_kv.pass_other_far()
    ring_near()
    spread_kv.from_core(15, other, spread_kv.left)
    spread_kv.from_core(17, other, spread_kv.right)
    spread_kv.from_core(19, other, spread_kv.far)
    lax.fori_loop(0, 6, two(lambda j: seen(ctx_of(other, (x + 1 + j // 2) % 4, j % 2))), 0)
    for h in range(heads):
        r = slice(h * HD, (h + 1) * HD)
        attended[:, r] = (acc_v[r, :] / total_v[h : h + 1, :]).T.astype(attended.dtype)

    loads[3].wait()
    keep_down = pltpu.make_async_copy(held_down, down_rows(me, 0, deep), local_sem.at[5])
    keep_down.start()
    ring_far()
    sends.arrived(54, down_rows(peer_of(0, 1), 0, deep))
    for flip in (0, 1):
        sends.arrived(59 + flip, down_rows(peer_of(2, flip), 0, half))
        sends.arrived(61 + flip, down_rows(peer_of(2, flip), 1, half))
    for k, y_step, flip in ((63, 1, 0), (64, 3, 0), (65, 1, 1), (66, 3, 1)):
        sends.arrived(k, down_rows(peer_of(4 - y_step, flip), 0, deep))
    sends.drain()
    keep_down.wait()


ANY = pl.BlockSpec(memory_space=pl.ANY)
VMEM = pl.BlockSpec(memory_space=pltpu.VMEM)


def run_front(tokens, gain, a, w_out, w_down, q_cols, call_id):
    bf16, f32 = jnp.bfloat16, jnp.float32
    tok, full = tokens.shape
    rows, cols = a.shape
    depth, deep, width = w_out.shape[0], w_down.shape[0], full // 8
    return pl.pallas_call(
        front_kernel,
        out_shape=(
            jax.ShapeDtypeStruct((tok, q_cols), bf16),
            jax.ShapeDtypeStruct((8, 8, depth // 8, width), bf16),
            jax.ShapeDtypeStruct((deep * 8, width), bf16),
        ),
        in_specs=[ANY, VMEM, ANY, ANY, ANY],
        out_specs=(VMEM, ANY, ANY),
        scratch_shapes=[
            pltpu.VMEM((tok, full), bf16),
            pltpu.VMEM((full, cols), bf16),
            pltpu.VMEM((2, rows // 2, cols), bf16),
            pltpu.VMEM((tok * 16, cols - q_cols), bf16),
            pltpu.VMEM((2, tok // 2, cols - q_cols), bf16),
            pltpu.VMEM((4, deep // 2, width), bf16),
            pltpu.VMEM((depth // 8, width), bf16),
            pltpu.VMEM((deep, width), bf16),
            pltpu.VMEM((tok, cols), f32),
            pltpu.VMEM((q_cols, tok), bf16),
            pltpu.VMEM((8, tok), f32),
            pltpu.VMEM((8, tok), f32),
            pltpu.VMEM((q_cols, tok), f32),
            pltpu.SemaphoreType.DMA((6,)),
            pltpu.SemaphoreType.DMA((68,)),
            pltpu.SemaphoreType.DMA((68,)),
        ],
        compiler_params=pltpu.CompilerParams(
            collective_id=call_id, has_side_effects=True, vmem_limit_bytes=56 << 20
        ),
        name="front",
    )(tokens, gain, a, w_out, w_down)


class Gather:
    def __init__(self, buf, row, rows, split, cols, sends, base, source=None):
        z_hi, x, core, y, z_lo = place()
        ctx = ctx_of(z_hi, x, core)
        self.buf, self.cols, self.sends, self.base, self.source = buf, cols, sends, base, source
        self.y, self.z, self.other = y, z_lo, 1 - z_lo
        self.right, self.left, self.far = (y + 1) % 4, (y + 3) % 4, (y + 2) % 4
        self.to_right, self.to_left = (ctx, self.right * 2 + z_lo), (ctx, self.left * 2 + z_lo)
        self.to_z = (ctx, y * 2 + self.other)
        half, rest = split // 2, rows - split
        self.first, self.first_0, self.first_1 = (row, split), (row, half), (row + half, half)
        self.rest, self.rest_0 = (row + split, rest), (row + split, rest // 2)
        self.rest_1 = (row + split + rest // 2, rest // 2)

    def at(self, y_of, z_of, part):
        return self.buf.at[pl.ds(part[0], part[1]), pl.ds((y_of * 2 + z_of) * self.cols, self.cols)]

    def go(self, k, y_of, z_of, part, device):
        ref = self.at(y_of, z_of, part)
        self.sends.start(self.base + k, ref, ref, device)

    def got(self, k, y_of, z_of, part):
        self.sends.arrived(self.base + k, self.at(y_of, z_of, part))

    def own(self):
        for k, part, device in (
            (0, self.first, self.to_z),
            (1, self.first, self.to_right),
            (2, self.first, self.to_left),
            (3, self.rest, self.to_right),
            (4, self.rest, self.to_left),
            (5, self.rest, self.to_z),
        ):
            here = self.at(self.y, self.z, part)
            src = here if self.source is None else self.source.at[pl.ds(part[0], part[1]), :]
            self.sends.start(self.base + k, src, here, device)

    def step_a(self):
        self.got(0, self.y, self.other, self.first)
        self.go(6, self.y, self.other, self.first, self.to_right)
        self.go(7, self.y, self.other, self.first, self.to_left)

    def step_b(self):
        self.got(3, self.left, self.z, self.rest)
        self.go(10, self.left, self.z, self.rest_0, self.to_right)
        self.go(11, self.left, self.z, self.rest, self.to_z)
        self.got(4, self.right, self.z, self.rest)
        self.go(12, self.right, self.z, self.rest_1, self.to_left)
        self.go(13, self.right, self.z, self.rest, self.to_z)

    def step_c(self):
        self.got(1, self.left, self.z, self.first)
        self.go(8, self.left, self.z, self.first_0, self.to_right)
        self.got(2, self.right, self.z, self.first)
        self.go(9, self.right, self.z, self.first_1, self.to_left)

    def step_d(self):
        self.got(10, self.far, self.z, self.rest_0)
        self.go(16, self.far, self.z, self.rest_0, self.to_z)
        self.got(12, self.far, self.z, self.rest_1)
        self.go(17, self.far, self.z, self.rest_1, self.to_z)

    def step_e(self):
        self.got(6, self.left, self.other, self.first)
        self.go(14, self.left, self.other, self.first_0, self.to_right)
        self.got(7, self.right, self.other, self.first)
        self.go(15, self.right, self.other, self.first_1, self.to_left)

    def finish_near(self, use):
        self.got(5, self.y, self.other, self.rest)
        use(self.y)
        self.got(11, self.left, self.other, self.rest)
        use(self.left)
        self.got(13, self.right, self.other, self.rest)
        use(self.right)

    def finish_far(self):
        self.got(8, self.far, self.z, self.first_0)
        self.got(9, self.far, self.z, self.first_1)
        self.got(14, self.far, self.other, self.first_0)
        self.got(15, self.far, self.other, self.first_1)
        self.got(16, self.far, self.other, self.rest_0)
        self.got(17, self.far, self.other, self.rest_1)

    def finish(self):
        self.finish_near(lambda y_of: None)
        self.finish_far()


PARTS = 4


def experts_kernel(
    attended, out_cols, tokens, gain, router, chosen, slots, w_gate, w_up, down_cols,
    out, share, all_att, out_v, stream, picks, buffer, back, parts, rows, hidden, done, gate_v, up_v, down_v,
    local_sem, send_sem, recv_sem,
):
    f32, bf16 = jnp.float32, jnp.bfloat16
    z_hi, x, core, y, z_lo = place()
    me, hx = ctx_of(z_hi, x, core), y * 2 + z_lo
    tok = tokens.shape[0]
    head_cols = attended.shape[1]
    width, deep = tokens.shape[1], w_gate.shape[1]
    total = buffer.shape[0]
    chunk = total // PARTS
    slot = chunk // 16
    loads = [
        pltpu.make_async_copy(w_gate, gate_v, local_sem.at[0]),
        pltpu.make_async_copy(w_up, up_v, local_sem.at[1]),
    ]
    loads.append(pltpu.make_async_copy(down_cols, down_v, local_sem.at[2]))
    mine = pl.ds(hx * width, width)
    early = (
        pltpu.make_async_copy(attended, all_att.at[:, pl.ds(hx * head_cols, head_cols)], local_sem.at[3]),
        pltpu.make_async_copy(out_cols, out_v, local_sem.at[4]),
    )
    for copy in early:
        copy.start()
    keeps = []
    greet([((me + k) % 16, hx) for k in range(1, 16)] + [(me, (hx + k) % 8) for k in range(1, 8)])
    sends = Sends(send_sem, recv_sem)

    def spot(c, p):
        return pl.ds(c * chunk + p * slot, slot)

    def dispatch(c):
        keep = pltpu.make_async_copy(buffer.at[spot(c, me), :], rows.at[spot(c, me), mine], local_sem.at[5 + c])
        keep.start()
        keeps.append(keep)
        for k in range(1, 16):
            peer = (me + k) % 16
            sends.start(c * 15 + k - 1, buffer.at[spot(c, peer), :], rows.at[spot(c, me), mine], (peer, hx))

    def dispatched(c):
        keeps[c].wait()
        for k in range(1, 16):
            sends.arrived(c * 15 + k - 1, rows.at[spot(c, (me + 16 - k) % 16), mine])

    def give(c):
        base = PARTS * 15
        for k in range(1, 16):
            peer = (me + k) % 16
            sends.start(base + c * 15 + k - 1, done.at[spot(c, peer), :], back.at[spot(c, me), :], (peer, hx))
        keep = pltpu.make_async_copy(done.at[spot(c, me), :], back.at[spot(c, me), :], local_sem.at[5 + PARTS + c])
        keep.start()
        keeps.append(keep)

    def given(c):
        base = PARTS * 15
        keeps[PARTS + c].wait()
        for k in range(1, 16):
            sends.arrived(base + c * 15 + k - 1, back.at[spot(c, (me + 16 - k) % 16), :])

    def hide(c):
        step = 256
        r = pl.ds(c * chunk, chunk)

        def some(n, carry):
            f = pl.ds(pl.multiple_of(n * step, step), step)
            gate = jnp.dot(rows[r, :], gate_v[:, f], preferred_element_type=jnp.float32)
            up = jnp.dot(rows[r, :], up_v[:, f], preferred_element_type=jnp.float32)
            spread = pl.ds(pl.multiple_of(hx * deep + n * step, step), step)
            hidden[r, spread] = (gate * jax.nn.sigmoid(gate) * up).astype(hidden.dtype)
            return carry

        lax.fori_loop(0, deep // step, some, 0)

    def lower(c):
        r = pl.ds(c * chunk, chunk)
        for at, step in ((0, 256), (256, 256), (512, 128)):
            f = pl.ds(at, step)
            done[r, f] = jnp.dot(hidden[r, :], down_v[:, f], preferred_element_type=jnp.float32).astype(done.dtype)

    base = PARTS * 30
    splits = [chunk * (10 - 2 * (c % 2)) // 16 // 32 * 32 for c in range(PARTS)]
    row_gathers = [Gather(rows, c * chunk, chunk, splits[c], width, sends, base + 18 * c) for c in range(PARTS)]
    base += 18 * PARTS
    hid_gathers = [Gather(hidden, c * chunk, chunk, splits[c], deep, sends, base + 18 * c) for c in range(PARTS)]
    r0, r1, r2, r3 = row_gathers
    h0, h1, h2, h3 = hid_gathers

    base += 18 * PARTS
    att = Gather(all_att, 0, tok, tok * 9 // 16 // 32 * 32, head_cols, sends, base, attended)
    base += 18
    att.own()
    for load in loads:
        load.start()
    row_slot = lax.broadcasted_iota(jnp.int32, (total, tok), 0)
    picks[...] = jnp.where(row_slot == slots[...], 1.0, 0.0).astype(bf16)
    att.step_a()
    att.step_b()
    att.step_c()
    att.step_d()
    att.step_e()
    for copy in early:
        copy.wait()
    share[...] = tokens[...].astype(f32)

    def project(y_of):
        at = pl.ds(pl.multiple_of(y_of * 2 * head_cols, 2 * head_cols), 2 * head_cols)
        share[...] += jnp.dot(all_att[:, at], out_v[at, :], preferred_element_type=f32)

    att.finish_near(project)
    att.finish_far()
    project(att.far)
    stream[...] = share[...].astype(bf16)
    floats = stream[...].astype(f32)
    logits = jnp.dot((floats * gain[...]).astype(bf16), router[...], preferred_element_type=f32)
    lane = lax.broadcasted_iota(jnp.int32, logits.shape, 1)
    logit = jnp.sum(jnp.where(lane == chosen[...], logits, 0.0), axis=1, keepdims=True)
    square = jnp.sum(floats * floats, axis=1, keepdims=True)
    parts[hx] = jnp.where(lane == 0, square, jnp.where(lane == 1, logit, 0.0)).T[:8, :]
    for k in range(1, 8):
        sends.start(base + k - 1, parts.at[hx], parts.at[hx], (me, (hx + k) % 8))
    for k in range(1, 8):
        sends.arrived(base + k - 1, parts.at[(hx + 8 - k) % 8])
    both = jnp.sum(parts[...], axis=0)
    inverse = lax.rsqrt(both[0:1, :] / rows.shape[1] + epsilon)
    score = jax.nn.sigmoid(both[1:2, :] * inverse)
    line = lax.broadcasted_iota(jnp.int32, (128, tok), 0)
    column = jnp.where(line == 0, inverse, jnp.where(line == 1, score, 0.0)).T
    normed = (stream[...].astype(f32) * column[:, 0:1] * gain[...]).astype(bf16)
    routed = (normed.astype(f32) * column[:, 1:2]).astype(bf16)
    for c in range(PARTS):
        r = pl.ds(c * chunk, chunk)
        buffer[r, :] = jnp.dot(picks[r, :], routed, preferred_element_type=f32).astype(bf16)
        dispatch(c)
    def tail(g):
        g.step_c()
        g.step_d()
        g.step_e()

    def head(g):
        g.step_a()
        g.step_b()

    dispatched(0)
    r0.own()
    head(r0)
    dispatched(1)
    r1.own()
    tail(r0)
    head(r1)
    dispatched(2)
    r2.own()
    r0.finish()
    tail(r1)
    head(r2)
    dispatched(3)
    r3.own()
    for load in loads:
        load.wait()
    hide(0)
    r1.finish()
    tail(r2)
    head(r3)
    h0.own()
    hide(1)
    tail(r3)
    r2.finish()
    head(h0)
    h1.own()
    hide(2)
    tail(h0)
    r3.finish()
    head(h1)
    h2.own()
    hide(3)
    tail(h1)
    h0.finish()
    head(h2)
    h3.own()
    lower(0)
    tail(h2)
    h1.finish()
    give(0)
    head(h3)
    lower(1)
    tail(h3)
    h2.finish()
    give(1)
    lower(2)
    h3.finish()
    give(2)
    lower(3)

    def placed(c):
        r = pl.ds(c * chunk, chunk)
        return lax.dot_general(picks[r, :], back[r, :], (((0,), (0,)), ((), ())), preferred_element_type=f32)

    given(0)
    found = placed(0)
    give(3)
    for c in range(1, PARTS):
        given(c)
        found = found + placed(c)
    found = found.astype(bf16).astype(f32)
    out[...] = (stream[...].astype(f32) + found).astype(out.dtype)
    sends.drain()


def run_experts(attended, out_cols, tokens, gain, router, chosen, slots, total, w_gate, w_up, down_cols, call_id):
    tok, width = tokens.shape
    full, deep = w_gate.shape
    bf16 = jnp.bfloat16
    copies = PARTS * 66 + 25
    return pl.pallas_call(
        experts_kernel,
        out_shape=jax.ShapeDtypeStruct((tok, width), bf16),
        in_specs=[ANY, ANY, VMEM, VMEM, VMEM, VMEM, VMEM, ANY, ANY, ANY],
        out_specs=VMEM,
        scratch_shapes=[
            pltpu.VMEM((tok, width), jnp.float32),
            pltpu.VMEM((tok, attended.shape[1] * 8), bf16),
            pltpu.VMEM(out_cols.shape, bf16),
            pltpu.VMEM((tok, width), bf16),
            pltpu.VMEM((total, tok), bf16),
            pltpu.VMEM((total, width), bf16),
            pltpu.VMEM((total, width), bf16),
            pltpu.VMEM((8, 8, tok), jnp.float32),
            pltpu.VMEM((total, full), bf16),
            pltpu.VMEM((total, deep * 8), bf16),
            pltpu.VMEM((total, width), bf16),
            pltpu.VMEM((full, deep), bf16),
            pltpu.VMEM((full, deep), bf16),
            pltpu.VMEM((deep * 8, width), bf16),
            pltpu.SemaphoreType.DMA((5 + 2 * PARTS,)),
            pltpu.SemaphoreType.DMA((copies,)),
            pltpu.SemaphoreType.DMA((copies,)),
        ],
        compiler_params=pltpu.CompilerParams(
            collective_id=call_id, has_side_effects=True, vmem_limit_bytes=63 << 20
        ),
        name="experts",
    )(attended, out_cols, tokens, gain, router, chosen, slots, w_gate, w_up, down_cols)


def body(tokens, attn_gain, ffn_gain, w_query, w_key, w_value, w_out, w_router, routes, w_gate, w_up, w_down):
    f32, bf16 = jnp.float32, jnp.bfloat16
    hx = lax.axis_index("hx")
    tok_rows, full_width = tokens.shape
    width = full_width // 8

    w_down = w_down[0]

    qkv = jnp.concatenate((w_query, w_key, w_value), axis=1)
    attended, out_cols, down_cols = run_front(
        tokens, attn_gain.astype(f32)[None, :], qkv, w_out, w_down, w_query.shape[1], 2
    )
    own_tokens = lax.dynamic_slice_in_dim(tokens, hx * width, width, 1)
    own_gain = lax.dynamic_slice_in_dim(ffn_gain, hx * width, width, 0).astype(f32)[None, :]
    own_router = lax.dynamic_slice_in_dim(w_router, hx * width, width, 0)
    experts = w_router.shape[1]
    own_router = jnp.pad(own_router, ((0, 0), (0, 128 - experts)))
    capacity = tok_rows // 8
    chosen = routes[:, 0]
    onehot = chosen[:, None] == jnp.arange(experts, dtype=jnp.int32)[None, :]
    counts = jnp.cumsum(onehot.astype(jnp.int32), axis=0)
    position = jnp.sum(jnp.where(onehot, counts, 0), axis=-1) - 1
    slots = capacity // PARTS
    slot = position // slots * (experts * slots) + chosen * slots + position % slots
    return run_experts(
        attended, out_cols.reshape(-1, width), own_tokens, own_gain, own_router, routes, slot[None, :], experts * capacity,
        w_gate[0], w_up[0], down_cols, 6,
    )


def solution(mesh):
    in_specs = (
        P("ctx", None),
        P(),
        P(),
        P("ctx", "hx"),
        P("ctx", "hx"),
        P("ctx", "hx"),
        P("hx", None),
        P(),
        P("ctx", None),
        P("ctx", None, "hx"),
        P("ctx", None, "hx"),
        P("ctx", "hx", None),
    )
    return jax.shard_map(body, mesh=mesh, in_specs=in_specs, out_specs=P("ctx", "hx"), check_vma=False)
```

```python
import functools
import math
import jax
import jax.numpy as jnp
from jax import lax
from jax.experimental import pallas as pl
from jax.experimental.pallas import tpu as pltpu
from jax.sharding import PartitionSpec as P

HD = 128
epsilon = 1e-05
MESH = pl.DeviceIdType.MESH


def place():
    ctx, hx = lax.axis_index("ctx"), lax.axis_index("hx")
    z_hi, x, core = ctx // 8, (ctx // 2) % 4, ctx % 2
    y, z_lo = hx // 2, hx % 2
    return z_hi, x, core, y, z_lo


def ctx_of(z_hi, x, core):
    return z_hi * 8 + x * 2 + core


def greet(devices):
    barrier = pltpu.get_barrier_semaphore()
    for device in devices:
        pl.semaphore_signal(barrier, inc=1, device_id=device, device_id_type=MESH)
    pl.semaphore_wait(barrier, len(devices))


class Sends:
    def __init__(self, send_sem, recv_sem):
        self.send_sem, self.recv_sem, self.started = send_sem, recv_sem, []

    def start(self, k, src, dst, device):
        copy = pltpu.make_async_remote_copy(
            src_ref=src,
            dst_ref=dst,
            send_sem=self.send_sem.at[k],
            recv_sem=self.recv_sem.at[k],
            device_id=device,
            device_id_type=MESH,
        )
        copy.start()
        self.started.append(copy)

    def arrived(self, k, dst):
        pltpu.make_async_copy(dst, dst, self.recv_sem.at[k]).wait()

    def drain(self):
        for copy in self.started:
            copy.wait_send()


def ctx_neighbours():
    z_hi, x, core, y, z_lo = place()
    hx = y * 2 + z_lo
    z = z_hi * 2 + z_lo
    up, down = (z + 1) % 4, (z + 3) % 4
    return (
        (ctx_of(z_hi, (x + 1) % 4, core), hx),
        (ctx_of(z_hi, (x + 3) % 4, core), hx),
        (ctx_of(up // 2, x, core), y * 2 + up % 2),
        (ctx_of(down // 2, x, core), y * 2 + down % 2),
        (ctx_of(z_hi, x, 1 - core), hx),
    )


class Spread:
    def __init__(self, own, out, transit, rows, sends, base):
        z_hi, x, core, y, z_lo = place()
        hx = y * 2 + z_lo
        z = z_hi * 2 + z_lo
        up, down = (z + 1) % 4, (z + 3) % 4
        self.own_ref, self.out, self.transit, self.rows, self.sends, self.base = own, out, transit, rows, sends, base
        self.z, self.x, self.core, self.other = z_hi, x, core, 1 - z_hi
        self.right, self.left, self.far = (x + 1) % 4, (x + 3) % 4, (x + 2) % 4
        self.z_up, self.z_down = up // 2, down // 2
        self.to_right, self.to_left = (ctx_of(z_hi, self.right, core), hx), (ctx_of(z_hi, self.left, core), hx)
        self.to_up = (ctx_of(up // 2, x, core), y * 2 + up % 2)
        self.to_down = (ctx_of(down // 2, x, core), y * 2 + down % 2)
        self.to_core = (ctx_of(z_hi, x, 1 - core), hx)
        self.whole, self.half_0, self.half_1 = (0, rows), (0, rows // 2), (rows // 2, rows // 2)

    def at(self, z_of, x_of, core_of, part):
        return self.out.at[pl.ds(ctx_of(z_of, x_of, core_of) * self.rows + part[0], part[1]), :]

    def go(self, k, z_of, x_of, part, device):
        ref = self.at(z_of, x_of, self.core, part)
        self.sends.start(self.base + k, ref, ref, device)

    def got(self, k, z_of, x_of, part):
        self.sends.arrived(self.base + k, self.at(z_of, x_of, self.core, part))

    def from_core(self, k, z_of, x_of):
        self.sends.arrived(self.base + k, self.at(z_of, x_of, 1 - self.core, self.whole))

    def start(self):
        def own(part):
            return self.own_ref.at[pl.ds(part[0], part[1]), :]

        here = self.at(self.z, self.x, self.core, self.whole)
        self.sends.start(self.base + 0, own(self.half_0), self.transit.at[0], self.to_up)
        self.sends.start(self.base + 1, own(self.half_1), self.transit.at[1], self.to_down)
        self.sends.start(self.base + 2, own(self.whole), here, self.to_right)
        self.sends.start(self.base + 3, own(self.whole), here, self.to_left)
        self.sends.start(self.base + 4, own(self.whole), here, self.to_core)

    def pass_z(self):
        self.sends.arrived(self.base + 0, self.transit.at[0])
        self.sends.start(
            self.base + 5, self.transit.at[0], self.at(self.z_down, self.x, self.core, self.half_0), self.to_up
        )
        self.sends.arrived(self.base + 1, self.transit.at[1])
        self.sends.start(
            self.base + 6, self.transit.at[1], self.at(self.z_up, self.x, self.core, self.half_1), self.to_down
        )

    def pass_near(self):
        self.got(2, self.z, self.left, self.whole)
        self.go(10, self.z, self.left, self.half_0, self.to_right)
        self.go(11, self.z, self.left, self.whole, self.to_core)
        self.got(3, self.z, self.right, self.whole)
        self.go(12, self.z, self.right, self.half_1, self.to_left)
        self.go(13, self.z, self.right, self.whole, self.to_core)

    def pass_other(self):
        self.got(5, self.other, self.x, self.half_0)
        self.got(6, self.other, self.x, self.half_1)
        self.go(7, self.other, self.x, self.whole, self.to_right)
        self.go(8, self.other, self.x, self.whole, self.to_left)
        self.go(9, self.other, self.x, self.whole, self.to_core)

    def pass_far(self):
        self.got(10, self.z, self.far, self.half_0)
        self.got(12, self.z, self.far, self.half_1)
        self.go(18, self.z, self.far, self.whole, self.to_core)

    def pass_other_near(self):
        self.got(7, self.other, self.left, self.whole)
        self.go(14, self.other, self.left, self.half_0, self.to_right)
        self.go(15, self.other, self.left, self.whole, self.to_core)
        self.got(8, self.other, self.right, self.whole)
        self.go(16, self.other, self.right, self.half_1, self.to_left)
        self.go(17, self.other, self.right, self.whole, self.to_core)

    def pass_other_far(self):
        self.got(14, self.other, self.far, self.half_0)
        self.got(16, self.other, self.far, self.half_1)
        self.go(19, self.other, self.far, self.whole, self.to_core)


def front_kernel(
    tokens, gain, a, w_out, w_down, attended, out_cols, down_cols,
    normed, weights, transit_w, kv, transit_kv, passing, held_out, held_down, sums, q_t, top_v, total_v, acc_v,
    local_sem, send_sem, recv_sem,
):
    z_hi, x, core, y, z_lo = place()
    ctx, me = ctx_of(z_hi, x, core), y * 2 + z_lo
    other = 1 - z_hi
    tok, full = tokens.shape
    rows = a.shape[0]
    q_cols = q_t.shape[0]
    heads = q_cols // HD
    width, deep = held_out.shape[1], w_down.shape[0]
    half = deep // 2
    sub, piece = x * 2 + core, out_cols.shape[2]
    mine = pl.ds(me * width, width)
    loads = (
        pltpu.make_async_copy(tokens, normed, local_sem.at[0]),
        pltpu.make_async_copy(a, weights.at[pl.ds(ctx * rows, rows), :], local_sem.at[1]),
        pltpu.make_async_copy(w_out.at[pl.ds(sub * piece, piece), mine], held_out, local_sem.at[2]),
        pltpu.make_async_copy(w_down.at[:, mine], held_down, local_sem.at[3]),
    )
    for load in loads:
        load.start()
    greet(ctx_neighbours() + tuple((ctx, (me + k) % 8) for k in range(1, 8)))
    sends = Sends(send_sem, recv_sem)

    def peer_of(y_step, flip):
        return (y + y_step) % 4 * 2 + (1 - z_lo if flip else z_lo)

    order = ((1, 0), (3, 0), (2, 0), (0, 1), (1, 1), (3, 1), (2, 1))

    def share(i):
        peer = peer_of(*order[i])
        src = w_out.at[pl.ds(sub * piece, piece), pl.ds(peer * width, width)]
        sends.start(40 + i, src, out_cols.at[me, sub], (ctx, peer))

    right, left, far = (x + 1) % 4, (x + 3) % 4, (x + 2) % 4
    to_right, to_left = (ctx_of(z_hi, right, core), me), (ctx_of(z_hi, left, core), me)
    to_core = (ctx_of(z_hi, x, 1 - core), me)
    whole, half_0, half_1 = (0, 8), (0, 4), (4, 4)

    def of_chip(x_of, core_of, part):
        return out_cols.at[pl.ds(part[0], part[1]), x_of * 2 + core_of]

    def pass_out(k, x_of, part, device):
        block = of_chip(x_of, core, part)
        sends.start(k, block, block, device)

    def ring_start():
        for i in range(7):
            y_step, flip = order[i]
            sends.arrived(40 + i, out_cols.at[peer_of(4 - y_step, flip), sub])
        keep_out.wait()
        pass_out(47, x, whole, to_right)
        pass_out(48, x, whole, to_left)
        pass_out(49, x, whole, to_core)

    def ring_near():
        sends.arrived(47, of_chip(left, core, whole))
        pass_out(50, left, half_0, to_right)
        pass_out(51, left, whole, to_core)
        sends.arrived(48, of_chip(right, core, whole))
        pass_out(52, right, half_1, to_left)
        pass_out(53, right, whole, to_core)

    def ring_far():
        sends.arrived(50, of_chip(far, core, half_0))
        sends.arrived(52, of_chip(far, core, half_1))
        pass_out(67, far, whole, to_core)
        for k, x_of in ((49, x), (51, left), (53, right), (67, far)):
            sends.arrived(k, of_chip(x_of, 1 - core, whole))

    def down_rows(source, h, count):
        return down_cols.at[pl.ds(source * deep + h * half, count), :]

    def down_block(k, peer):
        sends.start(k, w_down.at[:, pl.ds(peer * width, width)], down_rows(me, 0, deep), (ctx, peer))

    def first_hop():
        for k, h, flip, step in ((55, 0, 0, 1), (57, 1, 0, 3), (56, 0, 1, 1), (58, 1, 1, 3)):
            src = w_down.at[pl.ds(h * half, half), pl.ds(peer_of(2, flip) * width, width)]
            sends.start(k, src, passing.at[k - 55], (ctx, peer_of(step, 0)))

    def second_hop(flip):
        for k, h, step in ((55 + flip, 0, 1), (57 + flip, 1, 3)):
            sends.arrived(k, passing.at[k - 55])
            source = peer_of(4 - step, 0)
            sends.start(k + 4, passing.at[k - 55], down_rows(source, h, half), (ctx, peer_of(step, flip)))

    spread_w = Spread(a, weights, transit_w, rows, sends, 0)
    spread_w.start()
    for i in range(3):
        share(i)

    loads[0].wait()
    loads[2].wait()
    keep_out = pltpu.make_async_copy(held_out, out_cols.at[me, sub], local_sem.at[4])
    keep_out.start()

    def norm(i, carry):
        r = pl.ds(pl.multiple_of(i * 64, 64), 64)
        floats = normed[r, :].astype(jnp.float32)
        inverse = lax.rsqrt(jnp.mean(floats * floats, axis=-1, keepdims=True) + epsilon)
        normed[r, :] = (floats * inverse * gain[...]).astype(normed.dtype)
        return carry

    lax.fori_loop(0, tok // 64, norm, 0)
    sums[...] = jnp.zeros_like(sums)

    def project(z_of, x_of):
        at = pl.multiple_of(ctx_of(z_of, x_of, 0) * rows, 2 * rows)
        sums[...] += jnp.dot(
            normed[:, pl.ds(at, 2 * rows)], weights[pl.ds(at, 2 * rows), :], preferred_element_type=jnp.float32
        )

    def two(visit):
        return lambda j, carry: (visit(j), carry)[1]

    spread_w.pass_z()
    for i in range(3, 7):
        share(i)
    down_block(54, peer_of(0, 1))
    first_hop()
    down_block(63, peer_of(1, 0))
    down_block(64, peer_of(3, 0))
    spread_w.pass_near()
    loads[1].wait()
    spread_w.from_core(4, z_hi, x)
    project(z_hi, x)
    spread_w.pass_other()
    spread_w.from_core(11, z_hi, spread_w.left)
    spread_w.from_core(13, z_hi, spread_w.right)
    lax.fori_loop(0, 2, two(lambda j: project(z_hi, (x + 1 + 2 * j) % 4)), 0)
    spread_w.pass_far()
    spread_w.from_core(9, other, x)
    project(other, x)
    spread_w.pass_other_near()
    spread_w.from_core(18, z_hi, spread_w.far)
    project(z_hi, spread_w.far)
    spread_w.from_core(15, other, spread_w.left)
    spread_w.from_core(17, other, spread_w.right)
    lax.fori_loop(0, 2, two(lambda j: project(other, (x + 1 + 2 * j) % 4)), 0)
    spread_w.pass_other_far()
    spread_w.from_core(19, other, spread_w.far)
    project(other, spread_w.far)

    own_rows = pl.ds(ctx * tok, tok)
    kv[own_rows, :] = sums[:, q_cols:].astype(kv.dtype)
    for h in range(heads):
        q_t[h * HD : (h + 1) * HD, :] = sums[:, h * HD : (h + 1) * HD].T.astype(q_t.dtype)
    top_v[...] = jnp.full_like(top_v, -1e30)
    total_v[...] = jnp.zeros_like(total_v)
    acc_v[...] = jnp.zeros_like(acc_v)
    scale = HD ** (-0.5) * math.log2(math.e)

    def visit(block, diagonal):
        at = pl.multiple_of(block * tok, tok)
        keys = kv[pl.ds(at, tok), :HD]
        values = kv[pl.ds(at, tok), HD:]
        for h in range(heads):
            r = slice(h * HD, (h + 1) * HD)
            top, total = top_v[h : h + 1, :], total_v[h : h + 1, :]
            scores = jnp.dot(keys, q_t[r, :], preferred_element_type=jnp.float32) * scale
            if diagonal:
                key_pos = lax.broadcasted_iota(jnp.int32, scores.shape, 0)
                query_pos = lax.broadcasted_iota(jnp.int32, scores.shape, 1)
                scores = jnp.where(key_pos <= query_pos, scores, -1e30)
            new_top = jnp.maximum(top, jnp.max(scores, axis=0, keepdims=True))
            weight = jnp.exp2(scores - new_top)
            factor = jnp.exp2(top - new_top)
            top_v[h : h + 1, :] = new_top
            total_v[h : h + 1, :] = total * factor + jnp.sum(weight, axis=0, keepdims=True)
            mixed = lax.dot_general(
                values, weight.astype(jnp.bfloat16), (((0,), (0,)), ((), ())), preferred_element_type=jnp.float32
            )
            acc_v[r, :] = acc_v[r, :] * factor + mixed

    def seen(block):
        @pl.when(block < ctx)
        def _():
            visit(block, False)

    spread_kv = Spread(kv.at[own_rows, :], kv, transit_kv, tok, sends, 20)
    spread_kv.start()
    visit(ctx, True)
    spread_kv.pass_z()
    down_block(65, peer_of(1, 1))
    down_block(66, peer_of(3, 1))
    spread_kv.pass_near()
    second_hop(0)
    spread_kv.pass_other()
    spread_kv.from_core(4, z_hi, x)
    seen(ctx_of(z_hi, x, 1 - core))
    spread_kv.from_core(11, z_hi, spread_kv.left)
    spread_kv.from_core(13, z_hi, spread_kv.right)
    lax.fori_loop(0, 4, two(lambda j: seen(ctx_of(z_hi, (x + 1 + j // 2 * 2) % 4, j % 2))), 0)
    spread_kv.pass_far()
    spread_kv.pass_other_near()
    ring_start()
    second_hop(1)
    spread_kv.from_core(9, other, x)
    spread_kv.from_core(18, z_hi, spread_kv.far)
    lax.fori_loop(0, 4, two(lambda j: seen(ctx_of((z_hi + 1 - j // 2) % 2, (x + j // 2 * 2) % 4, j % 2))), 0)
    spread_kv.pass_other_far()
    ring_near()
    spread_kv.from_core(15, other, spread_kv.left)
    spread_kv.from_core(17, other, spread_kv.right)
    spread_kv.from_core(19, other, spread_kv.far)
    lax.fori_loop(0, 6, two(lambda j: seen(ctx_of(other, (x + 1 + j // 2) % 4, j % 2))), 0)
    for h in range(heads):
        r = slice(h * HD, (h + 1) * HD)
        attended[:, r] = (acc_v[r, :] / total_v[h : h + 1, :]).T.astype(attended.dtype)

    loads[3].wait()
    keep_down = pltpu.make_async_copy(held_down, down_rows(me, 0, deep), local_sem.at[5])
    keep_down.start()
    ring_far()
    sends.arrived(54, down_rows(peer_of(0, 1), 0, deep))
    for flip in (0, 1):
        sends.arrived(59 + flip, down_rows(peer_of(2, flip), 0, half))
        sends.arrived(61 + flip, down_rows(peer_of(2, flip), 1, half))
    for k, y_step, flip in ((63, 1, 0), (64, 3, 0), (65, 1, 1), (66, 3, 1)):
        sends.arrived(k, down_rows(peer_of(4 - y_step, flip), 0, deep))
    sends.drain()
    keep_down.wait()


ANY = pl.BlockSpec(memory_space=pl.ANY)
VMEM = pl.BlockSpec(memory_space=pltpu.VMEM)


def run_front(tokens, gain, a, w_out, w_down, q_cols, call_id):
    bf16, f32 = jnp.bfloat16, jnp.float32
    tok, full = tokens.shape
    rows, cols = a.shape
    depth, deep, width = w_out.shape[0], w_down.shape[0], full // 8
    return pl.pallas_call(
        front_kernel,
        out_shape=(
            jax.ShapeDtypeStruct((tok, q_cols), bf16),
            jax.ShapeDtypeStruct((8, 8, depth // 8, width), bf16),
            jax.ShapeDtypeStruct((deep * 8, width), bf16),
        ),
        in_specs=[ANY, VMEM, ANY, ANY, ANY],
        out_specs=(VMEM, ANY, ANY),
        scratch_shapes=[
            pltpu.VMEM((tok, full), bf16),
            pltpu.VMEM((full, cols), bf16),
            pltpu.VMEM((2, rows // 2, cols), bf16),
            pltpu.VMEM((tok * 16, cols - q_cols), bf16),
            pltpu.VMEM((2, tok // 2, cols - q_cols), bf16),
            pltpu.VMEM((4, deep // 2, width), bf16),
            pltpu.VMEM((depth // 8, width), bf16),
            pltpu.VMEM((deep, width), bf16),
            pltpu.VMEM((tok, cols), f32),
            pltpu.VMEM((q_cols, tok), bf16),
            pltpu.VMEM((8, tok), f32),
            pltpu.VMEM((8, tok), f32),
            pltpu.VMEM((q_cols, tok), f32),
            pltpu.SemaphoreType.DMA((6,)),
            pltpu.SemaphoreType.DMA((68,)),
            pltpu.SemaphoreType.DMA((68,)),
        ],
        compiler_params=pltpu.CompilerParams(
            collective_id=call_id, has_side_effects=True, vmem_limit_bytes=56 << 20
        ),
        name="front",
    )(tokens, gain, a, w_out, w_down)


class Gather:
    def __init__(self, buf, row, rows, split, cols, sends, base, source=None):
        z_hi, x, core, y, z_lo = place()
        ctx = ctx_of(z_hi, x, core)
        self.buf, self.cols, self.sends, self.base, self.source = buf, cols, sends, base, source
        self.y, self.z, self.other = y, z_lo, 1 - z_lo
        self.right, self.left, self.far = (y + 1) % 4, (y + 3) % 4, (y + 2) % 4
        self.to_right, self.to_left = (ctx, self.right * 2 + z_lo), (ctx, self.left * 2 + z_lo)
        self.to_z = (ctx, y * 2 + self.other)
        half, rest = split // 2, rows - split
        self.first, self.first_0, self.first_1 = (row, split), (row, half), (row + half, half)
        self.rest, self.rest_0 = (row + split, rest), (row + split, rest // 2)
        self.rest_1 = (row + split + rest // 2, rest // 2)

    def at(self, y_of, z_of, part):
        return self.buf.at[pl.ds(part[0], part[1]), pl.ds((y_of * 2 + z_of) * self.cols, self.cols)]

    def go(self, k, y_of, z_of, part, device):
        ref = self.at(y_of, z_of, part)
        self.sends.start(self.base + k, ref, ref, device)

    def got(self, k, y_of, z_of, part):
        self.sends.arrived(self.base + k, self.at(y_of, z_of, part))

    def own(self):
        for k, part, device in (
            (0, self.first, self.to_z),
            (1, self.first, self.to_right),
            (2, self.first, self.to_left),
            (3, self.rest, self.to_right),
            (4, self.rest, self.to_left),
            (5, self.rest, self.to_z),
        ):
            here = self.at(self.y, self.z, part)
            src = here if self.source is None else self.source.at[pl.ds(part[0], part[1]), :]
            self.sends.start(self.base + k, src, here, device)

    def step_a(self):
        self.got(0, self.y, self.other, self.first)
        self.go(6, self.y, self.other, self.first, self.to_right)
        self.go(7, self.y, self.other, self.first, self.to_left)

    def step_b(self):
        self.got(3, self.left, self.z, self.rest)
        self.go(10, self.left, self.z, self.rest_0, self.to_right)
        self.go(11, self.left, self.z, self.rest, self.to_z)
        self.got(4, self.right, self.z, self.rest)
        self.go(12, self.right, self.z, self.rest_1, self.to_left)
        self.go(13, self.right, self.z, self.rest, self.to_z)

    def step_c(self):
        self.got(1, self.left, self.z, self.first)
        self.go(8, self.left, self.z, self.first_0, self.to_right)
        self.got(2, self.right, self.z, self.first)
        self.go(9, self.right, self.z, self.first_1, self.to_left)

    def step_d(self):
        self.got(10, self.far, self.z, self.rest_0)
        self.go(16, self.far, self.z, self.rest_0, self.to_z)
        self.got(12, self.far, self.z, self.rest_1)
        self.go(17, self.far, self.z, self.rest_1, self.to_z)

    def step_e(self):
        self.got(6, self.left, self.other, self.first)
        self.go(14, self.left, self.other, self.first_0, self.to_right)
        self.got(7, self.right, self.other, self.first)
        self.go(15, self.right, self.other, self.first_1, self.to_left)

    def finish_near(self, use):
        self.got(5, self.y, self.other, self.rest)
        use(self.y)
        self.got(11, self.left, self.other, self.rest)
        use(self.left)
        self.got(13, self.right, self.other, self.rest)
        use(self.right)

    def finish_far(self):
        self.got(8, self.far, self.z, self.first_0)
        self.got(9, self.far, self.z, self.first_1)
        self.got(14, self.far, self.other, self.first_0)
        self.got(15, self.far, self.other, self.first_1)
        self.got(16, self.far, self.other, self.rest_0)
        self.got(17, self.far, self.other, self.rest_1)

    def finish(self):
        self.finish_near(lambda y_of: None)
        self.finish_far()


PARTS = 4


def experts_kernel(
    attended, out_cols, tokens, gain, router, chosen, slots, w_gate, w_up, down_cols,
    out, own_tokens, share, all_att, out_v, stream, picks, buffer, back, parts, rows, hidden, done, gate_v, up_v, down_v,
    local_sem, send_sem, recv_sem,
):
    f32, bf16 = jnp.float32, jnp.bfloat16
    z_hi, x, core, y, z_lo = place()
    me, hx = ctx_of(z_hi, x, core), y * 2 + z_lo
    tok = tokens.shape[0]
    head_cols = attended.shape[1]
    width, deep = out.shape[1], w_gate.shape[1]
    total = buffer.shape[0]
    chunk = total // PARTS
    slot = chunk // 16
    loads = [
        pltpu.make_async_copy(w_gate, gate_v, local_sem.at[0]),
        pltpu.make_async_copy(w_up, up_v, local_sem.at[1]),
    ]
    loads.append(pltpu.make_async_copy(down_cols, down_v, local_sem.at[2]))
    mine = pl.ds(hx * width, width)
    early = (
        pltpu.make_async_copy(attended, all_att.at[:, pl.ds(hx * head_cols, head_cols)], local_sem.at[3]),
        pltpu.make_async_copy(out_cols, out_v, local_sem.at[4]),
        pltpu.make_async_copy(tokens.at[:, mine], own_tokens, local_sem.at[5 + 2 * PARTS]),
    )
    for copy in early:
        copy.start()
    keeps = []
    greet([((me + k) % 16, hx) for k in range(1, 16)] + [(me, (hx + k) % 8) for k in range(1, 8)])
    sends = Sends(send_sem, recv_sem)

    def spot(c, p):
        return pl.ds(c * chunk + p * slot, slot)

    def dispatch(c):
        keep = pltpu.make_async_copy(buffer.at[spot(c, me), :], rows.at[spot(c, me), mine], local_sem.at[5 + c])
        keep.start()
        keeps.append(keep)
        for k in range(1, 16):
            peer = (me + k) % 16
            sends.start(c * 15 + k - 1, buffer.at[spot(c, peer), :], rows.at[spot(c, me), mine], (peer, hx))

    def dispatched(c):
        keeps[c].wait()
        for k in range(1, 16):
            sends.arrived(c * 15 + k - 1, rows.at[spot(c, (me + 16 - k) % 16), mine])

    def give(c):
        base = PARTS * 15
        for k in range(1, 16):
            peer = (me + k) % 16
            sends.start(base + c * 15 + k - 1, done.at[spot(c, peer), :], back.at[spot(c, me), :], (peer, hx))
        keep = pltpu.make_async_copy(done.at[spot(c, me), :], back.at[spot(c, me), :], local_sem.at[5 + PARTS + c])
        keep.start()
        keeps.append(keep)

    def given(c):
        base = PARTS * 15
        keeps[PARTS + c].wait()
        for k in range(1, 16):
            sends.arrived(base + c * 15 + k - 1, back.at[spot(c, (me + 16 - k) % 16), :])

    def hide(c):
        step = 256
        r = pl.ds(c * chunk, chunk)

        def some(n, carry):
            f = pl.ds(pl.multiple_of(n * step, step), step)
            gate = jnp.dot(rows[r, :], gate_v[:, f], preferred_element_type=jnp.float32)
            up = jnp.dot(rows[r, :], up_v[:, f], preferred_element_type=jnp.float32)
            spread = pl.ds(pl.multiple_of(hx * deep + n * step, step), step)
            hidden[r, spread] = (gate * jax.nn.sigmoid(gate) * up).astype(hidden.dtype)
            return carry

        lax.fori_loop(0, deep // step, some, 0)

    def lower(c):
        r = pl.ds(c * chunk, chunk)
        for at, step in ((0, 256), (256, 256), (512, 128)):
            f = pl.ds(at, step)
            done[r, f] = jnp.dot(hidden[r, :], down_v[:, f], preferred_element_type=jnp.float32).astype(done.dtype)

    base = PARTS * 30
    splits = [chunk * (10 - 2 * (c % 2)) // 16 // 32 * 32 for c in range(PARTS)]
    row_gathers = [Gather(rows, c * chunk, chunk, splits[c], width, sends, base + 18 * c) for c in range(PARTS)]
    base += 18 * PARTS
    hid_gathers = [Gather(hidden, c * chunk, chunk, splits[c], deep, sends, base + 18 * c) for c in range(PARTS)]
    r0, r1, r2, r3 = row_gathers
    h0, h1, h2, h3 = hid_gathers

    base += 18 * PARTS
    att = Gather(all_att, 0, tok, tok * 9 // 16 // 32 * 32, head_cols, sends, base, attended)
    base += 18
    att.own()
    for load in loads:
        load.start()
    row_slot = lax.broadcasted_iota(jnp.int32, (total, tok), 0)
    picks[...] = jnp.where(row_slot == slots[...], 1.0, 0.0).astype(bf16)
    att.step_a()
    att.step_b()
    att.step_c()
    att.step_d()
    att.step_e()
    for copy in early:
        copy.wait()
    share[...] = own_tokens[...].astype(f32)

    def project(y_of):
        at = pl.ds(pl.multiple_of(y_of * 2 * head_cols, 2 * head_cols), 2 * head_cols)
        share[...] += jnp.dot(all_att[:, at], out_v[at, :], preferred_element_type=f32)

    att.finish_near(project)
    att.finish_far()
    project(att.far)
    stream[...] = share[...].astype(bf16)
    floats = stream[...].astype(f32)
    logits = jnp.dot((floats * gain[...]).astype(bf16), router[...], preferred_element_type=f32)
    lane = lax.broadcasted_iota(jnp.int32, logits.shape, 1)
    logit = jnp.sum(jnp.where(lane == chosen[...], logits, 0.0), axis=1, keepdims=True)
    square = jnp.sum(floats * floats, axis=1, keepdims=True)
    parts[hx] = jnp.where(lane == 0, square, jnp.where(lane == 1, logit, 0.0)).T[:8, :]
    for k in range(1, 8):
        sends.start(base + k - 1, parts.at[hx], parts.at[hx], (me, (hx + k) % 8))
    for k in range(1, 8):
        sends.arrived(base + k - 1, parts.at[(hx + 8 - k) % 8])
    both = jnp.sum(parts[...], axis=0)
    inverse = lax.rsqrt(both[0:1, :] / rows.shape[1] + epsilon)
    score = jax.nn.sigmoid(both[1:2, :] * inverse)
    line = lax.broadcasted_iota(jnp.int32, (128, tok), 0)
    column = jnp.where(line == 0, inverse, jnp.where(line == 1, score, 0.0)).T
    normed = (stream[...].astype(f32) * column[:, 0:1] * gain[...]).astype(bf16)
    routed = (normed.astype(f32) * column[:, 1:2]).astype(bf16)
    for c in range(PARTS):
        r = pl.ds(c * chunk, chunk)
        buffer[r, :] = jnp.dot(picks[r, :], routed, preferred_element_type=f32).astype(bf16)
        dispatch(c)
    def tail(g):
        g.step_c()
        g.step_d()
        g.step_e()

    def head(g):
        g.step_a()
        g.step_b()

    dispatched(0)
    r0.own()
    head(r0)
    dispatched(1)
    r1.own()
    tail(r0)
    head(r1)
    dispatched(2)
    r2.own()
    r0.finish()
    tail(r1)
    head(r2)
    dispatched(3)
    r3.own()
    for load in loads:
        load.wait()
    hide(0)
    r1.finish()
    tail(r2)
    head(r3)
    h0.own()
    hide(1)
    tail(r3)
    r2.finish()
    head(h0)
    h1.own()
    hide(2)
    tail(h0)
    r3.finish()
    head(h1)
    h2.own()
    hide(3)
    tail(h1)
    h0.finish()
    head(h2)
    h3.own()
    lower(0)
    tail(h2)
    h1.finish()
    give(0)
    head(h3)
    lower(1)
    tail(h3)
    h2.finish()
    give(1)
    lower(2)
    h3.finish()
    give(2)
    lower(3)

    def placed(c):
        r = pl.ds(c * chunk, chunk)
        return lax.dot_general(picks[r, :], back[r, :], (((0,), (0,)), ((), ())), preferred_element_type=f32)

    given(0)
    found = placed(0)
    give(3)
    for c in range(1, PARTS):
        given(c)
        found = found + placed(c)
    found = found.astype(bf16).astype(f32)
    out[...] = (stream[...].astype(f32) + found).astype(out.dtype)
    sends.drain()


def run_experts(attended, out_cols, tokens, gain, router, chosen, slots, total, w_gate, w_up, down_cols, call_id):
    tok, full = tokens.shape
    deep, width = w_gate.shape[1], full // 8
    bf16 = jnp.bfloat16
    copies = PARTS * 66 + 25
    return pl.pallas_call(
        experts_kernel,
        out_shape=jax.ShapeDtypeStruct((tok, width), bf16),
        in_specs=[ANY, ANY, ANY, VMEM, VMEM, VMEM, VMEM, ANY, ANY, ANY],
        out_specs=VMEM,
        scratch_shapes=[
            pltpu.VMEM((tok, width), bf16),
            pltpu.VMEM((tok, width), jnp.float32),
            pltpu.VMEM((tok, attended.shape[1] * 8), bf16),
            pltpu.VMEM(out_cols.shape, bf16),
            pltpu.VMEM((tok, width), bf16),
            pltpu.VMEM((total, tok), bf16),
            pltpu.VMEM((total, width), bf16),
            pltpu.VMEM((total, width), bf16),
            pltpu.VMEM((8, 8, tok), jnp.float32),
            pltpu.VMEM((total, full), bf16),
            pltpu.VMEM((total, deep * 8), bf16),
            pltpu.VMEM((total, width), bf16),
            pltpu.VMEM((full, deep), bf16),
            pltpu.VMEM((full, deep), bf16),
            pltpu.VMEM((deep * 8, width), bf16),
            pltpu.SemaphoreType.DMA((6 + 2 * PARTS,)),
            pltpu.SemaphoreType.DMA((copies,)),
            pltpu.SemaphoreType.DMA((copies,)),
        ],
        compiler_params=pltpu.CompilerParams(
            collective_id=call_id, has_side_effects=True, vmem_limit_bytes=63 << 20
        ),
        name="experts",
    )(attended, out_cols, tokens, gain, router, chosen, slots, w_gate, w_up, down_cols)


def body(tokens, attn_gain, ffn_gain, w_query, w_key, w_value, w_out, w_router, routes, w_gate, w_up, w_down):
    f32, bf16 = jnp.float32, jnp.bfloat16
    hx = lax.axis_index("hx")
    tok_rows, full_width = tokens.shape
    width = full_width // 8

    w_down = w_down[0]

    qkv = jnp.concatenate((w_query, w_key, w_value), axis=1)
    attended, out_cols, down_cols = run_front(
        tokens, attn_gain.astype(f32)[None, :], qkv, w_out, w_down, w_query.shape[1], 2
    )
    own_gain = lax.dynamic_slice_in_dim(ffn_gain, hx * width, width, 0).astype(f32)[None, :]
    own_router = lax.dynamic_slice_in_dim(w_router, hx * width, width, 0)
    experts = w_router.shape[1]
    own_router = jnp.pad(own_router, ((0, 0), (0, 128 - experts)))
    capacity = tok_rows // 8
    chosen = routes[:, 0]
    onehot = chosen[:, None] == jnp.arange(experts, dtype=jnp.int32)[None, :]
    counts = jnp.cumsum(onehot.astype(jnp.int32), axis=0)
    position = jnp.sum(jnp.where(onehot, counts, 0), axis=-1) - 1
    slots = capacity // PARTS
    slot = position // slots * (experts * slots) + chosen * slots + position % slots
    return run_experts(
        attended, out_cols.reshape(-1, width), tokens, own_gain, own_router, routes, slot[None, :], experts * capacity,
        w_gate[0], w_up[0], down_cols, 6,
    )


def solution(mesh):
    in_specs = (
        P("ctx", None),
        P(),
        P(),
        P("ctx", "hx"),
        P("ctx", "hx"),
        P("ctx", "hx"),
        P("hx", None),
        P(),
        P("ctx", None),
        P("ctx", None, "hx"),
        P("ctx", None, "hx"),
        P("ctx", "hx", None),
    )
    return jax.shard_map(body, mesh=mesh, in_specs=in_specs, out_specs=P("ctx", "hx"), check_vma=False)
```
